32 devices in a mesh: dp: 8 (over z, y), mp: 4 (over x, core).
Axes of the slice: x: 2, y: 2, z: 4, core: 2. Of those that a mesh axis runs over, the one named last changes fastest.
Arguments:
- tokens: bfloat16 [8192, 1024], P('dp'), may hold values from -6 to 6
- doc_lengths: int32 [8], P('dp'), may hold values from 256 to 1024, as said below
- cls_pos: int32 [8, 4], P('dp'), may hold values from 0 to 1023, as said below
- cls_count: int32 [8], P('dp'), may hold values from 1 to 4, as said below
- q_weight: bfloat16 [1024, 1024], P(None, 'mp'), may hold values from -0.1875 to 0.1875
- q_bias: bfloat16 [1024], P('mp'), may hold values from -2 to 2
- k_weight: bfloat16 [1024, 1024], P(None, 'mp'), may hold values from -0.1875 to 0.1875
- v_weight: bfloat16 [1024, 1024], P(None, 'mp'), may hold values from -0.1875 to 0.1875
- v_bias: bfloat16 [1024], P('mp'), may hold values from -2 to 2
- o_weight: bfloat16 [1024, 1024], P('mp'), may hold values from -1.5 to 1.5
- o_bias: bfloat16 [1024], replicated, may hold values from -2 to 2
- ln1_gain: bfloat16 [1024], replicated, may hold values from 0.5 to 1.5
- ln1_bias: bfloat16 [1024], replicated, may hold values from -2 to 2
- up_weight: bfloat16 [1024, 4096], P(None, 'mp'), may hold values from -0.1875 to 0.1875
- up_bias: bfloat16 [4096], P('mp'), may hold values from -2 to 2
- down_weight: bfloat16 [4096, 1024], P('mp'), may hold values from -0.09375 to 0.09375
- down_bias: bfloat16 [1024], replicated, may hold values from -2 to 2
- ln2_gain: bfloat16 [1024], replicated, may hold values from 0.5 to 1.5
- ln2_bias: bfloat16 [1024], replicated, may hold values from -2 to 2
- out_grad: bfloat16 [8192, 1024], P('dp'), may hold values from -6 to 6
- pooled_grad: float32 [8, 4, 1024], P('dp'), may hold values from -6 to 6
Outputs:
- out: bfloat16 [8192, 1024], P('dp')
- pooled: float32 [8, 4, 1024], P('dp')
- in_grad: float32 [8192, 1024], P('dp')
- q_weight_grad: float32 [1024, 1024], P('dp', 'mp')
- q_bias_grad: float32 [1024], P('mp')
- k_weight_grad: float32 [1024, 1024], P('dp', 'mp')
- v_weight_grad: float32 [1024, 1024], P('dp', 'mp')
- v_bias_grad: float32 [1024], P('mp')
- o_weight_grad: float32 [1024, 1024], P('mp', 'dp')
- o_bias_grad: float32 [1024], replicated
- ln1_gain_grad: float32 [1024], replicated
- ln1_bias_grad: float32 [1024], replicated
- up_weight_grad: float32 [1024, 4096], P('dp', 'mp')
- up_bias_grad: float32 [4096], P('mp')
- down_weight_grad: float32 [4096, 1024], P('mp', 'dp')
- down_bias_grad: float32 [1024], replicated
- ln2_gain_grad: float32 [1024], replicated
- ln2_bias_grad: float32 [1024], replicated
The draws below stay inside these ranges and needn't reach their ends.
Inputs may be any that keep to these rules, and one draw needn't show every extreme that they name: `doc_lengths`: in every draw some document fills all 1024 slots. `cls_count`: A document's length divided by 256, rounded up; some document has 4. `cls_pos`: for j below the document's cls_count, entry j lies in [j * 256, (j + 1) * 256) and below the document's length; later entries are 0. In a document of 1024 tokens the last entry is 1023.
All inputs are finite; a program needn't handle non-finite values.
Results may differ from the reference program's by a relative error of at most 0.014.
The reference program's roundings to bfloat16 on the way count: a program that leaves them out, or rounds other values in their place, can miss the bound.
Values sent between devices are 32-bit elements; how exact they have to be, the bound alone decides.
No kernel may reach another device: no remote copies, remote signals or barrier semaphores. Data moves between devices by JAX's collectives and lax.ppermute only.
A program may use at most 128 MiB of HBM per device.

```python
import jax
import jax.numpy as jnp
from jax import lax

D = 1024
HEADS = 16
HEAD_DIM = 64
FF = 4096
SLOT = 1024
CLS_GAP = 256
CLS_MAX = 4
DOCS = 8
TOKENS = 8192


def length_draw(key):
    base_key = jax.random.fold_in(key, 71)
    first_key, second_key = jax.random.split(base_key)
    lengths = jax.random.randint(first_key, (DOCS,), SLOT // 4, SLOT + 1)
    longest = jax.random.randint(second_key, (), 0, DOCS)
    return jnp.where(jnp.arange(DOCS) == longest, SLOT, lengths).astype(jnp.int32)


def count_draw(key):
    return ((length_draw(key) + CLS_GAP - 1) // CLS_GAP).astype(jnp.int32)


def draw_doc_lengths(key, part):
    return length_draw(key)


def draw_cls_count(key, part):
    return count_draw(key)


def draw_cls_pos(key, part):
    lengths = length_draw(key)
    counts = count_draw(key)
    starts = jnp.arange(CLS_MAX) * CLS_GAP
    room_left = jnp.clip(lengths[:, None] - starts[None, :], 1, CLS_GAP)
    offsets = jax.random.randint(jax.random.fold_in(key, 72), (DOCS, CLS_MAX), 0, room_left)
    last_slot = (lengths[:, None] == SLOT) & (jnp.arange(CLS_MAX)[None, :] == CLS_MAX - 1)
    offsets = jnp.where(last_slot, CLS_GAP - 1, offsets)
    marked = jnp.arange(CLS_MAX)[None, :] < counts[:, None]
    return jnp.where(marked, starts[None, :] + offsets, 0).astype(jnp.int32)


def raised(entries, key, source, target, parts, factor):
    owner, partner = [(jnp.arange(entries.shape[dim]) // (entries.shape[dim] // parts)).reshape([-1 if axis == dim else 1 for axis in range(entries.ndim)]) for dim in (source, target)]
    chosen = jax.random.permutation(key, parts)[partner]
    strong = (owner == chosen) | (owner == (partner + parts // 2) % parts)
    return jnp.where(strong, factor * entries, entries)


def steps_of(own_key, dims, shards, least, high):
    def one(position, parts):
        steps = jax.random.uniform(jax.random.fold_in(jax.random.fold_in(own_key, 6), position), (parts,), jnp.float32, least / len(shards), high / len(shards))
        return jnp.repeat(jnp.exp(steps), dims[position] // parts).reshape((-1,) + (1,) * (len(dims) - position - 1))

    gain = one(*shards[0])
    for cut in shards[1:]:
        gain = gain * one(*cut)
    return gain


def gaussian(key, dims, width, most, cuts=(), kind=jnp.bfloat16):
    factor_of = steps_of(key, dims, cuts, -0.22, 0.18) if cuts else 1.0
    entries = jax.random.normal(key, dims, jnp.float32) * width * factor_of
    return jnp.minimum(jnp.maximum(entries, -most), most).astype(kind)


def bell_draw_with(own_key, dims, scale, reach, cuts, heavy, kind=jnp.bfloat16):
    result = scale * jax.random.normal(own_key, dims, jnp.float32)
    if cuts:
        result = result * steps_of(own_key, dims, cuts, -0.22, 0.18)
    return jnp.clip(raised(result, jax.random.fold_in(own_key, 3), *heavy), -reach, reach).astype(kind)


def setup_inputs(seed: int = 0) -> dict:
    keys = jax.random.split(jax.random.key(seed), 22)
    return {
        "tokens": bell_draw_with(keys[0], (TOKENS, D), 1.0, 6.0, ((0, 8),), (0, 1, 8, 2.0)),
        "doc_lengths": draw_doc_lengths(jax.random.fold_in(keys[21], 71), 0),
        "cls_pos": draw_cls_pos(jax.random.fold_in(keys[21], 71), 0),
        "cls_count": draw_cls_count(jax.random.fold_in(keys[21], 71), 0),
        "q_weight": gaussian(keys[4], (D, D), D ** -0.5, 0.1875, ((1, 4),)),
        "q_bias": gaussian(keys[5], (D,), 0.3, 2.0, ((0, 4),)),
        "k_weight": gaussian(keys[6], (D, D), D ** -0.5, 0.1875, ((1, 4),)),
        "v_weight": gaussian(keys[7], (D, D), D ** -0.5, 0.1875, ((1, 4),)),
        "v_bias": gaussian(keys[8], (D,), 0.3, 2.0, ((0, 4),)),
        "o_weight": gaussian(keys[9], (D, D), (max(D * 16 // SLOT, 1)) ** -0.5, 1.5, ((0, 4),)),
        "o_bias": gaussian(keys[10], (D,), 0.3, 2.0),
        "ln1_gain": jnp.clip(1.0 + 0.1 * jax.random.normal(keys[11], (D,), jnp.float32), 0.5, 1.5).astype(jnp.bfloat16),
        "ln1_bias": gaussian(keys[12], (D,), 0.3, 2.0),
        "up_weight": gaussian(keys[13], (D, FF), D ** -0.5, 0.1875, ((1, 4),)),
        "up_bias": gaussian(keys[14], (FF,), 0.3, 2.0, ((0, 4),)),
        "down_weight": gaussian(keys[15], (FF, D), FF ** -0.5, 0.09375, ((0, 4),)),
        "down_bias": gaussian(keys[16], (D,), 0.3, 2.0),
        "ln2_gain": jnp.clip(1.0 + 0.1 * jax.random.normal(keys[17], (D,), jnp.float32), 0.5, 1.5).astype(jnp.bfloat16),
        "ln2_bias": gaussian(keys[18], (D,), 0.3, 2.0),
        "out_grad": bell_draw_with(keys[19], (TOKENS, D), 1.0, 6.0, ((0, 8),), (0, 1, 8, 2.0)),
        "pooled_grad": gaussian(keys[20], (DOCS, CLS_MAX, D), 1.0, 6.0, ((0, 8),), jnp.float32),
    }


norm_eps = 1e-05
highest = lax.Precision.HIGHEST

@jax.custom_vjp
def low(v):
    return lax.optimization_barrier(v.astype(jnp.bfloat16)).astype(jnp.float32)

@jax.custom_vjp
def low_back(v):
    return v

def low_keep(v):
    return (low(v), None)

def low_pass(kept, grad):
    return (grad,)

def back_keep(v):
    return (v, None)

def back_low(kept, grad):
    return (low(grad),)
low.defvjp(low_keep, low_pass)
low_back.defvjp(back_keep, back_low)

def matmul_high(left_side, right_side):
    return jnp.dot(left_side, right_side, precision=highest)

def both_ways(values):
    return low(low_back(values))

def layer_norm(values, gain_vec, shift_vec):
    centre = values - lax.optimization_barrier(jnp.mean(values, axis=-1, keepdims=True))
    spread = lax.optimization_barrier(jnp.mean(centre * centre, axis=-1, keepdims=True))
    return centre * lax.rsqrt(spread + norm_eps) * gain_vec + shift_vec

def one_document(doc_rows, length, positions, cls_total, weights_all):
    q_weight, q_bias, k_weight, v_weight, v_bias, o_weight, o_bias, ln1_gain, ln1_bias, up_weight, up_bias, down_weight, down_bias, ln2_gain, ln2_bias = weights_all
    keep_rows = (jnp.arange(SLOT) < length).astype(jnp.float32)
    queries = both_ways(matmul_high(doc_rows, q_weight) + q_bias).reshape(SLOT, HEADS, HEAD_DIM)
    key_rows = both_ways(matmul_high(doc_rows, k_weight)).reshape(SLOT, HEADS, HEAD_DIM)
    value_rows = both_ways(matmul_high(doc_rows, v_weight) + v_bias).reshape(SLOT, HEADS, HEAD_DIM)
    raw_scores = jnp.einsum('qhd,khd->hqk', queries, key_rows, precision=highest)
    scores = low_back(raw_scores * 0.125)
    scores = jnp.where(keep_rows[None, None, :] > 0, scores, -1e+30)
    probs_low = low(jax.nn.softmax(scores, axis=-1))
    context = jnp.einsum('hqk,khd->qhd', probs_low, value_rows, precision=highest)
    context = both_ways(context.reshape(SLOT, D))
    attended = low_back(matmul_high(context, o_weight) + o_bias)
    normed = layer_norm(doc_rows + attended, ln1_gain, ln1_bias)
    pre_active = low_back(matmul_high(low(normed), up_weight) + up_bias)
    active = low(jax.nn.gelu(pre_active, approximate=False))
    fed_rows = low_back(matmul_high(active, down_weight) + down_bias)
    out_rows = layer_norm(normed + fed_rows, ln2_gain, ln2_bias) * keep_rows[:, None]
    valid_slots = (jnp.arange(CLS_MAX) < cls_total).astype(jnp.float32)
    pooled = jnp.take(out_rows, positions, axis=0) * valid_slots[:, None]
    return (out_rows, pooled)

def reference(tokens, doc_lengths, cls_pos, cls_count, q_weight, q_bias, k_weight, v_weight, v_bias, o_weight, o_bias, ln1_gain, ln1_bias, up_weight, up_bias, down_weight, down_bias, ln2_gain, ln2_bias, out_grad, pooled_grad):
    weights_all = tuple((weight.astype(jnp.float32) for weight in (q_weight, q_bias, k_weight, v_weight, v_bias, o_weight, o_bias, ln1_gain, ln1_bias, up_weight, up_bias, down_weight, down_bias, ln2_gain, ln2_bias)))
    all_rows = tokens.astype(jnp.float32).reshape(DOCS, SLOT, D)
    doc_step = jax.checkpoint(one_document)

    def forward(all_rows, weights_all):

        def scan_step(carried, inputs):
            doc_rows, length, positions, cls_total = inputs
            return (carried, doc_step(doc_rows, length, positions, cls_total, weights_all))
        unused, outputs = lax.scan(scan_step, jnp.zeros((), jnp.float32), (all_rows, doc_lengths, cls_pos, cls_count))
        return outputs
    (out_rows, pooled), pull_back = jax.vjp(forward, all_rows, weights_all)
    row_grads, weight_grads = pull_back((out_grad.astype(jnp.float32).reshape(DOCS, SLOT, D), pooled_grad.astype(jnp.float32)))
    return (out_rows.reshape(TOKENS, D).astype(jnp.bfloat16), pooled, row_grads.reshape(TOKENS, D), weight_grads[0], weight_grads[1], weight_grads[2], weight_grads[3], weight_grads[4], weight_grads[5], weight_grads[6], weight_grads[7], weight_grads[8], weight_grads[9], weight_grads[10], weight_grads[11], weight_grads[12], weight_grads[13], weight_grads[14])
```

```python
import functools

import jax
import jax.numpy as jnp
from jax import lax
from jax.experimental import pallas as pl
from jax.experimental.pallas import tpu as pltpu
from jax.sharding import PartitionSpec as P

HEAD_DIM = 64
NORM_EPS = 1e-05
ROOT_HALF = 0.7071067811865476
INV_ROOT_TAU = 0.3989422804014327
LOG2E = 1.4426950408889634
SCORE_SCALE = 0.125 * LOG2E
MASKED = -1e30

f32 = jnp.float32
bf16 = jnp.bfloat16
VMEM_LIMIT = 48 * 1024 * 1024


def dot_nn(a, b):
    return lax.dot_general(a, b, (((1,), (0,)), ((), ())), preferred_element_type=f32)


def dot_nt(a, b):
    return lax.dot_general(a, b, (((1,), (1,)), ((), ())), preferred_element_type=f32)


def dot_tn(a, b):
    return lax.dot_general(a, b, (((0,), (0,)), ((), ())), preferred_element_type=f32)


def attn_fwd_kernel(q_ref, k_ref, v_ref, bias_ref, o_ref, lse_ref):
    rows, width = q_ref.shape
    heads = width // HEAD_DIM
    lane = lax.broadcasted_iota(jnp.int32, (1, width), 1) // HEAD_DIM
    lse_lane = lax.broadcasted_iota(jnp.int32, (1, 128), 1)
    q = q_ref[...]
    k = k_ref[...]
    v = v_ref[...]
    bias = bias_ref[...]
    out = jnp.zeros((rows, width), f32)
    lse = jnp.zeros((rows, 128), f32)
    for h in range(heads):
        qh = jnp.where(lane == h, q, jnp.zeros_like(q))
        s = dot_nt(qh, k) * SCORE_SCALE + bias
        top = jnp.max(s, axis=1, keepdims=True)
        e = jnp.exp2(s - top)
        total = jnp.sum(e, axis=1, keepdims=True)
        p = (e * (1.0 / total)).astype(bf16)
        c = dot_nn(p, v)
        out = jnp.where(lane == h, c, out)
        lse = jnp.where(lse_lane == h, top + jnp.log2(total), lse)
    o_ref[...] = out.astype(o_ref.dtype)
    lse_ref[...] = lse


def attn_fwd(q, k, v, bias, block, dtype):
    rows, width = q.shape
    keys = k.shape[0]
    full = pl.BlockSpec((keys, width), lambda i: (0, 0))
    return pl.pallas_call(
        attn_fwd_kernel,
        grid=(rows // block,),
        in_specs=[
            pl.BlockSpec((block, width), lambda i: (i, 0)),
            full,
            full,
            pl.BlockSpec((1, keys), lambda i: (0, 0)),
        ],
        out_specs=[
            pl.BlockSpec((block, width), lambda i: (i, 0)),
            pl.BlockSpec((block, 128), lambda i: (i, 0)),
        ],
        out_shape=[
            jax.ShapeDtypeStruct((rows, width), dtype),
            jax.ShapeDtypeStruct((rows, 128), f32),
        ],
        compiler_params=pltpu.CompilerParams(vmem_limit_bytes=VMEM_LIMIT),
        cost_estimate=pl.CostEstimate(
            flops=4 * rows * keys * width * (width // HEAD_DIM),
            bytes_accessed=4 * keys * width + 8 * rows * width,
            transcendentals=rows * keys * (width // HEAD_DIM),
        ),
        name="attn_fwd",
    )(q, k, v, bias)


def attn_bwd_kernel(q_ref, g_ref, k_ref, v_ref, bias_ref, lse_ref, gq_ref, gk_ref, gv_ref, gk_acc, gv_acc):
    step = pl.program_id(0)
    rows, width = q_ref.shape
    heads = width // HEAD_DIM
    lane = lax.broadcasted_iota(jnp.int32, (1, width), 1) // HEAD_DIM
    q = q_ref[...]
    g = g_ref[...]
    k = k_ref[...]
    v = v_ref[...]
    bias = bias_ref[...]
    lse = lse_ref[...]
    gq = jnp.zeros((rows, width), f32)

    @pl.when(step == 0)
    def _():
        gk_acc[...] = jnp.zeros_like(gk_acc)
        gv_acc[...] = jnp.zeros_like(gv_acc)

    for h in range(heads):
        mine = lane == h
        qh = jnp.where(mine, q, jnp.zeros_like(q))
        gh = jnp.where(mine, g, jnp.zeros_like(g))
        s = dot_nt(qh, k) * SCORE_SCALE + bias
        p = jnp.exp2(s - lse[:, h : h + 1])
        dp = dot_nt(gh, v)
        inner = jnp.sum(p * dp, axis=1, keepdims=True)
        ds = (p * (dp - inner)).astype(bf16)
        p_low = p.astype(bf16)
        gq = jnp.where(mine, dot_nn(ds, k), gq)
        gk_acc[...] += dot_tn(ds, qh)
        gv_acc[...] += dot_tn(p_low, gh)
    gq_ref[...] = (gq * 0.125).astype(bf16)

    @pl.when(step == pl.num_programs(0) - 1)
    def _():
        gk_ref[...] = (gk_acc[...] * 0.125).astype(bf16)
        gv_ref[...] = gv_acc[...].astype(bf16)


def attn_bwd(q, g, k, v, bias, lse, block):
    rows, width = q.shape
    keys = k.shape[0]
    full = pl.BlockSpec((keys, width), lambda i: (0, 0))
    part = pl.BlockSpec((block, width), lambda i: (i, 0))
    return pl.pallas_call(
        attn_bwd_kernel,
        grid=(rows // block,),
        in_specs=[
            part,
            part,
            full,
            full,
            pl.BlockSpec((1, keys), lambda i: (0, 0)),
            pl.BlockSpec((block, 128), lambda i: (i, 0)),
        ],
        out_specs=[part, full, full],
        out_shape=[
            jax.ShapeDtypeStruct((rows, width), bf16),
            jax.ShapeDtypeStruct((keys, width), bf16),
            jax.ShapeDtypeStruct((keys, width), bf16),
        ],
        scratch_shapes=[pltpu.VMEM((keys, width), f32), pltpu.VMEM((keys, width), f32)],
        compiler_params=pltpu.CompilerParams(vmem_limit_bytes=VMEM_LIMIT),
        cost_estimate=pl.CostEstimate(
            flops=10 * rows * keys * width * (width // HEAD_DIM),
            bytes_accessed=12 * keys * width,
            transcendentals=rows * keys * (width // HEAD_DIM),
        ),
        name="attn_bwd",
    )(q, g, k, v, bias, lse)


def swap_core(value):
    return lax.ppermute(value, "mp", [(i, i ^ 1) for i in range(4)])


def swap_chip(value):
    return lax.ppermute(value, "mp", [(i, i ^ 2) for i in range(4)])


def gather_rows(own):
    other = swap_chip(own)
    sibling = swap_core(own)
    diagonal = swap_core(other)
    return own, sibling, other, diagonal


def scatter_rows(part):
    from_sibling = swap_core(part(3))
    from_chip = swap_chip(part(2) + from_sibling)
    near = swap_core(part(1))
    return part(0) + near + from_chip


def rounder(count):
    one = jnp.minimum(count, 1).astype(f32)
    return lambda value: (value * one).astype(bf16)


def bit_order_blocks(parts, order):
    bits = len(order)
    blocks = []
    for position in range(parts):
        block = 0
        for level, bit in enumerate(order):
            block |= ((position >> (bits - 1 - level)) & 1) << bit
        blocks.append(block)
    return blocks


def bit_order_columns(matrix, parts, order):
    width = matrix.shape[1] // parts
    return jnp.concatenate(
        [matrix[:, b * width : (b + 1) * width] for b in bit_order_blocks(parts, order)], axis=1
    )


def halving_sum(left, right, parts, order, place):
    def swap(value, bit):
        return lax.ppermute(value, "dp", [(i, i ^ (1 << bit)) for i in range(parts)])

    if not order:
        return dot_tn(left, right)
    half = left.shape[1] // 2
    mine = (place >> order[0]) & 1
    away = dot_tn(lax.dynamic_slice_in_dim(left, (1 - mine) * half, half, 1), right)
    got = swap(away, order[0])
    total = dot_tn(lax.dynamic_slice_in_dim(left, mine * half, half, 1), right) + got
    for bit in order[1:]:
        half = total.shape[0] // 2
        mine = (place >> bit) & 1
        away = lax.dynamic_slice_in_dim(total, (1 - mine) * half, half, 0)
        got = swap(away, bit)
        total = lax.dynamic_slice_in_dim(total, mine * half, half, 0) + got
    return total


def sum_over(value, axis, parts):
    step = 1
    while step < parts:
        value = value + lax.ppermute(value, axis, [(i, i ^ step) for i in range(parts)])
        step *= 2
    return value


def row_norm(values):
    centre = values - jnp.mean(values, axis=-1, keepdims=True)
    spread = jnp.mean(centre * centre, axis=-1, keepdims=True)
    scale_inv = lax.rsqrt(spread + NORM_EPS)
    return centre * scale_inv, scale_inv


def norm_back(grad_rows, unit_rows, scale_inv, gain):
    scaled = grad_rows * gain
    return scale_inv * (
        scaled
        - jnp.mean(scaled, axis=-1, keepdims=True)
        - unit_rows * jnp.mean(scaled * unit_rows, axis=-1, keepdims=True)
    )


def col_sum(rows):
    return jnp.sum(rows, axis=0)


def shards(
    dp_size,
    tokens,
    doc_lengths,
    cls_pos,
    cls_count,
    q_weight,
    q_bias,
    k_weight,
    v_weight,
    v_bias,
    o_weight,
    o_bias,
    ln1_gain,
    ln1_bias,
    up_weight,
    up_bias,
    down_weight,
    down_bias,
    ln2_gain,
    ln2_bias,
    out_grad,
    pooled_grad,
):
    slot_len, width = tokens.shape
    rows = slot_len // 4
    rank = lax.axis_index("mp")
    place = lax.axis_index("dp")
    bits = dp_size.bit_length() - 1
    order_a = list(range(bits))
    order_b = [1, 0] + list(range(2, bits)) if bits > 1 else order_a
    length = doc_lengths[0]
    rounded = rounder(cls_count[0])
    blocks = [rank ^ j for j in range(4)]

    def take(array, j):
        return lax.dynamic_slice_in_dim(array, blocks[j] * rows, rows, 0)

    o_near = o_weight
    o_far = rounded(swap_chip(o_weight.astype(f32)))
    gain_one = ln1_gain.astype(f32)
    gain_two = ln2_gain.astype(f32)
    shift_one = ln1_bias.astype(f32)
    shift_two = ln2_bias.astype(f32)

    local = jnp.concatenate([take(tokens, j) for j in range(4)], axis=0)
    row_ids = lax.iota(jnp.int32, rows)
    positions = jnp.concatenate([row_ids + blocks[j] * rows for j in range(4)])
    bias = jnp.where(positions < length, 0.0, MASKED).astype(f32)[None, :]
    queries = (dot_nn(local, q_weight) + q_bias.astype(f32)).astype(bf16)
    key_rows = dot_nn(local, k_weight).astype(bf16)
    value_rows = (dot_nn(local, v_weight) + v_bias.astype(f32)).astype(bf16)

    half = 2 * rows
    away_context, lse_far = attn_fwd(queries[half:], key_rows, value_rows, bias, 256, f32)
    context_far = away_context.astype(bf16)
    context_other = rounded(swap_chip(away_context))
    context_near, lse_near = attn_fwd(queries[:half], key_rows, value_rows, bias, 256, bf16)

    def attended_part(j):
        cut = slice(j * rows, (j + 1) * rows)
        return dot_nn(context_near[cut], o_near) + dot_nn(context_other[cut], o_far)

    attended = attended_part(0) + swap_core(attended_part(1)) + o_bias.astype(f32)
    unit_one, inv_one = row_norm(local[:rows].astype(f32) + attended)
    normed = unit_one * gain_one + shift_one
    n0, n1, n2, n3 = gather_rows(normed)
    low_near = jnp.concatenate([n0.astype(bf16), rounded(n1)], axis=0)
    low_far = jnp.concatenate([rounded(n2), rounded(n3)], axis=0)

    def feed(low):
        pre = dot_nn(low, up_weight) + up_bias.astype(f32)
        return pre, jax.nn.gelu(pre, approximate=False).astype(bf16)

    pre_near, active_near = feed(low_near)
    pre_far, active_far = feed(low_far)

    def pick(near, far, j):
        source = near if j < 2 else far
        return source[(j % 2) * rows : (j % 2 + 1) * rows]

    fed = scatter_rows(lambda j: dot_nn(pick(active_near, active_far, j), down_weight))
    second = gather_rows(normed + fed + down_bias.astype(f32))

    outs = []
    grads_low = []
    markers = []
    for j in range(4):
        unit_two, inv_two = row_norm(second[j])
        keep = ((row_ids + blocks[j] * rows) < length).astype(f32)[:, None]
        outs.append(((unit_two * gain_two + shift_two) * keep).astype(bf16))
        spot = lax.dynamic_index_in_dim(cls_pos[0], blocks[j], keepdims=False) - blocks[j] * rows
        live = blocks[j] < cls_count[0]
        extra = lax.dynamic_index_in_dim(pooled_grad[0], blocks[j], keepdims=True)
        placed = jnp.where(((row_ids == spot) & live)[:, None], extra, 0.0)
        grad_out = (take(out_grad, j).astype(f32) + placed) * keep
        grad_two = norm_back(grad_out, unit_two, inv_two, gain_two)
        grads_low.append(grad_two.astype(bf16))
        marker = lax.dynamic_slice_in_dim(second[j], jnp.clip(spot, 0, rows - 1), 1, 0)
        markers.append(marker)
        if j == 0:
            grad_two_own = grad_two
            ln2_gain_grad = col_sum(grad_out * unit_two)
            ln2_bias_grad = col_sum(grad_out)
            down_bias_grad = col_sum(grads_low[0].astype(f32))
    marked = jnp.concatenate(
        [
            lax.dynamic_index_in_dim(
                jnp.concatenate(markers, axis=0), rank ^ j, keepdims=True
            )
            for j in range(4)
        ],
        axis=0,
    )
    marked_unit, _ = row_norm(marked)
    valid = (lax.iota(jnp.int32, 4) < cls_count[0]).astype(f32)[:, None]
    pooled = ((marked_unit * gain_two + shift_two) * valid)[None]

    grad_near = jnp.concatenate(grads_low[:2], axis=0)
    grad_far = jnp.concatenate(grads_low[2:], axis=0)

    def slope(pre):
        normal_cdf = 0.5 * (1.0 + lax.erf(pre * ROOT_HALF))
        density = jnp.exp(-0.5 * pre * pre) * INV_ROOT_TAU
        return normal_cdf + pre * density

    grad_pre_near = (dot_nt(grad_near, down_weight) * slope(pre_near)).astype(bf16)
    grad_pre_far = (dot_nt(grad_far, down_weight) * slope(pre_far)).astype(bf16)
    up_bias_grad = col_sum(grad_pre_near.astype(f32)) + col_sum(grad_pre_far.astype(f32))
    back = scatter_rows(lambda j: dot_nt(pick(grad_pre_near, grad_pre_far, j), up_weight))

    active = jnp.concatenate([active_near, active_far], axis=0)
    grad_fed = jnp.concatenate([grad_near, grad_far], axis=0)
    normed_low = jnp.concatenate([low_near, low_far], axis=0)
    grad_pre = jnp.concatenate([grad_pre_near, grad_pre_far], axis=0)
    down_sum = halving_sum(
        bit_order_columns(grad_fed, dp_size, order_a), active, dp_size, order_a, place
    ).T
    up_sum = halving_sum(
        bit_order_columns(normed_low, dp_size, order_b), grad_pre, dp_size, order_b, place
    )

    grad_normed = grad_two_own + back
    grad_first = norm_back(grad_normed, unit_one, inv_one, gain_one)
    ln1_gain_grad = col_sum(grad_normed * unit_one)
    ln1_bias_grad = col_sum(grad_normed)
    grad_attended_own = grad_first.astype(bf16)
    o_bias_grad = col_sum(grad_attended_own.astype(f32))
    grad_attended = jnp.concatenate(
        [grad_attended_own, rounded(swap_core(grad_first))], axis=0
    )
    grad_context_far = rounded(swap_chip(dot_nt(grad_attended, o_far)))
    grad_context_near = dot_nt(grad_attended, o_near).astype(bf16)
    grad_context = jnp.concatenate([grad_context_near, grad_context_far], axis=0)

    ga_cols = bit_order_columns(grad_attended, dp_size, order_b)
    o_part = dot_tn(ga_cols, context_near) + swap_chip(dot_tn(ga_cols, context_other))

    grad_q, grad_k, grad_v = attn_bwd(
        queries,
        grad_context,
        key_rows,
        value_rows,
        bias,
        jnp.concatenate([lse_near, lse_far], axis=0),
        256,
    )
    grad_qkv = jnp.concatenate([grad_q, grad_k, grad_v], axis=1)
    qkv_weight = jnp.concatenate([q_weight, k_weight, v_weight], axis=1)
    in_own = grad_first + scatter_rows(
        lambda j: dot_nt(grad_qkv[j * rows : (j + 1) * rows], qkv_weight)
    )
    in_parts = gather_rows(in_own)

    def place_rows(parts):
        result = jnp.zeros((slot_len, width), parts[0].dtype)
        for j in range(4):
            result = lax.dynamic_update_slice_in_dim(result, parts[j], blocks[j] * rows, 0)
        return result

    qkv_sum = halving_sum(
        bit_order_columns(local, dp_size, order_a), grad_qkv, dp_size, order_a, place
    )

    def rest(total, order):
        for bit in order:
            cut = total.shape[0] // 2
            mine = (place >> bit) & 1
            away = lax.dynamic_slice_in_dim(total, (1 - mine) * cut, cut, 0)
            got = lax.ppermute(away, "dp", [(i, i ^ (1 << bit)) for i in range(dp_size)])
            total = lax.dynamic_slice_in_dim(total, mine * cut, cut, 0) + got
        return total

    o_sum = rest(o_part, order_b).T
    head_width = q_weight.shape[1]
    q_bias_grad = col_sum(grad_q.astype(f32))
    v_bias_grad = col_sum(grad_v.astype(f32))
    shared = sum_over(
        jnp.stack(
            [o_bias_grad, ln1_gain_grad, ln1_bias_grad, down_bias_grad, ln2_gain_grad, ln2_bias_grad]
        ),
        "mp",
        4,
    )
    head_row = jnp.concatenate(
        [q_bias_grad, v_bias_grad, jnp.zeros((width - 2 * head_width,), f32)]
    )
    sums = sum_over(
        jnp.concatenate([shared, head_row[None], up_bias_grad[None]], axis=0), "dp", dp_size
    )
    q_sum = qkv_sum[:, :head_width]
    k_sum = qkv_sum[:, head_width : 2 * head_width]
    v_sum = qkv_sum[:, 2 * head_width :]
    return (
        place_rows(outs),
        pooled,
        place_rows(in_parts),
        q_sum,
        sums[6, :head_width],
        k_sum,
        v_sum,
        sums[6, head_width : 2 * head_width],
        o_sum,
        sums[0],
        sums[1],
        sums[2],
        up_sum,
        sums[7],
        down_sum,
        sums[3],
        sums[4],
        sums[5],
    )


def solution(mesh):
    return jax.shard_map(
        functools.partial(shards, mesh.shape["dp"]),
        mesh=mesh,
        in_specs=(
            P("dp", None),
            P("dp"),
            P("dp", None),
            P("dp"),
            P(None, "mp"),
            P("mp"),
            P(None, "mp"),
            P(None, "mp"),
            P("mp"),
            P("mp", None),
            P(),
            P(),
            P(),
            P(None, "mp"),
            P("mp"),
            P("mp", None),
            P(),
            P(),
            P(),
            P("dp", None),
            P("dp", None, None),
        ),
        out_specs=(
            P("dp", None),
            P("dp", None, None),
            P("dp", None),
            P("dp", "mp"),
            P("mp"),
            P("dp", "mp"),
            P("dp", "mp"),
            P("mp"),
            P("mp", "dp"),
            P(),
            P(),
            P(),
            P("dp", "mp"),
            P("mp"),
            P("mp", "dp"),
            P(),
            P(),
            P(),
        ),
        check_vma=False,
    )
```

```python
import functools

import jax
import jax.numpy as jnp
from jax import lax
from jax.experimental import pallas as pl
from jax.experimental.pallas import tpu as pltpu
from jax.sharding import PartitionSpec as P

HEAD_DIM = 64
NORM_EPS = 1e-05
ROOT_HALF = 0.7071067811865476
INV_ROOT_TAU = 0.3989422804014327
LOG2E = 1.4426950408889634
SCORE_SCALE = 0.125 * LOG2E
MASKED = -1e30

f32 = jnp.float32
bf16 = jnp.bfloat16
VMEM_LIMIT = 20 * 1024 * 1024
ROW_LIMIT = 8 * 1024 * 1024


def dot_nn(a, b):
    return lax.dot_general(a, b, (((1,), (0,)), ((), ())), preferred_element_type=f32)


def dot_nt(a, b):
    return lax.dot_general(a, b, (((1,), (1,)), ((), ())), preferred_element_type=f32)


def dot_tn(a, b):
    return lax.dot_general(a, b, (((0,), (0,)), ((), ())), preferred_element_type=f32)


def attn_fwd_kernel(q_ref, k_ref, v_ref, bias_ref, o_ref, lse_ref):
    rows, width = q_ref.shape
    heads = width // HEAD_DIM
    lane = lax.broadcasted_iota(jnp.int32, (1, width), 1) // HEAD_DIM
    lse_lane = lax.broadcasted_iota(jnp.int32, (1, 128), 1)
    q = q_ref[...]
    k = k_ref[...]
    v = v_ref[...]
    bias = bias_ref[...]
    out = jnp.zeros((rows, width), f32)
    lse = jnp.zeros((rows, 128), f32)
    for h in range(heads):
        qh = jnp.where(lane == h, q, jnp.zeros_like(q))
        s = dot_nt(qh, k) * SCORE_SCALE + bias
        top = jnp.max(s, axis=1, keepdims=True)
        e = jnp.exp2(s - top)
        total = jnp.sum(e, axis=1, keepdims=True)
        p = (e * (1.0 / total)).astype(bf16)
        c = dot_nn(p, v)
        out = jnp.where(lane == h, c, out)
        lse = jnp.where(lse_lane == h, top + jnp.log2(total), lse)
    o_ref[...] = out.astype(o_ref.dtype)
    lse_ref[...] = lse


def attn_fwd(q, k, v, bias, block, dtype):
    rows, width = q.shape
    keys = k.shape[0]
    full = pl.BlockSpec((keys, width), lambda i: (0, 0))
    return pl.pallas_call(
        attn_fwd_kernel,
        grid=(rows // block,),
        in_specs=[
            pl.BlockSpec((block, width), lambda i: (i, 0)),
            full,
            full,
            pl.BlockSpec((1, keys), lambda i: (0, 0)),
        ],
        out_specs=[
            pl.BlockSpec((block, width), lambda i: (i, 0)),
            pl.BlockSpec((block, 128), lambda i: (i, 0)),
        ],
        out_shape=[
            jax.ShapeDtypeStruct((rows, width), dtype),
            jax.ShapeDtypeStruct((rows, 128), f32),
        ],
        compiler_params=pltpu.CompilerParams(vmem_limit_bytes=VMEM_LIMIT),
        cost_estimate=pl.CostEstimate(flops=1024, bytes_accessed=1024, transcendentals=0),
        name="attn_fwd",
    )(q, k, v, bias)


def attn_bwd_kernel(carried, *refs):
    q_ref, g_ref, k_ref, v_ref, bias_ref, lse_ref = refs[:6]
    refs = refs[6:]
    if carried:
        gk_in, gv_in = refs[:2]
        refs = refs[2:]
    gq_ref, gk_ref, gv_ref, gk_acc, gv_acc = refs
    step = pl.program_id(0)
    rows, width = q_ref.shape
    heads = width // HEAD_DIM
    lane = lax.broadcasted_iota(jnp.int32, (1, width), 1) // HEAD_DIM
    q = q_ref[...]
    g = g_ref[...].astype(bf16)
    k = k_ref[...]
    v = v_ref[...]
    bias = bias_ref[...]
    lse = lse_ref[...]
    gq = jnp.zeros((rows, width), f32)

    @pl.when(step == 0)
    def _():
        gk_acc[...] = gk_in[...] if carried else jnp.zeros_like(gk_acc)
        gv_acc[...] = gv_in[...] if carried else jnp.zeros_like(gv_acc)

    for h in range(heads):
        mine = lane == h
        qh = jnp.where(mine, q, jnp.zeros_like(q))
        gh = jnp.where(mine, g, jnp.zeros_like(g))
        s = dot_nt(qh, k) * SCORE_SCALE + bias
        p = jnp.exp2(s - lse[:, h : h + 1])
        dp = dot_nt(gh, v)
        inner = jnp.sum(p * dp, axis=1, keepdims=True)
        ds = (p * (dp - inner)).astype(bf16)
        p_low = p.astype(bf16)
        gq = jnp.where(mine, dot_nn(ds, k), gq)
        gk_acc[...] += dot_tn(ds, qh)
        gv_acc[...] += dot_tn(p_low, gh)
    gq_ref[...] = (gq * 0.125).astype(bf16)

    @pl.when(step == pl.num_programs(0) - 1)
    def _():
        scale = 0.125 if carried else 1.0
        gk_ref[...] = (gk_acc[...] * scale).astype(gk_ref.dtype)
        gv_ref[...] = gv_acc[...].astype(gv_ref.dtype)


def attn_bwd(q, g, k, v, bias, lse, block, sums=()):
    rows, width = q.shape
    keys = k.shape[0]
    full = pl.BlockSpec((keys, width), lambda i: (0, 0))
    part = pl.BlockSpec((block, width), lambda i: (i, 0))
    sum_type = bf16 if sums else f32
    return pl.pallas_call(
        functools.partial(attn_bwd_kernel, bool(sums)),
        grid=(rows // block,),
        in_specs=[
            part,
            part,
            full,
            full,
            pl.BlockSpec((1, keys), lambda i: (0, 0)),
            pl.BlockSpec((block, 128), lambda i: (i, 0)),
        ]
        + [full] * len(sums),
        out_specs=[part, full, full],
        out_shape=[
            jax.ShapeDtypeStruct((rows, width), bf16),
            jax.ShapeDtypeStruct((keys, width), sum_type),
            jax.ShapeDtypeStruct((keys, width), sum_type),
        ],
        scratch_shapes=[pltpu.VMEM((keys, width), f32), pltpu.VMEM((keys, width), f32)],
        compiler_params=pltpu.CompilerParams(vmem_limit_bytes=VMEM_LIMIT),
        cost_estimate=pl.CostEstimate(flops=1024, bytes_accessed=1024, transcendentals=0),
        name="attn_bwd",
    )(q, g, k, v, bias, lse, *sums)


in_vmem = pl.BlockSpec(memory_space=pltpu.VMEM)
STRIP = 1024
LANES = 128


def strip(index, size=STRIP):
    return pl.ds(pl.multiple_of(index * size, size), size)


def shape(rows, cols, dtype=f32):
    return jax.ShapeDtypeStruct((rows, cols), dtype)


def whole(kernel, name, inputs, outputs, scalars=None, filled=(), sems=0, scratch=()):
    lead = [] if scalars is None else [scalars]
    anywhere = pl.BlockSpec(memory_space=pl.ANY)
    given = [v for v in filled if not isinstance(v, jax.ShapeDtypeStruct)]
    begun = [jax.ShapeDtypeStruct(v.shape, v.dtype) for v in filled]
    first = len(lead) + len(inputs)
    return pl.pallas_call(
        kernel,
        in_specs=[pl.BlockSpec(memory_space=pltpu.SMEM)] * len(lead)
        + [in_vmem] * len(inputs)
        + [anywhere] * len(given),
        out_specs=[anywhere] * len(begun) + [in_vmem] * len(outputs),
        out_shape=begun + list(outputs),
        scratch_shapes=list(scratch) + ([pltpu.SemaphoreType.DMA((sems,))] if sems else []),
        input_output_aliases={first + p: p for p in range(len(given))},
        compiler_params=pltpu.CompilerParams(vmem_limit_bytes=ROW_LIMIT),
        cost_estimate=pl.CostEstimate(flops=1024, bytes_accessed=1024, transcendentals=0),
        name=name,
    )(*lead, *inputs, *given)


class Copies:
    def __init__(self, sems):
        self.sems, self.made = sems, []

    def start(self, source, target):
        copy = pltpu.make_async_copy(source, target, self.sems.at[len(self.made)])
        copy.start()
        self.made.append(copy)

    def wait(self):
        for copy in self.made:
            copy.wait()


def project_kernel(mine_ref, near_ref, other_ref, o_near_ref, o_got_ref, o_other_ref, own_ref, sib_ref, low_ref, o_far_ref):
    rows = own_ref.shape[0]
    part = o_got_ref.shape[0]
    first = mine_ref[0] == 0
    o_far_ref[:part, :] = jnp.where(first, o_got_ref[...], o_other_ref[...]).astype(bf16)
    o_far_ref[part:, :] = jnp.where(first, o_other_ref[...], o_got_ref[...]).astype(bf16)
    low_ref[...] = other_ref[...].astype(bf16)
    both = dot_nn(near_ref[...], o_near_ref[...]) + dot_nn(low_ref[...], o_far_ref[...])
    own_ref[...] = both[:rows]
    sib_ref[...] = both[rows:]


def mean_of(values):
    return jnp.sum(values, axis=-1, keepdims=True) * (1.0 / values.shape[-1])


def norm_rows(values):
    centre = values - mean_of(values)
    scale_inv = lax.rsqrt(mean_of(centre * centre) + NORM_EPS)
    return centre * scale_inv, scale_inv


def norm_rows_back(grad_rows, unit_rows, scale_inv, gain):
    scaled = grad_rows * gain
    return scale_inv * (scaled - mean_of(scaled) - unit_rows * mean_of(scaled * unit_rows))


def first_norm_kernel(own_ref, near_ref, tok_ref, vec_ref, na_ref, nb_ref, all_ref, unit_ref, inv_ref):
    gain = vec_ref[1:2, :]
    shift = vec_ref[2:3, :]
    for half, out_ref in enumerate((na_ref, nb_ref)):
        size = out_ref.shape[0]
        rows = pl.ds(half * size, size)
        values = tok_ref[rows, :].astype(f32) + (own_ref[rows, :] + near_ref[rows, :] + vec_ref[0:1, :])
        unit, scale_inv = norm_rows(values)
        unit_ref[rows, :] = unit
        inv_ref[rows, :] = jnp.broadcast_to(scale_inv, (size, inv_ref.shape[1]))
        normed = unit * gain + shift
        out_ref[...] = normed
        all_ref[rows, :] = normed


def move_columns(source, target, blocks):
    wide = source.shape[1] // len(blocks)
    for place, block in enumerate(blocks):
        target[:, place * wide : (place + 1) * wide] = source[:, block * wide : (block + 1) * wide]


def order_kernel(blocks_a, blocks_b, in_ref, a_ref, b_ref):
    move_columns(in_ref, a_ref, blocks_a)
    move_columns(in_ref, b_ref, blocks_b)


def widen_part_kernel(mine_ref, in_ref, out_ref):
    out_ref[...] = in_ref[strip(mine_ref[0], out_ref.shape[0]), :].astype(f32)


def widen_kernel(a_ref, b_ref, wide_ref):
    rows = a_ref.shape[0]
    wide_ref[:rows, :] = a_ref[...].astype(f32)
    wide_ref[rows:, :] = b_ref[...].astype(f32)


def qkv_kernel(index_ref, all_ref, qw_ref, kw_ref, vw_ref, qb_ref, vb_ref, local_ref, near_ref, far_ref, k_ref, v_ref):
    half = near_ref.shape[0]
    rows = half // 2
    for p in range(4):
        local_ref[p * rows : (p + 1) * rows, :] = all_ref[strip(index_ref[p], rows), :]
    k_ref[...] = dot_nn(local_ref[...], kw_ref[...]).astype(bf16)
    v_ref[...] = (dot_nn(local_ref[...], vw_ref[...]) + vb_ref[...].astype(f32)).astype(bf16)
    q = (dot_nn(local_ref[...], qw_ref[...]) + qb_ref[...].astype(f32)).astype(bf16)
    near_ref[...] = q[:half]
    far_ref[...] = q[half:]


def add_kernel(*refs):
    total = refs[0][...]
    for ref in refs[1:-1]:
        total = total + ref[...]
    refs[-1][...] = total


def add(*values):
    return whole(add_kernel, "add", list(values), [shape(*values[0].shape)])[0]


def pair_kernel(side, fill, mine_ref, left_ref, right_ref, *refs):
    mine = mine_ref[0]
    half = left_ref.shape[1] // 2
    hidden = right_ref.shape[1] // 2
    right = right_ref[:, side * hidden : (side + 1) * hidden]
    for kept in range(2):
        start = pl.multiple_of((mine if kept else 1 - mine) * half, 128)
        value = dot_tn(left_ref[:, pl.ds(start, half)], right)
        if fill:
            refs[1 + kept][...] = value + refs[0][kept * half : (kept + 1) * half, :]
        else:
            refs[0][kept * half : (kept + 1) * half, :] = value


def fold_kernel(riders, ends, mine_ref, total_ref, got_ref, *refs):
    rows = total_ref.shape[0]
    if riders:
        extra_ref = refs[0]
        refs = refs[1:]
        extra = extra_ref[...] + got_ref[rows:, :]
    if ends:
        refs[0][...] = total_ref[...] + got_ref[:rows, :]
        if riders:
            refs[1][...] = extra
        return
    half = rows // 2
    away = strip(1 - mine_ref[0], half)
    kept = strip(mine_ref[0], half)
    refs[0][:half, :] = total_ref[away, :] + got_ref[away, :]
    refs[1][...] = total_ref[kept, :] + got_ref[kept, :]
    if riders:
        refs[0][half:, :] = extra
        refs[2][...] = extra


def qk_kernel(mine_ref, left_ref, near_ref, far_ref, gk_ref, away_ref, kept_ref):
    mine = mine_ref[0]
    half = left_ref.shape[1] // 2
    rows = near_ref.shape[0]
    wide = near_ref.shape[1]
    for kept, ref in enumerate((away_ref, kept_ref)):
        cols = pl.ds(pl.multiple_of((mine if kept else 1 - mine) * half, 128), half)
        ref[:, :wide] = dot_tn(left_ref[:rows, cols], near_ref[...]) + dot_tn(left_ref[rows:, cols], far_ref[...])
        ref[:, wide:] = dot_tn(left_ref[:, cols], gk_ref[...])


def vo_kernel(mine_ref, left_ref, gv_ref, kept_o_ref, got_o_ref, near_ref, far_ref, chip_ref, far_sums_ref, ub_ref, sib_ref, away_ref, kept_ref, extra_ref):
    mine = mine_ref[0]
    half = left_ref.shape[1] // 2
    wide = gv_ref.shape[1]
    riders = chip_ref.shape[0]
    extra_ref[...] = jnp.zeros_like(extra_ref)
    shared = chip_ref[...] + far_sums_ref[far_sums_ref.shape[0] - riders :, :]
    extra_ref[: riders // 2, :wide] = shared[: riders // 2]
    extra_ref[: riders // 2, wide:] = shared[riders // 2 :]
    row = riders // 2
    ones = (jnp.sum(near_ref[...].astype(f32), axis=0, keepdims=True) + jnp.sum(far_ref[...].astype(f32), axis=0, keepdims=True))
    extra_ref[row : row + 1, :wide] = ones
    extra_ref[row : row + 1, wide:] = jnp.sum(gv_ref[...].astype(f32), axis=0, keepdims=True)
    place = sib_ref.shape[0] - 8
    for k in range(ub_ref.shape[1] // (2 * wide)):
        cols = slice(2 * k * wide, 2 * (k + 1) * wide)
        extra_ref[row + 1 + k : row + 2 + k, :] = ub_ref[:, cols] + sib_ref[place : place + 1, cols]
    for kept, ref in enumerate((away_ref, kept_ref)):
        start = pl.multiple_of((mine if kept else 1 - mine) * half, 128)
        ref[:half, :wide] = dot_tn(left_ref[:, pl.ds(start, half)], gv_ref[...])
        rows = pl.ds(start, half)
        ref[:half, wide:] = kept_o_ref[rows, :] + got_o_ref[rows, :]
    away_ref[half:, :] = extra_ref[...]


def o_kernel(cols_ref, other_ref, near_ref, away_ref, kept_ref):
    away_ref[...] = dot_tn(cols_ref[...], other_ref[...])
    kept_ref[...] = dot_tn(cols_ref[...], near_ref[...])


def round_kernel(wide_ref, a_ref, b_ref):
    rows = a_ref.shape[0]
    a_ref[...] = wide_ref[:rows, :].astype(bf16)
    b_ref[...] = wide_ref[rows:, :].astype(bf16)


def feed_kernel(own, unit, blocks, targets, fresh, *refs):
    in_ref, up_ref, up2_ref, bias_ref, down_ref, down2_ref, shift_ref = refs[:7]
    refs = refs[7 + (0 if fresh else 2) :]
    lo_full, act_full, slope_ref = refs[:3]
    parts = refs[3:-4]
    low_ref, act_ref, cols_ref, sems = refs[-4:]
    hidden = up_ref.shape[1]
    copies = Copies(sems)
    low_ref[...] = in_ref[...].astype(bf16)
    if blocks:
        move_columns(low_ref, cols_ref, blocks)
    else:
        cols_ref[...] = low_ref[...]
    for p, target in enumerate(targets):
        copies.start(cols_ref.at[pl.ds(p * unit, unit), :], lo_full.at[pl.ds(target * unit, unit), :])
    for side, weight_ref in enumerate((up_ref, up2_ref)):

        @pl.loop(0, hidden // STRIP)
        def _(i):
            there = strip(i + side * (hidden // STRIP))
            pre = dot_nn(low_ref[...], weight_ref[:, strip(i)]) + bias_ref[:, there]
            normal_cdf = 0.5 * (1.0 + lax.erf(pre * ROOT_HALF))
            density = jnp.exp(-0.5 * pre * pre) * INV_ROOT_TAU
            act_ref[:, there] = (pre * normal_cdf).astype(bf16)
            slope_ref[:, there] = normal_cdf + pre * density

    for p, target in enumerate(targets):
        copies.start(act_ref.at[pl.ds(p * unit, unit), :], act_full.at[pl.ds(target * unit, unit), :])

    @pl.loop(0, down_ref.shape[1] // STRIP)
    def _(i):
        cols = strip(i)
        part = dot_nn(act_ref[:, :hidden], down_ref[:, cols]) + dot_nn(act_ref[:, hidden:], down2_ref[:, cols])
        if own:
            part = part + (in_ref[:, cols] + shift_ref[:, cols])
        for p, part_ref in enumerate(parts):
            part_ref[:, cols] = part[p * unit : (p + 1) * unit]

    copies.wait()


def feed(own, unit, blocks, targets, rows_in, ups, up_bias, downs, down_bias, filled):
    rows, width = rows_in.shape
    hidden = 2 * ups[0].shape[1]
    return whole(
        functools.partial(feed_kernel, own, unit, blocks, targets, not filled),
        "feed",
        [rows_in, *ups, up_bias, *downs, down_bias],
        [shape(rows, hidden)] + [shape(unit, width)] * len(targets),
        filled=filled or [shape(4 * unit, width, bf16), shape(4 * unit, hidden, bf16)],
        scratch=[
            pltpu.VMEM((rows, width), bf16),
            pltpu.VMEM((rows, hidden), bf16),
            pltpu.VMEM((rows, width), bf16),
        ],
        sems=2 * len(targets),
    )


def back_kernel(own, blocks, offset, target, fresh, spot_ref, y_ref, og_ref, extra_ref, vec_ref, slope_ref, down_ref, down2_ref, up_ref, up2_ref, *refs):
    refs = refs[0 if fresh else 3 :]
    out_full, gf_full, gp_full, part_ref, ub_ref, mark_ref = refs[:6]
    refs = refs[6:]
    if own:
        two_ref, sums_ref = refs[:2]
        refs = refs[2:]
    gf_ref, out_ref, gp_ref, cols_ref, sems = refs
    rows = y_ref.shape[0]
    hidden = up_ref.shape[1]
    gain = vec_ref[0:1, :]
    shift = vec_ref[1:2, :]
    copies = Copies(sems)
    ids = lax.broadcasted_iota(jnp.int32, (rows, 1), 0)
    base = pl.multiple_of(spot_ref[0], rows)
    limit = spot_ref[1]
    spot = spot_ref[2]
    there = pl.ds(target * rows, rows)
    keep = (ids < limit).astype(f32)
    unit, scale_inv = norm_rows(y_ref[...])
    out_ref[...] = (unit * gain + shift) * keep
    copies.start(out_ref, out_full.at[there, :])
    grad_out = (og_ref[pl.ds(base, rows), :].astype(f32) + jnp.where(ids == spot, extra_ref[...], 0.0)) * keep
    grad_two = norm_rows_back(grad_out, unit, scale_inv, gain)
    grad_low = grad_two.astype(bf16)
    gf_ref[...] = grad_low
    if own:
        two_ref[...] = grad_two
        sums_ref[0:1, :] = jnp.sum(grad_low.astype(f32), axis=0, keepdims=True)
        sums_ref[1:2, :] = jnp.sum(grad_out * unit, axis=0, keepdims=True)
        sums_ref[2:3, :] = jnp.sum(grad_out, axis=0, keepdims=True)
        sums_ref[3:8, :] = jnp.zeros((5, sums_ref.shape[1]), f32)
    mark_ref[...] = jnp.zeros_like(mark_ref)

    @pl.when((spot >= 0) & (spot < rows))
    def _():
        row, _ = norm_rows(y_ref[pl.ds(jnp.clip(spot, 0, rows - 1), 1), :])
        mark_ref[0:1, :] = row * gain + shift

    if blocks:
        move_columns(gf_ref, cols_ref, blocks)
    else:
        cols_ref[...] = gf_ref[...]
    copies.start(cols_ref, gf_full.at[there, :])
    for side, weight_ref in enumerate((down_ref, down2_ref)):

        @pl.loop(0, hidden // STRIP)
        def _(i):
            cols = strip(i + side * (hidden // STRIP))
            grad_act = dot_nt(gf_ref[...], weight_ref[strip(i), :])
            grad_pre = (grad_act * slope_ref[pl.ds(offset, rows), cols]).astype(bf16)
            gp_ref[:, cols] = grad_pre
            ub_ref[:, cols] = jnp.sum(grad_pre.astype(f32), axis=0, keepdims=True)

    copies.start(gp_ref, gp_full.at[there, :])

    @pl.loop(0, up_ref.shape[0] // STRIP)
    def _(i):
        cols = strip(i)
        part_ref[:, cols] = dot_nt(gp_ref[:, :hidden], up_ref[cols, :]) + dot_nt(gp_ref[:, hidden:], up2_ref[cols, :])

    copies.wait()


def back(own, blocks, offset, target, scalars, y, out_grad, extra, vectors, slope, downs, ups, filled):
    rows, width = y.shape
    hidden = 2 * ups[0].shape[1]
    outputs = [shape(rows, width), shape(1, hidden), shape(8, width)]
    if own:
        outputs += [shape(rows, width), shape(8, width)]
    return whole(
        functools.partial(back_kernel, own, blocks, offset, target, not filled),
        "feed_back",
        [y, out_grad, extra, vectors, slope, *downs, *ups],
        outputs,
        scalars=scalars,
        filled=filled
        or [shape(4 * rows, width), shape(4 * rows, width, bf16), shape(4 * rows, hidden, bf16)],
        scratch=[
            pltpu.VMEM((rows, width), bf16),
            pltpu.VMEM((rows, width), f32),
            pltpu.VMEM((rows, hidden), bf16),
            pltpu.VMEM((rows, width), bf16),
        ],
        sems=3,
    )


def context_back_kernel(blocks, own_ref, first_ref, sib_ref, near_w_ref, far_w_ref, far_ref, near_ref, sums_ref, *refs):
    low_ref = refs[-1]
    rows = own_ref.shape[0]
    low_ref[:rows, :] = own_ref[...]
    low_ref[rows:, :] = sib_ref[:rows, :].astype(bf16)
    wide = far_ref.shape[1]
    far_ref[: 2 * rows, :] = dot_nt(low_ref[...], far_w_ref[...])
    near_ref[...] = dot_nt(low_ref[...], near_w_ref[...]).astype(bf16)
    for k in range(first_ref.shape[1] // wide):
        cols = slice(k * wide, (k + 1) * wide)
        chip = first_ref[rows : rows + 8, cols] + sib_ref[rows : rows + 8, cols]
        sums_ref[8 * k : 8 * k + 8, :] = chip
        far_ref[2 * rows + 8 * k : 2 * rows + 8 * k + 8, :] = chip
    if blocks:
        move_columns(low_ref, refs[0], blocks)


def first_back_kernel(*refs):
    streams = (refs[:4], refs[4:8])
    ub_refs = refs[8:12]
    marks = refs[12:16]
    unit_ref, inv_ref, vec_ref, first_ref, low_ref, ub_ref = refs[16:]
    hidden = ub_ref.shape[1]
    ub = ub_refs[0][...] + ub_refs[1][...] + ub_refs[2][...] + ub_refs[3][...]
    ub_ref[...] = ub[:, :hidden]
    gain = vec_ref[1:2, :]
    size, width = streams[0][0].shape
    rows = 2 * size
    sums = [0.0] * 6
    for half, (two_ref, own_ref, chip_ref, ffn_ref) in enumerate(streams):
        here = pl.ds(half * size, size)
        grad_normed = two_ref[...] + (own_ref[...] + chip_ref[...])
        unit = unit_ref[here, :]
        first = norm_rows_back(grad_normed, unit, inv_ref[here, 0:1], gain)
        low = first.astype(bf16)
        first_ref[here, :] = first
        low_ref[here, :] = low
        terms = [low.astype(f32), grad_normed * unit, grad_normed]
        for k in range(3):
            sums[k] = sums[k] + jnp.sum(terms[k], axis=0, keepdims=True)
            sums[k + 3] = sums[k + 3] + ffn_ref[k : k + 1, :]
    for k in range(6):
        first_ref[rows + k : rows + k + 1, :] = sums[k]
    first_ref[rows + 6 : rows + 8, :] = jnp.zeros((2, width), f32)
    first_ref[rows + 8 : rows + 9, :] = ub[:, hidden:]
    first_ref[rows + 9 : rows + 10, :] = marks[0][0:1, :] + marks[1][0:1, :]
    first_ref[rows + 10 : rows + 11, :] = marks[2][0:1, :] + marks[3][0:1, :]
    first_ref[rows + 11 : rows + 16, :] = jnp.zeros((5, width), f32)


def input_kernel(index_ref, near_ref, far_ref, gk_ref, gv_ref, qw_ref, kw_ref, vw_ref, first_ref, out_ref):
    rows = near_ref.shape[0] // 2
    for p in range(4):
        gq_ref = (near_ref, far_ref)[p // 2]
        mine = pl.ds(p * rows, rows)
        value = (
            dot_nt(gq_ref[pl.ds((p % 2) * rows, rows), :], qw_ref[...])
            + dot_nt(gk_ref[mine, :], kw_ref[...])
            + dot_nt(gv_ref[mine, :], vw_ref[...])
        )
        if p == 0:
            value = value + first_ref[:rows, :]
        out_ref[strip(index_ref[p], rows), :] = value


def round_place_kernel(index_ref, near_ref, far_ref, out_ref, low_ref, sems):
    rows = near_ref.shape[0] // 2
    copies = Copies(sems)
    for p, ref in enumerate((near_ref, far_ref)):
        low_ref[2 * rows * p : 2 * rows * (p + 1), :] = ref[...].astype(bf16)
    for p in range(4):
        there = pl.ds(pl.multiple_of(index_ref[p] * rows, rows), rows)
        copies.start(low_ref.at[pl.ds(p * rows, rows), :], out_ref.at[there, :])
    copies.wait()


def swap_core(value):
    return lax.ppermute(value, "mp", [(i, i ^ 1) for i in range(4)])


def swap_chip(value):
    return lax.ppermute(value, "mp", [(i, i ^ 2) for i in range(4)])


def gather_rows(own):
    other = swap_chip(own)
    sibling = swap_core(own)
    diagonal = swap_core(other)
    return own, sibling, other, diagonal


def bit_order_blocks(parts, order):
    bits = len(order)
    blocks = []
    for position in range(parts):
        block = 0
        for level, bit in enumerate(order):
            block |= ((position >> (bits - 1 - level)) & 1) << bit
        blocks.append(block)
    return blocks


def bit_order_columns(matrix, parts, order):
    width = matrix.shape[1] // parts
    return jnp.concatenate(
        [matrix[:, b * width : (b + 1) * width] for b in bit_order_blocks(parts, order)], axis=1
    )


def dp_swap(value, parts, bit):
    return lax.ppermute(value, "dp", [(i, i ^ (1 << bit)) for i in range(parts)])


class Sum:
    def __init__(self, parts, order, place, line):
        self.parts, self.order, self.line = parts, list(order), line
        self.bits = [((place >> bit) & 1).astype(jnp.int32)[None] for bit in order]
        self.extra = self.total = self.got = None

    def begin(self, away, total, extra=None):
        self.total, self.extra = total, extra
        self.level = 0
        self.ship(away)

    def ship(self, away):
        self.got = dp_swap(away, self.parts, self.order[self.level])
        self.level += 1
        self.line.mark(away)

    def step(self):
        if self.got is None:
            return
        got = self.line.hold(self.got)
        self.got = None
        rows, cols = self.total.shape
        ends = self.level == len(self.order)
        riders = 0 if self.extra is None else self.extra.shape[0]
        mine = self.bits[0 if ends else self.level]
        rest = [shape(riders, cols)] if riders else []
        outputs = [shape(rows, cols)] if ends else [shape(rows // 2 + riders, cols), shape(rows // 2, cols)]
        given = [self.total, got] + ([self.extra] if riders else [])
        result = whole(
            functools.partial(fold_kernel, riders, ends), "fold", given, outputs + rest, scalars=mine
        )
        if riders:
            self.extra = result[-1]
        if ends:
            self.total = result[0]
            self.line.mark(self.total)
        else:
            self.total = result[1]
            self.ship(result[0])

    def finish(self):
        while self.got is not None:
            self.step()
        return self.total


class Line:
    def __init__(self):
        self.token = None

    def mark(self, *values):
        self.token = values

    def hold(self, *values):
        if self.token is not None:
            values = lax.optimization_barrier(tuple(values) + self.token)[: len(values)]
        return values if len(values) > 1 else values[0]


def shards(
    dp_size,
    tokens,
    doc_lengths,
    cls_pos,
    cls_count,
    q_weight,
    q_bias,
    k_weight,
    v_weight,
    v_bias,
    o_weight,
    o_bias,
    ln1_gain,
    ln1_bias,
    up_weight,
    up_bias,
    down_weight,
    down_bias,
    ln2_gain,
    ln2_bias,
    out_grad,
    pooled_grad,
):
    slot_len, width = tokens.shape
    rows = slot_len // 4
    half = 2 * rows
    head_width = q_weight.shape[1]
    rank = lax.axis_index("mp")
    place_id = lax.axis_index("dp")
    bits = dp_size.bit_length() - 1
    order_a = list(range(bits))
    order_b = [1, 0] + list(range(2, bits)) if bits > 1 else order_a
    length = doc_lengths[0]
    blocks = [rank ^ j for j in range(4)]

    def take(array, j):
        return lax.dynamic_slice_in_dim(array, blocks[j] * rows, rows, 0)

    line = Line()
    sizes = width // dp_size
    fixed_a = bit_order_blocks(dp_size, order_a) if sizes % 128 == 0 else None
    fixed_b = bit_order_blocks(dp_size, order_b) if sizes % 128 == 0 else None
    unit = rows // 2

    index = jnp.stack(blocks).astype(jnp.int32)

    mine = (place_id & 1).astype(jnp.int32)[None]
    o_part = whole(
        widen_part_kernel, "widen_part", [o_weight], [shape(head_width // 2, width)], scalars=mine
    )[0]
    o_got = swap_chip(o_part)
    line.mark(o_part)
    row_ids = lax.iota(jnp.int32, rows)
    positions = jnp.concatenate([row_ids + blocks[j] * rows for j in range(4)])
    bias = jnp.where(positions < length, 0.0, MASKED).astype(f32)[None, :]
    local, queries_near, queries_far, key_rows, value_rows = whole(
        qkv_kernel,
        "qkv",
        [line.hold(tokens), q_weight, k_weight, v_weight, q_bias[None], v_bias[None]],
        [shape(slot_len, width, bf16)] + [shape(half, head_width, bf16)] * 2 + [shape(slot_len, head_width, bf16)] * 2,
        scalars=index,
    )
    away_context, lse_far = attn_fwd(queries_far, key_rows, value_rows, bias, 256, f32)
    arrived = swap_chip(away_context)
    line.mark(away_context)
    o_got = line.hold(o_got)
    o_other = dp_swap(o_got, dp_size, 0)
    line.mark(o_got)
    up_held, down_held = line.hold(up_weight, down_weight)
    hidden = up_bias.shape[0]
    wide = whole(widen_kernel, "widen", [up_held, down_held], [shape(width + hidden, width)])[0]
    line.mark(wide)
    wide = swap_core(wide)
    context_near, lse_near = attn_fwd(line.hold(queries_near), key_rows, value_rows, bias, 256, bf16)
    line.mark(context_near)
    if fixed_a:
        local_a, local_b = whole(
            functools.partial(order_kernel, fixed_a, fixed_b),
            "order",
            [line.hold(local)],
            [shape(slot_len, width, bf16)] * 2,
        )
    else:
        local_a = bit_order_columns(local, dp_size, order_a)
        local_b = bit_order_columns(local, dp_size, order_b)
    line.mark(local_a)
    own, sib, context_other, o_far = whole(
        project_kernel,
        "project",
        [context_near, line.hold(arrived), o_weight, o_got, line.hold(o_other)],
        [shape(rows, width), shape(rows, width), shape(half, head_width, bf16), shape(head_width, width, bf16)],
        scalars=mine,
    )
    vectors_one = jnp.stack([o_bias, ln1_gain, ln1_bias]).astype(f32)
    vectors_two = jnp.stack([ln2_gain, ln2_bias]).astype(f32)
    bias_here = up_bias.astype(f32)
    up_row = jnp.concatenate([bias_here, swap_core(bias_here)])[None]
    down_row = down_bias.astype(f32)[None]
    n_a, n_b, normed, unit_one, inv_one = whole(
        first_norm_kernel,
        "first_norm",
        [own, swap_core(sib), local, vectors_one],
        [shape(unit, width), shape(unit, width), shape(rows, width), shape(rows, width), shape(rows, 128)],
    )
    line.mark(n_a)
    chip_a = swap_chip(n_a)
    chip_b = swap_chip(n_b)
    up_far, down_far = whole(
        round_kernel, "round", [line.hold(wide)], [shape(width, hidden, bf16), shape(hidden, width, bf16)]
    )
    ups = (up_weight, up_far)
    downs = (down_weight, down_far)
    scalars = []
    extras = []
    for j in (0, 2):
        spot = lax.dynamic_index_in_dim(cls_pos[0], blocks[j], keepdims=False) - blocks[j] * rows
        live = blocks[j] < cls_count[0]
        extras.append(lax.dynamic_index_in_dim(pooled_grad[0], blocks[j], keepdims=True))
        for k in range(2):
            base = blocks[j] * rows + k * unit
            scalars.append(jnp.stack([base, length - base, jnp.where(live, spot - k * unit, -1)]).astype(jnp.int32))

    lo, act, slope_near, own_a, own_b = feed(True, unit, fixed_b, (0, 1), normed, ups, up_row, downs, down_row, ())
    line.mark(own_a)
    lo, act, slope_a, part = feed(
        False, unit, fixed_b, (2,), line.hold(chip_a), ups, up_row, downs, down_row, (lo, act)
    )
    got_a = swap_chip(part)
    line.mark(part)
    lo, act, slope_b, part = feed(
        False, unit, fixed_b, (3,), line.hold(chip_b), ups, up_row, downs, down_row, (lo, act)
    )
    got_b = swap_chip(part)
    line.mark(part)

    def back_rows(own, k, y, slope, offset, filled):
        place = k if own else 2 + k
        return back(
            own, fixed_a, offset, place, scalars[place], y, out_grad, extras[0 if own else 1], vectors_two,
            slope, downs, ups, filled,
        )

    y_a = add(own_a, line.hold(got_a))
    chip_a = swap_chip(y_a)
    *filled, back_a, ub_a, mark_a, two_a, sums_a = back_rows(True, 0, y_a, slope_near, 0, ())
    line.mark(back_a)
    y_b = add(own_b, line.hold(got_b))
    chip_b = swap_chip(y_b)
    *filled, back_b, ub_b, mark_b, two_b, sums_b = back_rows(True, 1, y_b, slope_near, unit, filled)
    line.mark(back_b)
    *filled, part, ub_c, mark_c = back_rows(False, 0, line.hold(chip_a), slope_a, 0, filled)
    got_a = swap_chip(part)
    line.mark(part)
    *filled, part, ub_d, mark_d = back_rows(False, 1, line.hold(chip_b), slope_b, 0, filled)
    got_b = swap_chip(part)
    line.mark(part)
    out_wide, grad_fed, grad_pre = filled

    def in_order(value, fixed, order):
        return value if fixed else bit_order_columns(value, dp_size, order)

    gf_cols, lo_cols = in_order(grad_fed, fixed_a, order_a), in_order(lo, fixed_b, order_b)
    down_sum = Sum(dp_size, order_a, place_id, line)
    up_sum = Sum(dp_size, order_b, place_id, line)

    def pair(side, sum_of, left, right, given=()):
        half_rows = width // 2
        return whole(
            functools.partial(pair_kernel, side, bool(given)),
            "pair",
            [left, right, *given],
            [shape(half_rows, hidden)] * 2 if given else [shape(width, hidden)],
            scalars=sum_of.bits[0],
        )

    down_other = pair(1, down_sum, line.hold(gf_cols), act)[0]
    down_given = swap_core(down_other)
    line.mark(down_other)
    up_other = pair(1, up_sum, lo_cols, line.hold(grad_pre))[0]
    up_given = swap_core(up_other)
    line.mark(up_other)

    down_sum.begin(*pair(0, down_sum, gf_cols, act, [line.hold(down_given)]))
    up_sum.begin(*pair(0, up_sum, lo_cols, grad_pre, [line.hold(up_given)]))

    got_a, got_b = line.hold(got_a, got_b)
    first_ext, grad_attended_own, up_bias_own = whole(
        first_back_kernel,
        "first_norm_back",
        [two_a, back_a, got_a, sums_a, two_b, back_b, got_b, sums_b, ub_a, ub_b, ub_c, ub_d]
        + [mark_a, mark_b, mark_c, mark_d, unit_one, inv_one, vectors_one],
        [shape(rows + 16, width), shape(rows, width, bf16), shape(1, hidden)],
    )
    sib_ext = swap_core(first_ext)
    riders = 8 * width // head_width
    context_far_grad, grad_context_near, chip_sums, *ga_cols = whole(
        functools.partial(context_back_kernel, fixed_b),
        "context_back",
        [grad_attended_own, first_ext, sib_ext, o_weight, o_far],
        [shape(half + riders, head_width), shape(half, head_width, bf16), shape(riders, head_width)]
        + [shape(half, width, bf16)] * (2 if fixed_b else 1),
    )
    ga_cols = in_order(ga_cols[0], fixed_b, order_b)
    grad_context_far = swap_chip(context_far_grad)
    line.mark(context_far_grad)

    queries_near = line.hold(queries_near)
    grad_q_near, key_sum, value_sum = attn_bwd(
        queries_near, grad_context_near, key_rows, value_rows, bias, lse_near, 256
    )
    line.mark(grad_q_near)
    grad_context_far = line.hold(grad_context_far)
    line.mark(grad_context_far)
    o_away, o_kept = whole(
        o_kernel, "o_grad", [line.hold(ga_cols), context_other, context_near], [shape(width, head_width)] * 2
    )
    o_got = swap_chip(o_away)
    line.mark(o_away)
    queries_far = line.hold(queries_far)
    grad_q_far, grad_k, grad_v = attn_bwd(
        queries_far, grad_context_far, key_rows, value_rows, bias, lse_far, 256, (key_sum, value_sum)
    )
    line.mark(grad_k)

    in_part = whole(
        input_kernel,
        "input_grad",
        [grad_q_near, grad_q_far, grad_k, grad_v, q_weight, k_weight, v_weight, first_ext],
        [shape(slot_len, width)],
        scalars=index,
    )[0]
    in_grad = lax.psum(in_part, "mp")
    line.mark(in_part)
    qk_sum = Sum(dp_size, order_a, place_id, line)
    vo_sum = Sum(dp_size, order_b, place_id, line)
    qk_away, qk_kept = whole(
        qk_kernel,
        "qk_grad",
        [local_a, line.hold(grad_q_near), grad_q_far, grad_k],
        [shape(width // 2, 2 * head_width)] * 2,
        scalars=qk_sum.bits[0],
    )
    line.mark(qk_away)
    riders = 8 * width // head_width
    extra_rows = -(-(riders // 2 + 1 + hidden // (2 * head_width)) // 8) * 8
    down_sum.step()
    up_sum.step()
    qk_sum.begin(qk_away, qk_kept)
    vo_away, vo_kept, vo_extra = whole(
        vo_kernel,
        "vo_grad",
        [local_b, line.hold(grad_v), o_kept, line.hold(o_got), grad_q_near, grad_q_far, chip_sums, grad_context_far]
        + [up_bias_own, sib_ext],
        [
            shape(width // 2 + extra_rows, 2 * head_width),
            shape(width // 2, 2 * head_width),
            shape(extra_rows, 2 * head_width),
        ],
        scalars=vo_sum.bits[0],
    )
    vo_sum.begin(vo_away, vo_kept, vo_extra)
    out_far = swap_core(line.hold(out_wide))
    for bit in range(bits):
        down_sum.step()
        up_sum.step()
        qk_sum.step()
        vo_sum.step()
        if bit == 0:
            in_grad = line.hold(in_grad)
            line.mark(in_grad)
    out_index = jnp.stack([blocks[0], blocks[2], blocks[1], blocks[3]]).astype(jnp.int32)
    out = whole(
        round_place_kernel,
        "round_place",
        [out_wide, out_far],
        [],
        scalars=out_index,
        filled=[shape(slot_len, width, bf16)],
        scratch=[pltpu.VMEM((slot_len, width), bf16)],
        sems=4,
    )[0]
    qk_sum, vo_total = qk_sum.finish(), vo_sum.finish()
    riding = vo_sum.extra
    row = riders // 2
    shared = jnp.concatenate([riding[:row, :head_width], riding[:row, head_width:]], axis=0)
    shared = shared.reshape(-1, 8, head_width).transpose(1, 0, 2).reshape(8, width)
    biases = riding[row].reshape(2, head_width)
    up_bias_sum = riding[row + 1 : row + 1 + hidden // (2 * head_width)].reshape(-1)
    v_sum = vo_total[:, :head_width]
    o_sum = vo_total[:, head_width:].T
    down_sum = down_sum.finish().T
    up_sum = up_sum.finish()

    mine = first_ext[rows + 9 : rows + 11]
    theirs = sib_ext[rows + 9 : rows + 11]
    marks = jnp.concatenate([mine[:1], theirs[:1], mine[1:], theirs[1:]], axis=0)
    pooled = jnp.concatenate(
        [lax.dynamic_index_in_dim(marks, blocks[j], keepdims=True) for j in range(4)], axis=0
    )[None]
    return (
        out,
        pooled,
        in_grad,
        qk_sum[:, :head_width],
        biases[0],
        qk_sum[:, head_width:],
        v_sum,
        biases[1],
        o_sum,
        shared[0],
        shared[1],
        shared[2],
        up_sum,
        up_bias_sum,
        down_sum,
        shared[3],
        shared[4],
        shared[5],
    )


def solution(mesh):
    return jax.shard_map(
        functools.partial(shards, mesh.shape["dp"]),
        mesh=mesh,
        in_specs=(
            P("dp", None),
            P("dp"),
            P("dp", None),
            P("dp"),
            P(None, "mp"),
            P("mp"),
            P(None, "mp"),
            P(None, "mp"),
            P("mp"),
            P("mp", None),
            P(),
            P(),
            P(),
            P(None, "mp"),
            P("mp"),
            P("mp", None),
            P(),
            P(),
            P(),
            P("dp", None),
            P("dp", None, None),
        ),
        out_specs=(
            P("dp", None),
            P("dp", None, None),
            P("dp", None),
            P("dp", "mp"),
            P("mp"),
            P("dp", "mp"),
            P("dp", "mp"),
            P("mp"),
            P("mp", "dp"),
            P(),
            P(),
            P(),
            P("dp", "mp"),
            P("mp"),
            P("mp", "dp"),
            P(),
            P(),
            P(),
        ),
        check_vma=False,
    )
```

```python
import functools

import jax
import jax.numpy as jnp
from jax import lax
from jax.experimental import pallas as pl
from jax.experimental.pallas import tpu as pltpu
from jax.sharding import PartitionSpec as P

HEAD_DIM = 64
NORM_EPS = 1e-05
ROOT_HALF = 0.7071067811865476
INV_ROOT_TAU = 0.3989422804014327
LOG2E = 1.4426950408889634
SCORE_SCALE = 0.125 * LOG2E
MASKED = -1e30

f32 = jnp.float32
bf16 = jnp.bfloat16
VMEM_LIMIT = 20 * 1024 * 1024


def dot_nn(a, b):
    return lax.dot_general(a, b, (((1,), (0,)), ((), ())), preferred_element_type=f32)


def dot_nt(a, b):
    return lax.dot_general(a, b, (((1,), (1,)), ((), ())), preferred_element_type=f32)


def dot_tn(a, b):
    return lax.dot_general(a, b, (((0,), (0,)), ((), ())), preferred_element_type=f32)


def attn_fwd_kernel(q_ref, k_ref, v_ref, bias_ref, o_ref, lse_ref):
    rows, width = q_ref.shape
    heads = width // HEAD_DIM
    lane = lax.broadcasted_iota(jnp.int32, (1, width), 1) // HEAD_DIM
    lse_lane = lax.broadcasted_iota(jnp.int32, (1, 128), 1)
    q = q_ref[...]
    k = k_ref[...]
    v = v_ref[...]
    bias = bias_ref[...]
    out = jnp.zeros((rows, width), f32)
    lse = jnp.zeros((rows, 128), f32)
    for h in range(heads):
        qh = jnp.where(lane == h, q, jnp.zeros_like(q))
        s = dot_nt(qh, k) * SCORE_SCALE + bias
        top = jnp.max(s, axis=1, keepdims=True)
        e = jnp.exp2(s - top)
        total = jnp.sum(e, axis=1, keepdims=True)
        p = (e * (1.0 / total)).astype(bf16)
        c = dot_nn(p, v)
        out = jnp.where(lane == h, c, out)
        lse = jnp.where(lse_lane == h, top + jnp.log2(total), lse)
    o_ref[...] = out.astype(o_ref.dtype)
    lse_ref[...] = lse


def attn_fwd(q, k, v, bias, block, dtype):
    rows, width = q.shape
    keys = k.shape[0]
    full = pl.BlockSpec((keys, width), lambda i: (0, 0))
    return pl.pallas_call(
        attn_fwd_kernel,
        grid=(rows // block,),
        in_specs=[
            pl.BlockSpec((block, width), lambda i: (i, 0)),
            full,
            full,
            pl.BlockSpec((1, keys), lambda i: (0, 0)),
        ],
        out_specs=[
            pl.BlockSpec((block, width), lambda i: (i, 0)),
            pl.BlockSpec((block, 128), lambda i: (i, 0)),
        ],
        out_shape=[
            jax.ShapeDtypeStruct((rows, width), dtype),
            jax.ShapeDtypeStruct((rows, 128), f32),
        ],
        compiler_params=pltpu.CompilerParams(vmem_limit_bytes=VMEM_LIMIT),
        cost_estimate=pl.CostEstimate(flops=1024, bytes_accessed=1024, transcendentals=0),
        name="attn_fwd",
    )(q, k, v, bias)


def attn_bwd_kernel(carried, *refs):
    q_ref, g_ref, k_ref, v_ref, bias_ref, lse_ref = refs[:6]
    refs = refs[6:]
    if carried:
        gk_in, gv_in = refs[:2]
        refs = refs[2:]
    gq_ref, gk_ref, gv_ref, gk_acc, gv_acc, gq_acc = refs
    step = pl.program_id(0)
    width = q_ref.shape[1]
    lane = lax.broadcasted_iota(jnp.int32, (1, width), 1) // HEAD_DIM
    lse_lane = lax.broadcasted_iota(jnp.int32, (1, 128), 1)

    @pl.when(step == 0)
    def _():
        gk_acc[...] = gk_in[...] if carried else jnp.zeros_like(gk_acc)
        gv_acc[...] = gv_in[...] if carried else jnp.zeros_like(gv_acc)

    @pl.loop(0, width // HEAD_DIM)
    def _(h):
        mine = lane == h
        zero = jnp.zeros(q_ref.shape, bf16)
        qh = jnp.where(mine, q_ref[...], zero)
        gh = jnp.where(mine, g_ref[...].astype(bf16), zero)
        lse = jnp.sum(jnp.where(lse_lane == h, lse_ref[...], 0.0), axis=1, keepdims=True)
        s = dot_nt(qh, k_ref[...]) * SCORE_SCALE + bias_ref[...]
        p = jnp.exp2(s - lse)
        dp = dot_nt(gh, v_ref[...])
        inner = jnp.sum(p * dp, axis=1, keepdims=True)
        ds = (p * (dp - inner)).astype(bf16)
        gq_acc[...] = jnp.where(mine, dot_nn(ds, k_ref[...]), gq_acc[...])
        gk_acc[...] += dot_tn(ds, qh)
        gv_acc[...] += dot_tn(p.astype(bf16), gh)

    gq_ref[...] = (gq_acc[...] * 0.125).astype(bf16)

    @pl.when(step == pl.num_programs(0) - 1)
    def _():
        scale = 0.125 if carried else 1.0
        gk_ref[...] = (gk_acc[...] * scale).astype(gk_ref.dtype)
        gv_ref[...] = gv_acc[...].astype(gv_ref.dtype)


def attn_bwd(q, g, k, v, bias, lse, block, sums=()):
    rows, width = q.shape
    keys = k.shape[0]
    full = pl.BlockSpec((keys, width), lambda i: (0, 0))
    part = pl.BlockSpec((block, width), lambda i: (i, 0))
    sum_type = bf16 if sums else f32
    return pl.pallas_call(
        functools.partial(attn_bwd_kernel, bool(sums)),
        grid=(rows // block,),
        in_specs=[
            part,
            part,
            full,
            full,
            pl.BlockSpec((1, keys), lambda i: (0, 0)),
            pl.BlockSpec((block, 128), lambda i: (i, 0)),
        ]
        + [full] * len(sums),
        out_specs=[part, full, full],
        out_shape=[
            jax.ShapeDtypeStruct((rows, width), bf16),
            jax.ShapeDtypeStruct((keys, width), sum_type),
            jax.ShapeDtypeStruct((keys, width), sum_type),
        ],
        scratch_shapes=[pltpu.VMEM((keys, width), f32)] * 2 + [pltpu.VMEM((block, width), f32)],
        compiler_params=pltpu.CompilerParams(vmem_limit_bytes=VMEM_LIMIT),
        cost_estimate=pl.CostEstimate(flops=1024, bytes_accessed=1024, transcendentals=0),
        name="attn_bwd",
    )(q, g, k, v, bias, lse, *sums)


in_vmem = pl.BlockSpec(memory_space=pltpu.VMEM)
STRIP = 256
LENGTH, COUNT, MARKS, BITS = 4, 5, 6, 10
O_BIAS, GAIN_ONE, SHIFT_ONE, GAIN_TWO, SHIFT_TWO, DOWN_BIAS, UP_BIAS, QV_BIAS = range(8)


def row_of(ref, index):
    return ref[index : index + 1, :]


def strip(index, size=STRIP):
    return pl.ds(pl.multiple_of(index * size, size), size)


def shape(rows, cols, dtype=f32):
    return jax.ShapeDtypeStruct((rows, cols), dtype)


def whole(kernel, name, inputs, outputs, scalars=None, filled=(), sems=0, scratch=(), limit=8, far=False):
    lead = [] if scalars is None else [scalars]
    anywhere = pl.BlockSpec(memory_space=pl.ANY)
    given = [v for v in filled if not isinstance(v, jax.ShapeDtypeStruct)]
    begun = [jax.ShapeDtypeStruct(v.shape, v.dtype) for v in filled]
    first = len(lead) + len(inputs)
    return pl.pallas_call(
        kernel,
        in_specs=[pl.BlockSpec(memory_space=pltpu.SMEM)] * len(lead)
        + [in_vmem] * len(inputs)
        + [anywhere] * len(given),
        out_specs=[pl.BlockSpec(memory_space=pltpu.HBM) if far else anywhere] * len(begun)
        + [in_vmem] * len(outputs),
        out_shape=begun + list(outputs),
        scratch_shapes=list(scratch) + ([pltpu.SemaphoreType.DMA((sems,))] if sems else []),
        input_output_aliases={first + p: p for p in range(len(given))},
        compiler_params=pltpu.CompilerParams(vmem_limit_bytes=limit * 1024 * 1024),
        cost_estimate=pl.CostEstimate(flops=1024, bytes_accessed=1024, transcendentals=0),
        name=name,
    )(*lead, *inputs, *given)


class Copies:
    def __init__(self, sems):
        self.sems, self.made = sems, []

    def start(self, source, target):
        copy = pltpu.make_async_copy(source, target, self.sems.at[len(self.made)])
        copy.start()
        self.made.append(copy)

    def wait(self):
        for copy in self.made:
            copy.wait()


def project_kernel(meta_ref, near_ref, other_ref, o_near_ref, o_got_ref, o_other_ref, own_ref, sib_ref, low_ref, o_far_ref):
    rows = own_ref.shape[0]
    part = o_got_ref.shape[0]
    first = meta_ref[BITS] == 0
    o_far_ref[:part, :] = jnp.where(first, o_got_ref[...], o_other_ref[...]).astype(bf16)
    o_far_ref[part:, :] = jnp.where(first, o_other_ref[...], o_got_ref[...]).astype(bf16)
    low_ref[...] = other_ref[...].astype(bf16)
    both = dot_nn(near_ref[...], o_near_ref[...]) + dot_nn(low_ref[...], o_far_ref[...])
    own_ref[...] = both[:rows]
    sib_ref[...] = both[rows:]


def mean_of(values):
    return jnp.sum(values, axis=-1, keepdims=True) * (1.0 / values.shape[-1])


def norm_rows(values):
    centre = values - mean_of(values)
    scale_inv = lax.rsqrt(mean_of(centre * centre) + NORM_EPS)
    return centre * scale_inv, scale_inv


def norm_rows_back(grad_rows, unit_rows, scale_inv, gain):
    scaled = grad_rows * gain
    return scale_inv * (scaled - mean_of(scaled) - unit_rows * mean_of(scaled * unit_rows))


def first_norm_kernel(own_ref, near_ref, tok_ref, vec_ref, na_ref, nb_ref, all_ref, unit_ref, inv_ref):
    gain = row_of(vec_ref, GAIN_ONE)
    shift = row_of(vec_ref, SHIFT_ONE)
    for half, out_ref in enumerate((na_ref, nb_ref)):
        size = out_ref.shape[0]
        rows = pl.ds(half * size, size)
        values = tok_ref[rows, :].astype(f32) + (own_ref[rows, :] + near_ref[rows, :] + row_of(vec_ref, O_BIAS))
        unit, scale_inv = norm_rows(values)
        unit_ref[rows, :] = unit
        inv_ref[rows, :] = jnp.broadcast_to(scale_inv, (size, inv_ref.shape[1]))
        normed = unit * gain + shift
        out_ref[...] = normed
        all_ref[rows, :] = normed


def move_columns(source, target, blocks):
    wide = source.shape[1] // len(blocks)
    for place, block in enumerate(blocks):
        target[:, place * wide : (place + 1) * wide] = source[:, block * wide : (block + 1) * wide]


def order_kernel(blocks_a, blocks_b, in_ref, a_ref, b_ref):
    move_columns(in_ref, a_ref, blocks_a)
    move_columns(in_ref, b_ref, blocks_b)


def prepare_kernel(meta_ref, o_ref, *refs):
    given = refs[:7]
    part_ref, vec_ref, o_in = refs[7:10]
    lines = refs[10:17]
    sems = refs[17]
    copies = Copies(sems)
    copies.start(o_ref.at[strip(meta_ref[BITS], part_ref.shape[0]), :], o_in)
    for line_ref, vector_ref in zip(lines, given):
        copies.start(vector_ref, line_ref)
    copies.wait()
    part_ref[...] = o_in[...].astype(f32)
    vec_ref[...] = jnp.zeros_like(vec_ref)
    for k, line_ref in enumerate(lines):
        vec_ref[k, :] = line_ref[...].astype(f32)


def prepare(meta, o_weight, vectors):
    rows, width = o_weight.shape
    far = pl.BlockSpec(memory_space=pltpu.HBM)
    return pl.pallas_call(
        prepare_kernel,
        in_specs=[pl.BlockSpec(memory_space=pltpu.SMEM)] + [far] * 8,
        out_specs=[in_vmem] * 2,
        out_shape=[shape(rows // 2, width), shape(8, width)],
        scratch_shapes=[pltpu.VMEM((rows // 2, width), bf16)]
        + [pltpu.VMEM((width,), bf16)] * 7
        + [pltpu.SemaphoreType.DMA((8,))],
        compiler_params=pltpu.CompilerParams(vmem_limit_bytes=60 * 1024 * 1024),
        cost_estimate=pl.CostEstimate(flops=1024, bytes_accessed=1024, transcendentals=0),
        name="prepare",
    )(meta, o_weight, *vectors)


def widen_kernel(a_ref, b_ref, vec_ref, wide_ref):
    rows = a_ref.shape[0]
    step = 64

    @pl.loop(0, rows // step)
    def _(i):
        wide_ref[strip(i, step), :] = a_ref[strip(i, step), :].astype(f32)

    @pl.loop(0, b_ref.shape[0] // step)
    def _(i):
        wide_ref[strip(i + rows // step, step), :] = b_ref[strip(i, step), :].astype(f32)

    wide_ref[rows + b_ref.shape[0] :, :] = vec_ref[...]


def qkv_kernel(meta_ref, all_ref, qw_ref, kw_ref, vw_ref, *refs):
    given = refs[:2]
    vec_ref, local_ref, near_ref, far_ref, k_ref, v_ref, q_in, k_in, v_in, qb_in, vb_in, sems = refs[2:]
    half, wide = near_ref.shape
    rows = half // 2
    copies = Copies(sems)
    copies.start(given[0], qb_in)
    copies.start(given[1], vb_in)
    for p in range(4):
        copies.start(all_ref.at[strip(meta_ref[p], rows), :], local_ref.at[pl.ds(p * rows, rows), :])
    copies.start(kw_ref, k_in)
    copies.start(qw_ref, q_in)
    copies.start(vw_ref, v_in)
    copies.wait()
    k_ref[...] = dot_nn(local_ref[...], k_in[...]).astype(bf16)
    vec_ref[0, :] = qb_in[...].astype(f32)
    vec_ref[1, :] = vb_in[...].astype(f32)
    q = (dot_nn(local_ref[...], q_in[...]) + vec_ref[0:1, :]).astype(bf16)
    near_ref[...] = q[:half]
    far_ref[...] = q[half:]
    v_ref[...] = (dot_nn(local_ref[...], v_in[...]) + vec_ref[1:2, :]).astype(bf16)


def qkv(meta, tokens, weights, biases):
    rows, width = tokens.shape
    wide = weights[0].shape[1]
    far = pl.BlockSpec(memory_space=pltpu.HBM)
    return pl.pallas_call(
        qkv_kernel,
        in_specs=[pl.BlockSpec(memory_space=pltpu.SMEM)] + [far] * 6,
        out_specs=[in_vmem] * 6,
        out_shape=[shape(8, wide), shape(rows, width, bf16)]
        + [shape(rows // 2, wide, bf16)] * 2
        + [shape(rows, wide, bf16)] * 2,
        scratch_shapes=[pltpu.VMEM((width, wide), bf16)] * 3
        + [pltpu.VMEM((wide,), bf16)] * 2
        + [pltpu.SemaphoreType.DMA((9,))],
        compiler_params=pltpu.CompilerParams(vmem_limit_bytes=58 * 1024 * 1024),
        cost_estimate=pl.CostEstimate(flops=1024, bytes_accessed=1024, transcendentals=0),
        name="qkv",
    )(meta, tokens, *weights, *biases)[1:]


def add_kernel(*refs):
    step = 64

    @pl.loop(0, refs[0].shape[0] // step)
    def _(i):
        here = strip(i, step)
        total = refs[0][here, :]
        for ref in refs[1:-1]:
            total = total + ref[here, :]
        refs[-1][here, :] = total


def add(*values):
    return whole(add_kernel, "add", list(values), [shape(*values[0].shape)])[0]


def pair_kernel(side, fill, bit, meta_ref, left_ref, right_ref, *refs):
    mine = meta_ref[BITS + bit]
    half = left_ref.shape[1] // 2
    hidden = right_ref.shape[1] // 2
    right = right_ref[:, side * hidden : (side + 1) * hidden]
    for kept in range(2):
        start = pl.multiple_of((mine if kept else 1 - mine) * half, 128)
        value = dot_tn(left_ref[:, pl.ds(start, half)], right)
        if fill:
            refs[1 + kept][...] = value + refs[0][kept * half : (kept + 1) * half, :]
        else:
            refs[0][kept * half : (kept + 1) * half, :] = value


def fold_kernel(riders, ends, bit, meta_ref, total_ref, got_ref, *refs):
    rows = total_ref.shape[0]
    if riders:
        extra_ref = refs[0]
        refs = refs[1:]
        extra = extra_ref[...] + got_ref[rows:, :]
    if ends:
        refs[0][...] = total_ref[...] + got_ref[:rows, :]
        if riders:
            refs[1][...] = extra
        return
    half = rows // 2
    mine = meta_ref[BITS + bit]
    step = min(64, half)

    @pl.loop(0, half // step)
    def _(i):
        away = strip((1 - mine) * (half // step) + i, step)
        kept = strip(mine * (half // step) + i, step)
        refs[0][strip(i, step), :] = total_ref[away, :] + got_ref[away, :]
        refs[1][strip(i, step), :] = total_ref[kept, :] + got_ref[kept, :]

    if riders:
        refs[0][half:, :] = extra
        refs[2][...] = extra
    elif refs[0].shape[0] > half:
        refs[0][half:, :] = jnp.zeros((refs[0].shape[0] - half, refs[0].shape[1]), f32)


def qk_kernel(bit, meta_ref, left_ref, near_ref, far_ref, gk_ref, away_ref, kept_ref):
    mine = meta_ref[BITS + bit]
    half = left_ref.shape[1] // 2
    rows = near_ref.shape[0]
    wide = near_ref.shape[1]
    for kept, ref in enumerate((away_ref, kept_ref)):
        cols = pl.ds(pl.multiple_of((mine if kept else 1 - mine) * half, 128), half)
        ref[:, :wide] = dot_tn(left_ref[:rows, cols], near_ref[...]) + dot_tn(left_ref[rows:, cols], far_ref[...])
        ref[:, wide:] = dot_tn(left_ref[:, cols], gk_ref[...])


def vo_kernel(bit, meta_ref, left_ref, gv_ref, kept_o_ref, got_a_ref, got_b_ref, near_ref, far_ref, chip_ref, far_sums_ref, ub_ref, sib_ref, away_ref, kept_ref, extra_ref):
    mine = meta_ref[BITS + bit]
    half = left_ref.shape[1] // 2
    wide = gv_ref.shape[1]
    riders = chip_ref.shape[0]
    extra_ref[...] = jnp.zeros_like(extra_ref)
    shared = chip_ref[...] + far_sums_ref[far_sums_ref.shape[0] - riders :, :]
    extra_ref[: riders // 2, :wide] = shared[: riders // 2]
    extra_ref[: riders // 2, wide:] = shared[riders // 2 :]
    row = riders // 2
    ones = (jnp.sum(near_ref[...].astype(f32), axis=0, keepdims=True) + jnp.sum(far_ref[...].astype(f32), axis=0, keepdims=True))
    extra_ref[row : row + 1, :wide] = ones
    extra_ref[row : row + 1, wide:] = jnp.sum(gv_ref[...].astype(f32), axis=0, keepdims=True)
    place = sib_ref.shape[0] - 8
    for k in range(ub_ref.shape[1] // (2 * wide)):
        cols = slice(2 * k * wide, 2 * (k + 1) * wide)
        extra_ref[row + 1 + k : row + 2 + k, :] = ub_ref[:, cols] + sib_ref[place : place + 1, cols]
    for kept, ref in enumerate((away_ref, kept_ref)):
        start = pl.multiple_of((mine if kept else 1 - mine) * half, 128)
        ref[:half, :wide] = dot_tn(left_ref[:, pl.ds(start, half)], gv_ref[...])
        rows = pl.ds(start, half)
        top = jnp.where(start == 0, got_a_ref[...], got_b_ref[...])
        ref[:half, wide:] = kept_o_ref[rows, :] + top
    away_ref[half:, :] = extra_ref[...]


def o_kernel(cols_ref, other_ref, near_ref, first_ref, second_ref, kept_ref):
    half = first_ref.shape[0]
    first_ref[...] = dot_tn(cols_ref[:, :half], other_ref[...])
    second_ref[...] = dot_tn(cols_ref[:, half:], other_ref[...])
    kept_ref[...] = dot_tn(cols_ref[...], near_ref[...])


def round_kernel(wide_ref, a_ref, b_ref, vec_ref):
    rows = a_ref.shape[0]
    step = 64

    @pl.loop(0, rows // step)
    def _(i):
        a_ref[strip(i, step), :] = wide_ref[strip(i, step), :].astype(bf16)

    @pl.loop(0, b_ref.shape[0] // step)
    def _(i):
        b_ref[strip(i, step), :] = wide_ref[strip(i + rows // step, step), :].astype(bf16)

    vec_ref[...] = wide_ref[rows + b_ref.shape[0] :, :]


def feed_kernel(own, unit, blocks, targets, fresh, *refs):
    in_ref, up_ref, up2_ref, vec_ref, vec2_ref, down_ref, down2_ref = refs[:7]
    refs = refs[7 + (0 if fresh else 2) :]
    lo_full, act_full, slope_ref = refs[:3]
    parts = refs[3:-4]
    low_ref, act_ref, cols_ref, sems = refs[-4:]
    hidden = up_ref.shape[1]
    copies = Copies(sems)
    low_ref[...] = in_ref[...].astype(bf16)
    if blocks:
        move_columns(low_ref, cols_ref, blocks)
    else:
        cols_ref[...] = low_ref[...]
    for p, target in enumerate(targets):
        copies.start(cols_ref.at[pl.ds(p * unit, unit), :], lo_full.at[pl.ds(target * unit, unit), :])
    for side, (weight_ref, bias_ref) in enumerate(((up_ref, vec_ref), (up2_ref, vec2_ref))):

        @pl.loop(0, hidden // STRIP)
        def _(i):
            there = strip(i + side * (hidden // STRIP))
            pre = dot_nn(low_ref[...], weight_ref[:, strip(i)]) + bias_ref[UP_BIAS : UP_BIAS + 1, strip(i)]
            normal_cdf = 0.5 * (1.0 + lax.erf(pre * ROOT_HALF))
            density = jnp.exp(-0.5 * pre * pre) * INV_ROOT_TAU
            act_ref[:, there] = (pre * normal_cdf).astype(bf16)
            slope_ref[:, there] = normal_cdf + pre * density

    for p, target in enumerate(targets):
        copies.start(act_ref.at[pl.ds(p * unit, unit), :], act_full.at[pl.ds(target * unit, unit), :])

    @pl.loop(0, down_ref.shape[1] // STRIP)
    def _(i):
        cols = strip(i)
        part = dot_nn(act_ref[:, :hidden], down_ref[:, cols]) + dot_nn(act_ref[:, hidden:], down2_ref[:, cols])
        if own:
            part = part + (in_ref[:, cols] + vec_ref[DOWN_BIAS : DOWN_BIAS + 1, cols])
        for p, part_ref in enumerate(parts):
            part_ref[:, cols] = part[p * unit : (p + 1) * unit]

    copies.wait()


def feed(own, unit, blocks, targets, rows_in, ups, vectors, downs, filled):
    rows, width = rows_in.shape
    hidden = 2 * ups[0].shape[1]
    return whole(
        functools.partial(feed_kernel, own, unit, blocks, targets, not filled),
        "feed",
        [rows_in, *ups, *vectors, *downs],
        [shape(rows, hidden)] + [shape(unit, width)] * len(targets),
        filled=filled or [shape(4 * unit, width, bf16), shape(4 * unit, hidden, bf16)],
        scratch=[
            pltpu.VMEM((rows, width), bf16),
            pltpu.VMEM((rows, hidden), bf16),
            pltpu.VMEM((rows, width), bf16),
        ],
        sems=2 * len(targets),
    )


def back_kernel(own, blocks, offset, target, fresh, block, part, meta_ref, y_ref, og_ref, extra_ref, vec_ref, slope_ref, down_ref, down2_ref, up_ref, up2_ref, *refs):
    refs = refs[0 if fresh else 3 :]
    out_full, gf_full, gp_full, part_ref, ub_ref, mark_ref = refs[:6]
    refs = refs[6:]
    if own:
        two_ref, sums_ref = refs[:2]
        refs = refs[2:]
    gf_ref, out_ref, gp_ref, cols_ref, sems = refs
    rows = y_ref.shape[0]
    hidden = up_ref.shape[1]
    gain = row_of(vec_ref, GAIN_TWO)
    shift = row_of(vec_ref, SHIFT_TWO)
    copies = Copies(sems)
    ids = lax.broadcasted_iota(jnp.int32, (rows, 1), 0)
    number = meta_ref[block]
    base = pl.multiple_of((2 * number + part) * rows, rows)
    limit = meta_ref[LENGTH] - base
    spot = jnp.where(number < meta_ref[COUNT], meta_ref[MARKS + number] - base, -1)
    there = pl.ds(target * rows, rows)
    keep = (ids < limit).astype(f32)
    unit, scale_inv = norm_rows(y_ref[...])
    out_ref[...] = (unit * gain + shift) * keep
    copies.start(out_ref, out_full.at[there, :])
    grad_out = (og_ref[pl.ds(base, rows), :].astype(f32) + jnp.where(ids == spot, extra_ref[pl.ds(number, 1), :], 0.0)) * keep
    grad_two = norm_rows_back(grad_out, unit, scale_inv, gain)
    grad_low = grad_two.astype(bf16)
    gf_ref[...] = grad_low
    if own:
        two_ref[...] = grad_two
        sums_ref[0:1, :] = jnp.sum(grad_low.astype(f32), axis=0, keepdims=True)
        sums_ref[1:2, :] = jnp.sum(grad_out * unit, axis=0, keepdims=True)
        sums_ref[2:3, :] = jnp.sum(grad_out, axis=0, keepdims=True)
        sums_ref[3:8, :] = jnp.zeros((5, sums_ref.shape[1]), f32)
    mark_ref[...] = jnp.zeros_like(mark_ref)

    @pl.when((spot >= 0) & (spot < rows))
    def _():
        row, _ = norm_rows(y_ref[pl.ds(jnp.clip(spot, 0, rows - 1), 1), :])
        mark_ref[0:1, :] = row * gain + shift

    if blocks:
        move_columns(gf_ref, cols_ref, blocks)
    else:
        cols_ref[...] = gf_ref[...]
    copies.start(cols_ref, gf_full.at[there, :])
    for side, weight_ref in enumerate((down_ref, down2_ref)):

        @pl.loop(0, hidden // STRIP)
        def _(i):
            cols = strip(i + side * (hidden // STRIP))
            grad_act = dot_nt(gf_ref[...], weight_ref[strip(i), :])
            grad_pre = (grad_act * slope_ref[pl.ds(offset, rows), cols]).astype(bf16)
            gp_ref[:, cols] = grad_pre
            ub_ref[:, cols] = jnp.sum(grad_pre.astype(f32), axis=0, keepdims=True)

    copies.start(gp_ref, gp_full.at[there, :])

    @pl.loop(0, up_ref.shape[0] // STRIP)
    def _(i):
        cols = strip(i)
        part_ref[:, cols] = dot_nt(gp_ref[:, :hidden], up_ref[cols, :]) + dot_nt(gp_ref[:, hidden:], up2_ref[cols, :])

    copies.wait()


def back(own, blocks, offset, target, block, part, meta, y, out_grad, extra, vectors, slope, downs, ups, filled):
    rows, width = y.shape
    hidden = 2 * ups[0].shape[1]
    outputs = [shape(rows, width), shape(1, hidden), shape(8, width)]
    if own:
        outputs += [shape(rows, width), shape(8, width)]
    return whole(
        functools.partial(back_kernel, own, blocks, offset, target, not filled, block, part),
        "feed_back",
        [y, out_grad, extra, vectors, slope, *downs, *ups],
        outputs,
        scalars=meta,
        filled=filled
        or [shape(4 * rows, width), shape(4 * rows, width, bf16), shape(4 * rows, hidden, bf16)],
        scratch=[
            pltpu.VMEM((rows, width), bf16),
            pltpu.VMEM((rows, width), f32),
            pltpu.VMEM((rows, hidden), bf16),
            pltpu.VMEM((rows, width), bf16),
        ],
        sems=3,
    )


def context_back_kernel(blocks, own_ref, first_ref, sib_ref, near_w_ref, far_w_ref, far_ref, near_ref, sums_ref, *refs):
    low_ref = refs[-1]
    rows = own_ref.shape[0]
    low_ref[:rows, :] = own_ref[...]
    low_ref[rows:, :] = sib_ref[:rows, :].astype(bf16)
    wide = far_ref.shape[1]
    far_ref[: 2 * rows, :] = dot_nt(low_ref[...], far_w_ref[...])
    near_ref[...] = dot_nt(low_ref[...], near_w_ref[...]).astype(bf16)
    for k in range(first_ref.shape[1] // wide):
        cols = slice(k * wide, (k + 1) * wide)
        chip = first_ref[rows : rows + 8, cols] + sib_ref[rows : rows + 8, cols]
        sums_ref[8 * k : 8 * k + 8, :] = chip
        far_ref[2 * rows + 8 * k : 2 * rows + 8 * k + 8, :] = chip
    if blocks:
        move_columns(low_ref, refs[0], blocks)


def first_back_kernel(*refs):
    streams = (refs[:3], refs[3:6])
    chip_ref = refs[6]
    ub_refs = refs[7:11]
    marks = refs[11:15]
    unit_ref, inv_ref, vec_ref, first_ref, low_ref, ub_ref = refs[15:]
    hidden = ub_ref.shape[1]
    ub = ub_refs[0][...] + ub_refs[1][...] + ub_refs[2][...] + ub_refs[3][...]
    ub_ref[...] = ub[:, :hidden]
    gain = row_of(vec_ref, GAIN_ONE)
    size, width = streams[0][0].shape
    rows = 2 * size
    sums = [0.0] * 6
    for half, (two_ref, own_ref, ffn_ref) in enumerate(streams):
        here = pl.ds(half * size, size)
        grad_normed = two_ref[...] + own_ref[...]
        if half:
            grad_normed = grad_normed + chip_ref[...]
        unit = unit_ref[here, :]
        first = norm_rows_back(grad_normed, unit, inv_ref[here, 0:1], gain)
        low = first.astype(bf16)
        first_ref[here, :] = first
        low_ref[here, :] = low
        terms = [low.astype(f32), grad_normed * unit, grad_normed]
        for k in range(3):
            sums[k] = sums[k] + jnp.sum(terms[k], axis=0, keepdims=True)
            sums[k + 3] = sums[k + 3] + ffn_ref[k : k + 1, :]
    for k in range(6):
        first_ref[rows + k : rows + k + 1, :] = sums[k]
    first_ref[rows + 6 : rows + 8, :] = jnp.zeros((2, width), f32)
    first_ref[rows + 8 : rows + 9, :] = ub[:, hidden:]
    first_ref[rows + 9 : rows + 10, :] = marks[0][0:1, :] + marks[1][0:1, :]
    first_ref[rows + 10 : rows + 11, :] = marks[2][0:1, :] + marks[3][0:1, :]
    first_ref[rows + 11 : rows + 16, :] = jnp.zeros((5, width), f32)


def input_kernel(near_ref, far_ref, gk_ref, gv_ref, qw_ref, kw_ref, vw_ref, first_ref, mine_ref, away_ref):
    rows = near_ref.shape[0] // 2
    for p in range(4):
        gq_ref = (near_ref, far_ref)[p // 2]
        here = pl.ds(p * rows, rows)
        value = (
            dot_nt(gq_ref[pl.ds((p % 2) * rows, rows), :], qw_ref[...])
            + dot_nt(gk_ref[here, :], kw_ref[...])
            + dot_nt(gv_ref[here, :], vw_ref[...])
        )
        if p == 0:
            value = value + first_ref[:rows, :]
        (mine_ref, away_ref)[p % 2][pl.ds((p // 2) * rows, rows), :] = value


def chip_kernel(mine_ref, got_ref, keep_ref, send_ref):
    rows = mine_ref.shape[0] // 2
    step = 64

    @pl.loop(0, rows // step)
    def _(i):
        for p in range(2):
            here = strip(i + p * (rows // step), step)
            there = strip(i + (1 - p) * (rows // step), step)
            value = mine_ref[here, :] + got_ref[here, :]
            keep_ref[here, :] = value
            send_ref[there, :] = value


def place_kernel(meta_ref, mine_ref, other_ref, out_ref, sems):
    rows = mine_ref.shape[0] // 2
    copies = Copies(sems)
    for p, block in enumerate((0, 2, 1, 3)):
        ref = (mine_ref, other_ref)[p // 2]
        copies.start(ref.at[pl.ds((p % 2) * rows, rows), :], out_ref.at[strip(meta_ref[block], rows), :])
    copies.wait()


def round_place_kernel(meta_ref, near_ref, far_ref, out_ref, low_ref, sems):
    rows = near_ref.shape[0] // 2
    copies = Copies(sems)
    for p, block in enumerate((0, 2, 1, 3)):
        ref = (near_ref, far_ref)[p // 2]
        low_ref[p * rows : (p + 1) * rows, :] = ref[(p % 2) * rows : (p % 2 + 1) * rows, :].astype(bf16)
        copies.start(low_ref.at[pl.ds(p * rows, rows), :], out_ref.at[strip(meta_ref[block], rows), :])
    copies.wait()


def swap_core(value):
    return lax.ppermute(value, "mp", [(i, i ^ 1) for i in range(4)])


def swap_chip(value):
    return lax.ppermute(value, "mp", [(i, i ^ 2) for i in range(4)])


def gather_rows(own):
    other = swap_chip(own)
    sibling = swap_core(own)
    diagonal = swap_core(other)
    return own, sibling, other, diagonal


def bit_order_blocks(parts, order):
    bits = len(order)
    blocks = []
    for position in range(parts):
        block = 0
        for level, bit in enumerate(order):
            block |= ((position >> (bits - 1 - level)) & 1) << bit
        blocks.append(block)
    return blocks


def bit_order_columns(matrix, parts, order):
    width = matrix.shape[1] // parts
    return jnp.concatenate(
        [matrix[:, b * width : (b + 1) * width] for b in bit_order_blocks(parts, order)], axis=1
    )


def dp_swap(value, parts, bit):
    return lax.ppermute(value, "dp", [(i, i ^ (1 << bit)) for i in range(parts)])


class Sum:
    def __init__(self, parts, order, meta, line, spare=0):
        self.parts, self.order, self.meta, self.line = parts, list(order), meta, line
        self.spare = spare
        self.extra = self.total = self.got = None

    def begin(self, away, total, extra=None):
        self.total, self.extra = total, extra
        self.level = 0
        self.ship(away)

    def ship(self, away):
        self.got = dp_swap(away, self.parts, self.order[self.level])
        self.level += 1

    def step(self):
        if self.got is None:
            return
        got = self.line.hold(self.got)
        self.got = None
        rows, cols = self.total.shape
        ends = self.level == len(self.order)
        riders = 0 if self.extra is None else self.extra.shape[0]
        bit = 0 if ends else self.order[self.level]
        rest = [shape(riders, cols)] if riders else []
        outputs = [shape(rows, cols)]
        if not ends:
            outputs = [shape(rows // 2 + riders + self.spare, cols), shape(rows // 2, cols)]
        given = [self.total, got] + ([self.extra] if riders else [])
        result = whole(
            functools.partial(fold_kernel, riders, ends, bit), "fold", given, outputs + rest, scalars=self.meta
        )
        if riders:
            self.extra = result[-1]
        if ends:
            self.total = result[0]
            self.line.mark(self.total)
        else:
            self.total = result[1]
            self.ship(result[0])
            self.line.mark(result[0])

    def finish(self):
        while self.got is not None:
            self.step()
        return self.total


class Line:
    def __init__(self):
        self.token = None

    def mark(self, *values):
        self.token = values

    def hold(self, *values):
        if self.token is not None:
            values = lax.optimization_barrier(tuple(values) + self.token)[: len(values)]
        return values if len(values) > 1 else values[0]


def shards(
    dp_size,
    tokens,
    doc_lengths,
    cls_pos,
    cls_count,
    q_weight,
    q_bias,
    k_weight,
    v_weight,
    v_bias,
    o_weight,
    o_bias,
    ln1_gain,
    ln1_bias,
    up_weight,
    up_bias,
    down_weight,
    down_bias,
    ln2_gain,
    ln2_bias,
    out_grad,
    pooled_grad,
):
    slot_len, width = tokens.shape
    rows = slot_len // 4
    half = 2 * rows
    head_width = q_weight.shape[1]
    rank = lax.axis_index("mp")
    place_id = lax.axis_index("dp")
    bits = dp_size.bit_length() - 1
    order_a = list(range(bits))
    order_b = [1, 0] + list(range(2, bits)) if bits > 1 else order_a
    length = doc_lengths[0]
    blocks = [rank ^ j for j in range(4)]

    line = Line()
    sizes = width // dp_size
    fixed_a = bit_order_blocks(dp_size, order_a) if sizes % 128 == 0 else None
    fixed_b = bit_order_blocks(dp_size, order_b) if sizes % 128 == 0 else None
    unit = rows // 2

    row_ids = lax.iota(jnp.int32, rows)
    positions = jnp.concatenate([row_ids + blocks[j] * rows for j in range(4)])
    bias = jnp.where(positions < length, 0.0, MASKED).astype(f32)[None, :]
    meta = jnp.concatenate(
        [
            jnp.stack(blocks).astype(jnp.int32),
            doc_lengths,
            cls_count,
            cls_pos[0],
            jnp.stack([(place_id >> bit) & 1 for bit in range(max(bits, 1))]).astype(jnp.int32),
        ]
    )
    hidden = up_bias.shape[0]

    meta, bias = lax.optimization_barrier((meta, bias))

    o_part, vectors = prepare(
        meta, o_weight, [o_bias, ln1_gain, ln1_bias, ln2_gain, ln2_bias, down_bias, up_bias]
    )
    o_got = swap_chip(o_part)
    line.mark(o_part)
    local, queries_near, queries_far, key_rows, value_rows = qkv(
        meta, line.hold(tokens), (q_weight, k_weight, v_weight), (q_bias, v_bias)
    )
    away_context, lse_far = attn_fwd(queries_far, key_rows, value_rows, bias, 256, f32)
    arrived = swap_chip(away_context)
    line.mark(away_context)
    o_got = line.hold(o_got)
    o_other = dp_swap(o_got, dp_size, 0)
    line.mark(o_got)
    up_held, down_held = line.hold(up_weight, down_weight)
    wide = whole(
        widen_kernel,
        "widen",
        [up_held, down_held, vectors],
        [shape(width + hidden + 8, width)],
        limit=20,
    )[0]
    line.mark(wide)
    wide = swap_core(wide)
    context_near, lse_near = attn_fwd(line.hold(queries_near), key_rows, value_rows, bias, 256, bf16)
    line.mark(context_near)
    if fixed_a:
        local_a, local_b = whole(
            functools.partial(order_kernel, fixed_a, fixed_b),
            "order",
            [line.hold(local)],
            [shape(slot_len, width, bf16)] * 2,
        )
    else:
        local_a = bit_order_columns(local, dp_size, order_a)
        local_b = bit_order_columns(local, dp_size, order_b)
    line.mark(local_a)
    own, sib, context_other, o_far = whole(
        project_kernel,
        "project",
        [context_near, line.hold(arrived), o_weight, o_got, line.hold(o_other)],
        [shape(rows, width), shape(rows, width), shape(half, head_width, bf16), shape(head_width, width, bf16)],
        scalars=meta,
    )
    n_a, n_b, normed, unit_one, inv_one = whole(
        first_norm_kernel,
        "first_norm",
        [own, swap_core(sib), local, vectors],
        [shape(unit, width), shape(unit, width), shape(rows, width), shape(rows, width), shape(rows, 128)],
    )
    line.mark(n_a)
    chip_a = swap_chip(n_a)
    chip_b = swap_chip(n_b)
    up_far, down_far, vectors_far = whole(
        round_kernel,
        "round",
        [line.hold(wide)],
        [shape(width, hidden, bf16), shape(hidden, width, bf16), shape(8, width)],
        limit=20,
    )
    ups = (up_weight, up_far)
    downs = (down_weight, down_far)
    both = (vectors, vectors_far)
    lo, act, slope_near, own_a, own_b = feed(True, unit, fixed_b, (0, 1), normed, ups, both, downs, ())
    line.mark(own_a)
    lo, act, slope_a, part = feed(
        False, unit, fixed_b, (2,), line.hold(chip_a), ups, both, downs, (lo, act)
    )
    got_a = swap_chip(part)
    line.mark(part)
    lo, act, slope_b, part = feed(
        False, unit, fixed_b, (3,), line.hold(chip_b), ups, both, downs, (lo, act)
    )
    got_b = swap_chip(part)
    line.mark(part)

    def back_rows(own, k, y, slope, offset, filled):
        place = k if own else 2 + k
        return back(
            own, fixed_a, offset, place, 0 if own else 2, k, meta, y, out_grad, pooled_grad[0], vectors,
            slope, downs, ups, filled,
        )

    y_a = add(own_a, line.hold(got_a))
    chip_a = swap_chip(y_a)
    *filled, back_a, ub_a, mark_a, two_a, sums_a = back_rows(True, 0, y_a, slope_near, 0, ())
    line.mark(back_a)
    y_b = add(own_b, line.hold(got_b))
    chip_b = swap_chip(y_b)
    *filled, back_b, ub_b, mark_b, two_b, sums_b = back_rows(True, 1, y_b, slope_near, unit, filled)
    line.mark(back_b)
    *filled, part, ub_c, mark_c = back_rows(False, 0, line.hold(chip_a), slope_a, 0, filled)
    got_a = swap_chip(part)
    line.mark(part)
    *filled, part, ub_d, mark_d = back_rows(False, 1, line.hold(chip_b), slope_b, 0, filled)
    got_b = swap_chip(part)
    line.mark(part)
    back_a = add(back_a, line.hold(got_a))
    line.mark(back_a)
    out_wide, grad_fed, grad_pre = filled

    def in_order(value, fixed, order):
        return value if fixed else bit_order_columns(value, dp_size, order)

    gf_cols, lo_cols = in_order(grad_fed, fixed_a, order_a), in_order(lo, fixed_b, order_b)
    down_sum = Sum(dp_size, order_a, meta, line, 16)
    up_sum = Sum(dp_size, order_b, meta, line, 16)

    def pair(side, sum_of, left, right, given=()):
        half_rows = width // 2
        return whole(
            functools.partial(pair_kernel, side, bool(given), sum_of.order[0]),
            "pair",
            [left, right, *given],
            [shape(half_rows, hidden)] * 2 if given else [shape(width, hidden)],
            scalars=meta,
        )

    down_other = pair(1, down_sum, line.hold(gf_cols), act)[0]
    down_given = swap_core(down_other)
    line.mark(down_other)
    up_other = pair(1, up_sum, lo_cols, line.hold(grad_pre))[0]
    up_given = swap_core(up_other)
    line.mark(up_other)

    down_sum.begin(*pair(0, down_sum, gf_cols, act, [line.hold(down_given)]))
    up_sum.begin(*pair(0, up_sum, lo_cols, grad_pre, [line.hold(up_given)]))

    line.mark(down_sum.total, up_sum.total)
    got_b = line.hold(got_b)
    first_ext, grad_attended_own, up_bias_own = whole(
        first_back_kernel,
        "first_norm_back",
        [two_a, back_a, sums_a, two_b, back_b, sums_b, got_b, ub_a, ub_b, ub_c, ub_d]
        + [mark_a, mark_b, mark_c, mark_d, unit_one, inv_one, vectors],
        [shape(rows + 16, width), shape(rows, width, bf16), shape(1, hidden)],
    )
    sib_ext = swap_core(first_ext)
    riders = 8 * width // head_width
    context_far_grad, grad_context_near, chip_sums, *ga_cols = whole(
        functools.partial(context_back_kernel, fixed_b),
        "context_back",
        [grad_attended_own, first_ext, sib_ext, o_weight, o_far],
        [shape(half + riders, head_width), shape(half, head_width, bf16), shape(riders, head_width)]
        + [shape(half, width, bf16)] * (2 if fixed_b else 1),
    )
    ga_cols = in_order(ga_cols[0], fixed_b, order_b)
    grad_context_far = swap_chip(context_far_grad)
    line.mark(context_far_grad)
    *o_away, o_kept = whole(
        o_kernel,
        "o_grad",
        [line.hold(ga_cols), context_other, context_near],
        [shape(width // 2, head_width)] * 2 + [shape(width, head_width)],
    )
    o_got = [swap_chip(v) for v in o_away]
    line.mark(o_kept)

    queries_near = line.hold(queries_near)
    grad_q_near, key_sum, value_sum = attn_bwd(
        queries_near, grad_context_near, key_rows, value_rows, bias, lse_near, 256
    )
    line.mark(grad_q_near)
    grad_context_far = line.hold(grad_context_far)
    line.mark(grad_context_far)
    queries_far = line.hold(queries_far)
    grad_q_far, grad_k, grad_v = attn_bwd(
        queries_far, grad_context_far, key_rows, value_rows, bias, lse_far, 256, (key_sum, value_sum)
    )
    line.mark(grad_k)

    qk_sum = Sum(dp_size, order_a, meta, line)
    vo_sum = Sum(dp_size, order_b, meta, line)
    qk_away, qk_kept = whole(
        functools.partial(qk_kernel, qk_sum.order[0]),
        "qk_grad",
        [local_a, line.hold(grad_q_near), grad_q_far, grad_k],
        [shape(width // 2, 2 * head_width)] * 2,
        scalars=meta,
    )
    line.mark(qk_away)
    riders = 8 * width // head_width
    extra_rows = -(-(riders // 2 + 1 + hidden // (2 * head_width)) // 8) * 8
    o_got = line.hold(*o_got)
    line.mark(*o_got)
    in_mine, in_away = whole(
        input_kernel,
        "input_grad",
        [line.hold(grad_q_near), grad_q_far, grad_k, grad_v, q_weight, k_weight, v_weight, first_ext],
        [shape(half, width)] * 2,
    )
    in_got = swap_core(in_away)
    line.mark(in_mine)
    down_sum.step()
    up_sum.step()
    qk_sum.begin(qk_away, qk_kept)
    in_kept, in_sent = whole(
        chip_kernel, "chip_sum", [in_mine, line.hold(in_got)], [shape(half, width)] * 2
    )
    in_got = swap_chip(in_sent)
    line.mark(in_sent)
    vo_away, vo_kept, vo_extra = whole(
        functools.partial(vo_kernel, vo_sum.order[0]),
        "vo_grad",
        [local_b, line.hold(grad_v), o_kept, *o_got, grad_q_near, grad_q_far, chip_sums, grad_context_far]
        + [up_bias_own, sib_ext],
        [
            shape(width // 2 + extra_rows, 2 * head_width),
            shape(width // 2, 2 * head_width),
            shape(extra_rows, 2 * head_width),
        ],
        scalars=meta,
    )
    vo_sum.begin(vo_away, vo_kept, vo_extra)
    line.mark(vo_away)
    for bit in range(bits):
        down_sum.step()
        up_sum.step()
        qk_sum.step()
        vo_sum.step()
        if bit == min(1, bits - 1):
            in_final = add(in_kept, line.hold(in_got))
            in_other = swap_core(in_final)
            out_far = swap_core(line.hold(out_wide))
            line.mark(in_final)
            in_grad = whole(
                place_kernel,
                "place",
                [in_final, line.hold(in_other)],
                [],
                scalars=meta,
                filled=[shape(slot_len, width)],
                sems=4,
                far=True,
            )[0]
            line.mark(in_grad)
            out = whole(
                round_place_kernel,
                "round_place",
                [out_wide, line.hold(out_far)],
                [],
                scalars=meta,
                filled=[shape(slot_len, width, bf16)],
                scratch=[pltpu.VMEM((slot_len, width), bf16)],
                sems=4,
                far=True,
            )[0]
            line.mark(out)
    qk_sum, vo_total = qk_sum.finish(), vo_sum.finish()
    riding = vo_sum.extra
    row = riders // 2
    shared = jnp.concatenate([riding[:row, :head_width], riding[:row, head_width:]], axis=0)
    shared = shared.reshape(-1, 8, head_width).transpose(1, 0, 2).reshape(8, width)
    biases = riding[row].reshape(2, head_width)
    up_bias_sum = riding[row + 1 : row + 1 + hidden // (2 * head_width)].reshape(-1)
    v_sum = vo_total[:, :head_width]
    o_sum = vo_total[:, head_width:].T
    down_sum = down_sum.finish().T
    up_sum = up_sum.finish()

    mine = first_ext[rows + 9 : rows + 11]
    theirs = sib_ext[rows + 9 : rows + 11]
    marks = jnp.concatenate([mine[:1], theirs[:1], mine[1:], theirs[1:]], axis=0)
    pooled = jnp.concatenate(
        [lax.dynamic_index_in_dim(marks, blocks[j], keepdims=True) for j in range(4)], axis=0
    )[None]
    return (
        out,
        pooled,
        in_grad,
        qk_sum[:, :head_width],
        biases[0],
        qk_sum[:, head_width:],
        v_sum,
        biases[1],
        o_sum,
        shared[0],
        shared[1],
        shared[2],
        up_sum,
        up_bias_sum,
        down_sum,
        shared[3],
        shared[4],
        shared[5],
    )


def solution(mesh):
    return jax.shard_map(
        functools.partial(shards, mesh.shape["dp"]),
        mesh=mesh,
        in_specs=(
            P("dp", None),
            P("dp"),
            P("dp", None),
            P("dp"),
            P(None, "mp"),
            P("mp"),
            P(None, "mp"),
            P(None, "mp"),
            P("mp"),
            P("mp", None),
            P(),
            P(),
            P(),
            P(None, "mp"),
            P("mp"),
            P("mp", None),
            P(),
            P(),
            P(),
            P("dp", None),
            P("dp", None, None),
        ),
        out_specs=(
            P("dp", None),
            P("dp", None, None),
            P("dp", None),
            P("dp", "mp"),
            P("mp"),
            P("dp", "mp"),
            P("dp", "mp"),
            P("mp"),
            P("mp", "dp"),
            P(),
            P(),
            P(),
            P("dp", "mp"),
            P("mp"),
            P("mp", "dp"),
            P(),
            P(),
            P(),
        ),
        check_vma=False,
    )
```

```python
import functools

import jax
import jax.numpy as jnp
from jax import lax
from jax.experimental import pallas as pl
from jax.experimental.pallas import tpu as pltpu
from jax.sharding import PartitionSpec as P

HEAD_DIM = 64
NORM_EPS = 1e-05
ROOT_HALF = 0.7071067811865476
INV_ROOT_TAU = 0.3989422804014327
LOG2E = 1.4426950408889634
SCORE_SCALE = 0.125 * LOG2E
MASKED = -1e30

f32 = jnp.float32
bf16 = jnp.bfloat16
VMEM_LIMIT = 20 * 1024 * 1024


def dot_nn(a, b):
    return lax.dot_general(a, b, (((1,), (0,)), ((), ())), preferred_element_type=f32)


def dot_nt(a, b):
    return lax.dot_general(a, b, (((1,), (1,)), ((), ())), preferred_element_type=f32)


def dot_tn(a, b):
    return lax.dot_general(a, b, (((0,), (0,)), ((), ())), preferred_element_type=f32)


def attn_fwd_kernel(q_ref, k_ref, v_ref, bias_ref, o_ref, lse_ref):
    rows, width = q_ref.shape
    heads = width // HEAD_DIM
    lane = lax.broadcasted_iota(jnp.int32, (1, width), 1) // HEAD_DIM
    lse_lane = lax.broadcasted_iota(jnp.int32, (1, 128), 1)
    q = q_ref[...]
    k = k_ref[...]
    v = v_ref[...]
    bias = bias_ref[...]
    out = jnp.zeros((rows, width), f32)
    lse = jnp.zeros((rows, 128), f32)
    for h in range(heads):
        qh = jnp.where(lane == h, q, jnp.zeros_like(q))
        s = dot_nt(qh, k) * SCORE_SCALE + bias
        top = jnp.max(s, axis=1, keepdims=True)
        e = jnp.exp2(s - top)
        total = jnp.sum(e, axis=1, keepdims=True)
        p = (e * (1.0 / total)).astype(bf16)
        c = dot_nn(p, v)
        out = jnp.where(lane == h, c, out)
        lse = jnp.where(lse_lane == h, top + jnp.log2(total), lse)
    o_ref[...] = out.astype(o_ref.dtype)
    lse_ref[...] = lse


def attn_fwd(q, k, v, bias, block, dtype):
    rows, width = q.shape
    keys = k.shape[0]
    full = pl.BlockSpec((keys, width), lambda i: (0, 0))
    return pl.pallas_call(
        attn_fwd_kernel,
        grid=(rows // block,),
        in_specs=[
            pl.BlockSpec((block, width), lambda i: (i, 0)),
            full,
            full,
            pl.BlockSpec((1, keys), lambda i: (0, 0)),
        ],
        out_specs=[
            pl.BlockSpec((block, width), lambda i: (i, 0)),
            pl.BlockSpec((block, 128), lambda i: (i, 0)),
        ],
        out_shape=[
            jax.ShapeDtypeStruct((rows, width), dtype),
            jax.ShapeDtypeStruct((rows, 128), f32),
        ],
        compiler_params=pltpu.CompilerParams(vmem_limit_bytes=VMEM_LIMIT),
        cost_estimate=pl.CostEstimate(flops=1024, bytes_accessed=1024, transcendentals=0),
        name="attn_fwd",
    )(q, k, v, bias)


def attn_bwd_kernel(carried, *refs):
    q_ref, g_ref, k_ref, v_ref, bias_ref, lse_ref = refs[:6]
    refs = refs[6:]
    if carried:
        gk_in, gv_in = refs[:2]
        refs = refs[2:]
    gq_ref, gk_ref, gv_ref, gk_acc, gv_acc, gq_acc = refs
    step = pl.program_id(0)
    width = q_ref.shape[1]
    lane = lax.broadcasted_iota(jnp.int32, (1, width), 1) // HEAD_DIM
    lse_lane = lax.broadcasted_iota(jnp.int32, (1, 128), 1)

    @pl.when(step == 0)
    def _():
        gk_acc[...] = gk_in[...] if carried else jnp.zeros_like(gk_acc)
        gv_acc[...] = gv_in[...] if carried else jnp.zeros_like(gv_acc)

    @pl.loop(0, width // HEAD_DIM)
    def _(h):
        mine = lane == h
        zero = jnp.zeros(q_ref.shape, bf16)
        qh = jnp.where(mine, q_ref[...], zero)
        gh = jnp.where(mine, g_ref[...].astype(bf16), zero)
        lse = jnp.sum(jnp.where(lse_lane == h, lse_ref[...], 0.0), axis=1, keepdims=True)
        s = dot_nt(qh, k_ref[...]) * SCORE_SCALE + bias_ref[...]
        p = jnp.exp2(s - lse)
        dp = dot_nt(gh, v_ref[...])
        inner = jnp.sum(p * dp, axis=1, keepdims=True)
        ds = (p * (dp - inner)).astype(bf16)
        gq_acc[...] = jnp.where(mine, dot_nn(ds, k_ref[...]), gq_acc[...])
        gk_acc[...] += dot_tn(ds, qh)
        gv_acc[...] += dot_tn(p.astype(bf16), gh)

    gq_ref[...] = (gq_acc[...] * 0.125).astype(bf16)

    @pl.when(step == pl.num_programs(0) - 1)
    def _():
        scale = 0.125 if carried else 1.0
        gk_ref[...] = (gk_acc[...] * scale).astype(gk_ref.dtype)
        gv_ref[...] = gv_acc[...].astype(gv_ref.dtype)


def attn_bwd(q, g, k, v, bias, lse, block, sums=()):
    rows, width = q.shape
    keys = k.shape[0]
    full = pl.BlockSpec((keys, width), lambda i: (0, 0))
    part = pl.BlockSpec((block, width), lambda i: (i, 0))
    sum_type = bf16 if sums else f32
    return pl.pallas_call(
        functools.partial(attn_bwd_kernel, bool(sums)),
        grid=(rows // block,),
        in_specs=[
            part,
            part,
            full,
            full,
            pl.BlockSpec((1, keys), lambda i: (0, 0)),
            pl.BlockSpec((block, 128), lambda i: (i, 0)),
        ]
        + [full] * len(sums),
        out_specs=[part, full, full],
        out_shape=[
            jax.ShapeDtypeStruct((rows, width), bf16),
            jax.ShapeDtypeStruct((keys, width), sum_type),
            jax.ShapeDtypeStruct((keys, width), sum_type),
        ],
        scratch_shapes=[pltpu.VMEM((keys, width), f32)] * 2 + [pltpu.VMEM((block, width), f32)],
        compiler_params=pltpu.CompilerParams(vmem_limit_bytes=VMEM_LIMIT),
        cost_estimate=pl.CostEstimate(flops=1024, bytes_accessed=1024, transcendentals=0),
        name="attn_bwd",
    )(q, g, k, v, bias, lse, *sums)


in_vmem = pl.BlockSpec(memory_space=pltpu.VMEM)
STRIP = 256
LENGTH, COUNT, MARKS, BITS = 4, 5, 6, 10
O_BIAS, GAIN_ONE, SHIFT_ONE, GAIN_TWO, SHIFT_TWO, DOWN_BIAS, UP_BIAS, QV_BIAS = range(8)


def row_of(ref, index):
    return ref[index : index + 1, :]


def strip(index, size=STRIP):
    return pl.ds(pl.multiple_of(index * size, size), size)


def shape(rows, cols, dtype=f32):
    return jax.ShapeDtypeStruct((rows, cols), dtype)


def whole(kernel, name, inputs, outputs, scalars=None, filled=(), sems=0, scratch=(), limit=8, far=False):
    lead = [] if scalars is None else [scalars]
    anywhere = pl.BlockSpec(memory_space=pl.ANY)
    given = [v for v in filled if not isinstance(v, jax.ShapeDtypeStruct)]
    begun = [jax.ShapeDtypeStruct(v.shape, v.dtype) for v in filled]
    first = len(lead) + len(inputs)
    return pl.pallas_call(
        kernel,
        in_specs=[pl.BlockSpec(memory_space=pltpu.SMEM)] * len(lead)
        + [in_vmem] * len(inputs)
        + [anywhere] * len(given),
        out_specs=[pl.BlockSpec(memory_space=pltpu.HBM) if far else anywhere] * len(begun)
        + [in_vmem] * len(outputs),
        out_shape=begun + list(outputs),
        scratch_shapes=list(scratch) + ([pltpu.SemaphoreType.DMA((sems,))] if sems else []),
        input_output_aliases={first + p: p for p in range(len(given))},
        compiler_params=pltpu.CompilerParams(vmem_limit_bytes=limit * 1024 * 1024),
        cost_estimate=pl.CostEstimate(flops=1024, bytes_accessed=1024, transcendentals=0),
        name=name,
    )(*lead, *inputs, *given)


class Copies:
    def __init__(self, sems):
        self.sems, self.made = sems, []

    def start(self, source, target):
        copy = pltpu.make_async_copy(source, target, self.sems.at[len(self.made)])
        copy.start()
        self.made.append(copy)

    def wait(self):
        for copy in self.made:
            copy.wait()


def project_kernel(meta_ref, near_ref, other_ref, o_near_ref, o_got_ref, o_other_ref, own_ref, sib_ref, low_ref, o_far_ref):
    rows = own_ref.shape[0]
    part = o_got_ref.shape[0]
    first = meta_ref[BITS] == 0
    o_far_ref[:part, :] = jnp.where(first, o_got_ref[...], o_other_ref[...]).astype(bf16)
    o_far_ref[part:, :] = jnp.where(first, o_other_ref[...], o_got_ref[...]).astype(bf16)
    low_ref[...] = other_ref[...].astype(bf16)
    both = dot_nn(near_ref[...], o_near_ref[...]) + dot_nn(low_ref[...], o_far_ref[...])
    own_ref[...] = both[:rows]
    sib_ref[...] = both[rows:]


def mean_of(values):
    return jnp.sum(values, axis=-1, keepdims=True) * (1.0 / values.shape[-1])


def norm_rows(values):
    centre = values - mean_of(values)
    scale_inv = lax.rsqrt(mean_of(centre * centre) + NORM_EPS)
    return centre * scale_inv, scale_inv


def norm_rows_back(grad_rows, unit_rows, scale_inv, gain):
    scaled = grad_rows * gain
    return scale_inv * (scaled - mean_of(scaled) - unit_rows * mean_of(scaled * unit_rows))


def first_norm_kernel(own_ref, near_ref, tok_ref, vec_ref, na_ref, nb_ref, all_ref, unit_ref, inv_ref):
    gain = row_of(vec_ref, GAIN_ONE)
    shift = row_of(vec_ref, SHIFT_ONE)
    for half, out_ref in enumerate((na_ref, nb_ref)):
        size = out_ref.shape[0]
        rows = pl.ds(half * size, size)
        values = tok_ref[rows, :].astype(f32) + (own_ref[rows, :] + near_ref[rows, :] + row_of(vec_ref, O_BIAS))
        unit, scale_inv = norm_rows(values)
        unit_ref[rows, :] = unit
        inv_ref[rows, :] = jnp.broadcast_to(scale_inv, (size, inv_ref.shape[1]))
        normed = unit * gain + shift
        out_ref[...] = normed
        all_ref[rows, :] = normed


def move_columns(source, target, blocks):
    wide = source.shape[1] // len(blocks)
    for place, block in enumerate(blocks):
        target[:, place * wide : (place + 1) * wide] = source[:, block * wide : (block + 1) * wide]


def order_kernel(blocks_a, blocks_b, in_ref, a_ref, b_ref):
    move_columns(in_ref, a_ref, blocks_a)
    move_columns(in_ref, b_ref, blocks_b)


def prepare_kernel(meta_ref, o_ref, *refs):
    given = refs[:7]
    part_ref, vec_ref, o_in = refs[7:10]
    lines = refs[10:17]
    sems = refs[17]
    copies = Copies(sems)
    copies.start(o_ref.at[strip(meta_ref[BITS], part_ref.shape[0]), :], o_in)
    for line_ref, vector_ref in zip(lines, given):
        copies.start(vector_ref, line_ref)
    copies.wait()
    part_ref[...] = o_in[...].astype(f32)
    vec_ref[...] = jnp.zeros_like(vec_ref)
    for k, line_ref in enumerate(lines):
        vec_ref[k, :] = line_ref[...].astype(f32)


def prepare(meta, o_weight, vectors):
    rows, width = o_weight.shape
    far = pl.BlockSpec(memory_space=pltpu.HBM)
    return pl.pallas_call(
        prepare_kernel,
        in_specs=[pl.BlockSpec(memory_space=pltpu.SMEM)] + [far] * 8,
        out_specs=[in_vmem] * 2,
        out_shape=[shape(rows // 2, width), shape(8, width)],
        scratch_shapes=[pltpu.VMEM((rows // 2, width), bf16)]
        + [pltpu.VMEM((width,), bf16)] * 7
        + [pltpu.SemaphoreType.DMA((8,))],
        compiler_params=pltpu.CompilerParams(vmem_limit_bytes=60 * 1024 * 1024),
        cost_estimate=pl.CostEstimate(flops=1024, bytes_accessed=1024, transcendentals=0),
        name="prepare",
    )(meta, o_weight, *vectors)


def widen_kernel(a_ref, b_ref, vec_ref, wide_ref):
    rows = a_ref.shape[0]
    step = 64

    @pl.loop(0, rows // step)
    def _(i):
        wide_ref[strip(i, step), :] = a_ref[strip(i, step), :].astype(f32)

    @pl.loop(0, b_ref.shape[0] // step)
    def _(i):
        wide_ref[strip(i + rows // step, step), :] = b_ref[strip(i, step), :].astype(f32)

    wide_ref[rows + b_ref.shape[0] :, :] = vec_ref[...]


def qkv_kernel(meta_ref, all_ref, qw_ref, kw_ref, vw_ref, *refs):
    given = refs[:2]
    vec_ref, local_ref, near_ref, far_ref, k_ref, v_ref, q_in, k_in, v_in, qb_in, vb_in, sems = refs[2:]
    half, wide = near_ref.shape
    rows = half // 2
    copies = Copies(sems)
    copies.start(given[0], qb_in)
    copies.start(given[1], vb_in)
    for p in range(4):
        copies.start(all_ref.at[strip(meta_ref[p], rows), :], local_ref.at[pl.ds(p * rows, rows), :])
    copies.start(kw_ref, k_in)
    copies.start(qw_ref, q_in)
    copies.start(vw_ref, v_in)
    copies.wait()
    k_ref[...] = dot_nn(local_ref[...], k_in[...]).astype(bf16)
    vec_ref[0, :] = qb_in[...].astype(f32)
    vec_ref[1, :] = vb_in[...].astype(f32)
    q = (dot_nn(local_ref[...], q_in[...]) + vec_ref[0:1, :]).astype(bf16)
    near_ref[...] = q[:half]
    far_ref[...] = q[half:]
    v_ref[...] = (dot_nn(local_ref[...], v_in[...]) + vec_ref[1:2, :]).astype(bf16)


def qkv(meta, tokens, weights, biases):
    rows, width = tokens.shape
    wide = weights[0].shape[1]
    far = pl.BlockSpec(memory_space=pltpu.HBM)
    return pl.pallas_call(
        qkv_kernel,
        in_specs=[pl.BlockSpec(memory_space=pltpu.SMEM)] + [far] * 6,
        out_specs=[in_vmem] * 6,
        out_shape=[shape(8, wide), shape(rows, width, bf16)]
        + [shape(rows // 2, wide, bf16)] * 2
        + [shape(rows, wide, bf16)] * 2,
        scratch_shapes=[pltpu.VMEM((width, wide), bf16)] * 3
        + [pltpu.VMEM((wide,), bf16)] * 2
        + [pltpu.SemaphoreType.DMA((9,))],
        compiler_params=pltpu.CompilerParams(vmem_limit_bytes=58 * 1024 * 1024),
        cost_estimate=pl.CostEstimate(flops=1024, bytes_accessed=1024, transcendentals=0),
        name="qkv",
    )(meta, tokens, *weights, *biases)[1:]


def add_kernel(*refs):
    step = 64

    @pl.loop(0, refs[0].shape[0] // step)
    def _(i):
        here = strip(i, step)
        total = refs[0][here, :]
        for ref in refs[1:-1]:
            total = total + ref[here, :]
        refs[-1][here, :] = total


def add(*values):
    return whole(add_kernel, "add", list(values), [shape(*values[0].shape)])[0]


def pair_kernel(side, fill, bit, meta_ref, left_ref, right_ref, *refs):
    mine = meta_ref[BITS + bit]
    half = left_ref.shape[1] // 2
    hidden = right_ref.shape[1] // 2
    right = right_ref[:, side * hidden : (side + 1) * hidden]
    for kept in range(2):
        start = pl.multiple_of((mine if kept else 1 - mine) * half, 128)
        value = dot_tn(left_ref[:, pl.ds(start, half)], right)
        if fill:
            refs[1 + kept][...] = value + refs[0][kept * half : (kept + 1) * half, :]
        else:
            refs[0][kept * half : (kept + 1) * half, :] = value


def fold_kernel(riders, ends, bit, meta_ref, total_ref, got_ref, *refs):
    rows = total_ref.shape[0]
    if riders:
        extra_ref = refs[0]
        refs = refs[1:]
        extra = extra_ref[...] + got_ref[rows:, :]
    if ends and len(refs) == 2 and not riders:
        wide = total_ref.shape[1] // 2
        refs[0][...] = total_ref[:, :wide] + got_ref[:rows, :wide]
        refs[1][...] = (total_ref[:, wide:] + got_ref[:rows, wide:]).T
        return
    if ends:
        refs[0][...] = total_ref[...] + got_ref[:rows, :]
        if riders:
            refs[1][...] = extra
        return
    half = rows // 2
    mine = meta_ref[BITS + bit]
    step = min(64, half)

    @pl.loop(0, half // step)
    def _(i):
        away = strip((1 - mine) * (half // step) + i, step)
        kept = strip(mine * (half // step) + i, step)
        refs[0][strip(i, step), :] = total_ref[away, :] + got_ref[away, :]
        refs[1][strip(i, step), :] = total_ref[kept, :] + got_ref[kept, :]

    if riders:
        refs[0][half:, :] = extra
        refs[2][...] = extra
    elif refs[0].shape[0] > half:
        refs[0][half:, :] = jnp.zeros((refs[0].shape[0] - half, refs[0].shape[1]), f32)


def qk_kernel(bit, meta_ref, left_ref, near_ref, far_ref, gk_ref, gv_ref, chip_ref, far_sums_ref, ub_ref, sib_ref, away_ref, kept_ref, extra_ref):
    mine = meta_ref[BITS + bit]
    half = left_ref.shape[1] // 2
    rows = near_ref.shape[0]
    wide = near_ref.shape[1]
    riders = chip_ref.shape[0]
    extra_ref[...] = jnp.zeros_like(extra_ref)
    shared = chip_ref[...] + far_sums_ref[far_sums_ref.shape[0] - riders :, :]
    extra_ref[: riders // 2, :wide] = shared[: riders // 2]
    extra_ref[: riders // 2, wide:] = shared[riders // 2 :]
    row = riders // 2
    query_sum = jnp.sum(near_ref[...].astype(f32), axis=0, keepdims=True)
    extra_ref[row : row + 1, :wide] = query_sum + jnp.sum(far_ref[...].astype(f32), axis=0, keepdims=True)
    extra_ref[row : row + 1, wide:] = jnp.sum(gv_ref[...].astype(f32), axis=0, keepdims=True)
    place = sib_ref.shape[0] - 8
    for k in range(ub_ref.shape[1] // (2 * wide)):
        cols = slice(2 * k * wide, 2 * (k + 1) * wide)
        extra_ref[row + 1 + k : row + 2 + k, :] = ub_ref[:, cols] + sib_ref[place : place + 1, cols]
    for kept, ref in enumerate((away_ref, kept_ref)):
        cols = pl.ds(pl.multiple_of((mine if kept else 1 - mine) * half, 128), half)
        ref[:half, :wide] = dot_tn(left_ref[:rows, cols], near_ref[...]) + dot_tn(left_ref[rows:, cols], far_ref[...])
        ref[:half, wide:] = dot_tn(left_ref[:, cols], gk_ref[...])
    away_ref[half:, :] = extra_ref[...]


def vo_kernel(bit, meta_ref, left_ref, gv_ref, kept_o_ref, got_a_ref, got_b_ref, away_ref, kept_ref):
    mine = meta_ref[BITS + bit]
    half = left_ref.shape[1] // 2
    wide = gv_ref.shape[1]
    for kept, ref in enumerate((away_ref, kept_ref)):
        start = pl.multiple_of((mine if kept else 1 - mine) * half, 128)
        ref[:, :wide] = dot_tn(left_ref[:, pl.ds(start, half)], gv_ref[...])
        rows = pl.ds(start, half)
        top = jnp.where(start == 0, got_a_ref[...], got_b_ref[...])
        ref[:, wide:] = kept_o_ref[rows, :] + top


def o_kernel(cols_ref, other_ref, near_ref, first_ref, second_ref, kept_ref):
    half = first_ref.shape[0]
    first_ref[...] = dot_tn(cols_ref[:, :half], other_ref[...])
    second_ref[...] = dot_tn(cols_ref[:, half:], other_ref[...])
    kept_ref[...] = dot_tn(cols_ref[...], near_ref[...])


def round_kernel(wide_ref, a_ref, b_ref, vec_ref):
    rows = a_ref.shape[0]
    step = 64

    @pl.loop(0, rows // step)
    def _(i):
        a_ref[strip(i, step), :] = wide_ref[strip(i, step), :].astype(bf16)

    @pl.loop(0, b_ref.shape[0] // step)
    def _(i):
        b_ref[strip(i, step), :] = wide_ref[strip(i + rows // step, step), :].astype(bf16)

    vec_ref[...] = wide_ref[rows + b_ref.shape[0] :, :]


def feed_kernel(own, unit, blocks, targets, fresh, *refs):
    in_ref, up_ref, up2_ref, vec_ref, vec2_ref, down_ref, down2_ref = refs[:7]
    refs = refs[7 + (0 if fresh else 2) :]
    lo_full, act_full, slope_ref = refs[:3]
    parts = refs[3:-4]
    low_ref, act_ref, cols_ref, sems = refs[-4:]
    hidden = up_ref.shape[1]
    copies = Copies(sems)
    low_ref[...] = in_ref[...].astype(bf16)
    if blocks:
        move_columns(low_ref, cols_ref, blocks)
    else:
        cols_ref[...] = low_ref[...]
    for p, target in enumerate(targets):
        copies.start(cols_ref.at[pl.ds(p * unit, unit), :], lo_full.at[pl.ds(target * unit, unit), :])
    for side, (weight_ref, bias_ref) in enumerate(((up_ref, vec_ref), (up2_ref, vec2_ref))):

        @pl.loop(0, hidden // STRIP)
        def _(i):
            there = strip(i + side * (hidden // STRIP))
            pre = dot_nn(low_ref[...], weight_ref[:, strip(i)]) + bias_ref[UP_BIAS : UP_BIAS + 1, strip(i)]
            normal_cdf = 0.5 * (1.0 + lax.erf(pre * ROOT_HALF))
            density = jnp.exp(-0.5 * pre * pre) * INV_ROOT_TAU
            act_ref[:, there] = (pre * normal_cdf).astype(bf16)
            slope_ref[:, there] = normal_cdf + pre * density

    for p, target in enumerate(targets):
        copies.start(act_ref.at[pl.ds(p * unit, unit), :], act_full.at[pl.ds(target * unit, unit), :])

    @pl.loop(0, down_ref.shape[1] // STRIP)
    def _(i):
        cols = strip(i)
        part = dot_nn(act_ref[:, :hidden], down_ref[:, cols]) + dot_nn(act_ref[:, hidden:], down2_ref[:, cols])
        if own:
            part = part + (in_ref[:, cols] + vec_ref[DOWN_BIAS : DOWN_BIAS + 1, cols])
        for p, part_ref in enumerate(parts):
            part_ref[:, cols] = part[p * unit : (p + 1) * unit]

    copies.wait()


def feed(own, unit, blocks, targets, rows_in, ups, vectors, downs, filled):
    rows, width = rows_in.shape
    hidden = 2 * ups[0].shape[1]
    return whole(
        functools.partial(feed_kernel, own, unit, blocks, targets, not filled),
        "feed",
        [rows_in, *ups, *vectors, *downs],
        [shape(rows, hidden)] + [shape(unit, width)] * len(targets),
        filled=filled or [shape(4 * unit, width, bf16), shape(4 * unit, hidden, bf16)],
        scratch=[
            pltpu.VMEM((rows, width), bf16),
            pltpu.VMEM((rows, hidden), bf16),
            pltpu.VMEM((rows, width), bf16),
        ],
        sems=2 * len(targets),
    )


def back_kernel(own, blocks, offset, target, fresh, block, part, meta_ref, y_ref, og_ref, extra_ref, vec_ref, slope_ref, down_ref, down2_ref, up_ref, up2_ref, *refs):
    refs = refs[0 if fresh else 3 :]
    out_full, gf_full, gp_full, part_ref, ub_ref, mark_ref = refs[:6]
    refs = refs[6:]
    if own:
        two_ref, sums_ref = refs[:2]
        refs = refs[2:]
    gf_ref, out_ref, gp_ref, cols_ref, sems = refs
    rows = y_ref.shape[0]
    hidden = up_ref.shape[1]
    gain = row_of(vec_ref, GAIN_TWO)
    shift = row_of(vec_ref, SHIFT_TWO)
    copies = Copies(sems)
    ids = lax.broadcasted_iota(jnp.int32, (rows, 1), 0)
    number = meta_ref[block]
    base = pl.multiple_of((2 * number + part) * rows, rows)
    limit = meta_ref[LENGTH] - base
    spot = jnp.where(number < meta_ref[COUNT], meta_ref[MARKS + number] - base, -1)
    there = pl.ds(target * rows, rows)
    keep = (ids < limit).astype(f32)
    unit, scale_inv = norm_rows(y_ref[...])
    out_ref[...] = (unit * gain + shift) * keep
    copies.start(out_ref, out_full.at[there, :])
    grad_out = (og_ref[pl.ds(base, rows), :].astype(f32) + jnp.where(ids == spot, extra_ref[pl.ds(number, 1), :], 0.0)) * keep
    grad_two = norm_rows_back(grad_out, unit, scale_inv, gain)
    grad_low = grad_two.astype(bf16)
    gf_ref[...] = grad_low
    if own:
        two_ref[...] = grad_two
        sums_ref[0:1, :] = jnp.sum(grad_low.astype(f32), axis=0, keepdims=True)
        sums_ref[1:2, :] = jnp.sum(grad_out * unit, axis=0, keepdims=True)
        sums_ref[2:3, :] = jnp.sum(grad_out, axis=0, keepdims=True)
        sums_ref[3:8, :] = jnp.zeros((5, sums_ref.shape[1]), f32)
    mark_ref[...] = jnp.zeros_like(mark_ref)

    @pl.when((spot >= 0) & (spot < rows))
    def _():
        row, _ = norm_rows(y_ref[pl.ds(jnp.clip(spot, 0, rows - 1), 1), :])
        mark_ref[0:1, :] = row * gain + shift

    if blocks:
        move_columns(gf_ref, cols_ref, blocks)
    else:
        cols_ref[...] = gf_ref[...]
    copies.start(cols_ref, gf_full.at[there, :])
    for side, weight_ref in enumerate((down_ref, down2_ref)):

        @pl.loop(0, hidden // STRIP)
        def _(i):
            cols = strip(i + side * (hidden // STRIP))
            grad_act = dot_nt(gf_ref[...], weight_ref[strip(i), :])
            grad_pre = (grad_act * slope_ref[pl.ds(offset, rows), cols]).astype(bf16)
            gp_ref[:, cols] = grad_pre
            ub_ref[:, cols] = jnp.sum(grad_pre.astype(f32), axis=0, keepdims=True)

    copies.start(gp_ref, gp_full.at[there, :])

    @pl.loop(0, up_ref.shape[0] // STRIP)
    def _(i):
        cols = strip(i)
        part_ref[:, cols] = dot_nt(gp_ref[:, :hidden], up_ref[cols, :]) + dot_nt(gp_ref[:, hidden:], up2_ref[cols, :])

    copies.wait()


def back(own, blocks, offset, target, block, part, meta, y, out_grad, extra, vectors, slope, downs, ups, filled):
    rows, width = y.shape
    hidden = 2 * ups[0].shape[1]
    outputs = [shape(rows, width), shape(1, hidden), shape(8, width)]
    if own:
        outputs += [shape(rows, width), shape(8, width)]
    return whole(
        functools.partial(back_kernel, own, blocks, offset, target, not filled, block, part),
        "feed_back",
        [y, out_grad, extra, vectors, slope, *downs, *ups],
        outputs,
        scalars=meta,
        filled=filled
        or [shape(4 * rows, width), shape(4 * rows, width, bf16), shape(4 * rows, hidden, bf16)],
        scratch=[
            pltpu.VMEM((rows, width), bf16),
            pltpu.VMEM((rows, width), f32),
            pltpu.VMEM((rows, hidden), bf16),
            pltpu.VMEM((rows, width), bf16),
        ],
        sems=3,
    )


def context_back_kernel(blocks, own_ref, first_ref, sib_ref, near_w_ref, far_w_ref, far_ref, near_ref, sums_ref, *refs):
    low_ref = refs[-1]
    rows = own_ref.shape[0]
    low_ref[:rows, :] = own_ref[...]
    low_ref[rows:, :] = sib_ref[:rows, :].astype(bf16)
    wide = far_ref.shape[1]
    far_ref[: 2 * rows, :] = dot_nt(low_ref[...], far_w_ref[...])
    near_ref[...] = dot_nt(low_ref[...], near_w_ref[...]).astype(bf16)
    for k in range(first_ref.shape[1] // wide):
        cols = slice(k * wide, (k + 1) * wide)
        chip = first_ref[rows : rows + 8, cols] + sib_ref[rows : rows + 8, cols]
        sums_ref[8 * k : 8 * k + 8, :] = chip
        far_ref[2 * rows + 8 * k : 2 * rows + 8 * k + 8, :] = chip
    if blocks:
        move_columns(low_ref, refs[0], blocks)


def first_back_kernel(*refs):
    streams = (refs[:3], refs[3:6])
    chip_ref = refs[6]
    ub_refs = refs[7:11]
    marks = refs[11:15]
    unit_ref, inv_ref, vec_ref, first_ref, low_ref, ub_ref = refs[15:]
    hidden = ub_ref.shape[1]
    ub = ub_refs[0][...] + ub_refs[1][...] + ub_refs[2][...] + ub_refs[3][...]
    ub_ref[...] = ub[:, :hidden]
    gain = row_of(vec_ref, GAIN_ONE)
    size, width = streams[0][0].shape
    rows = 2 * size
    sums = [0.0] * 6
    for half, (two_ref, own_ref, ffn_ref) in enumerate(streams):
        here = pl.ds(half * size, size)
        grad_normed = two_ref[...] + own_ref[...]
        if half:
            grad_normed = grad_normed + chip_ref[...]
        unit = unit_ref[here, :]
        first = norm_rows_back(grad_normed, unit, inv_ref[here, 0:1], gain)
        low = first.astype(bf16)
        first_ref[here, :] = first
        low_ref[here, :] = low
        terms = [low.astype(f32), grad_normed * unit, grad_normed]
        for k in range(3):
            sums[k] = sums[k] + jnp.sum(terms[k], axis=0, keepdims=True)
            sums[k + 3] = sums[k + 3] + ffn_ref[k : k + 1, :]
    for k in range(6):
        first_ref[rows + k : rows + k + 1, :] = sums[k]
    first_ref[rows + 6 : rows + 8, :] = jnp.zeros((2, width), f32)
    first_ref[rows + 8 : rows + 9, :] = ub[:, hidden:]
    first_ref[rows + 9 : rows + 10, :] = marks[0][0:1, :] + marks[1][0:1, :]
    first_ref[rows + 10 : rows + 11, :] = marks[2][0:1, :] + marks[3][0:1, :]
    first_ref[rows + 11 : rows + 16, :] = jnp.zeros((5, width), f32)


def input_kernel(near_ref, far_ref, gk_ref, gv_ref, qw_ref, kw_ref, vw_ref, first_ref, mine_ref, away_ref):
    rows = near_ref.shape[0] // 2
    for p in range(4):
        gq_ref = (near_ref, far_ref)[p // 2]
        here = pl.ds(p * rows, rows)
        value = (
            dot_nt(gq_ref[pl.ds((p % 2) * rows, rows), :], qw_ref[...])
            + dot_nt(gk_ref[here, :], kw_ref[...])
            + dot_nt(gv_ref[here, :], vw_ref[...])
        )
        if p == 0:
            value = value + first_ref[:rows, :]
        (mine_ref, away_ref)[p % 2][pl.ds((p // 2) * rows, rows), :] = value


def chip_kernel(mine_ref, got_ref, keep_ref, send_ref):
    rows = mine_ref.shape[0] // 2
    step = 64

    @pl.loop(0, rows // step)
    def _(i):
        for p in range(2):
            here = strip(i + p * (rows // step), step)
            there = strip(i + (1 - p) * (rows // step), step)
            value = mine_ref[here, :] + got_ref[here, :]
            keep_ref[here, :] = value
            send_ref[there, :] = value


def place_kernel(meta_ref, mine_ref, other_ref, out_ref, sems):
    rows = mine_ref.shape[0] // 2
    copies = Copies(sems)
    for p, block in enumerate((0, 2, 1, 3)):
        ref = (mine_ref, other_ref)[p // 2]
        copies.start(ref.at[pl.ds((p % 2) * rows, rows), :], out_ref.at[strip(meta_ref[block], rows), :])
    copies.wait()


def round_place_kernel(meta_ref, near_ref, far_ref, out_ref, low_ref, sems):
    rows = near_ref.shape[0] // 2
    copies = Copies(sems)
    for p, block in enumerate((0, 2, 1, 3)):
        ref = (near_ref, far_ref)[p // 2]
        low_ref[p * rows : (p + 1) * rows, :] = ref[(p % 2) * rows : (p % 2 + 1) * rows, :].astype(bf16)
        copies.start(low_ref.at[pl.ds(p * rows, rows), :], out_ref.at[strip(meta_ref[block], rows), :])
    copies.wait()


def swap_core(value):
    return lax.ppermute(value, "mp", [(i, i ^ 1) for i in range(4)])


def swap_chip(value):
    return lax.ppermute(value, "mp", [(i, i ^ 2) for i in range(4)])


def gather_rows(own):
    other = swap_chip(own)
    sibling = swap_core(own)
    diagonal = swap_core(other)
    return own, sibling, other, diagonal


def bit_order_blocks(parts, order):
    bits = len(order)
    blocks = []
    for position in range(parts):
        block = 0
        for level, bit in enumerate(order):
            block |= ((position >> (bits - 1 - level)) & 1) << bit
        blocks.append(block)
    return blocks


def bit_order_columns(matrix, parts, order):
    width = matrix.shape[1] // parts
    return jnp.concatenate(
        [matrix[:, b * width : (b + 1) * width] for b in bit_order_blocks(parts, order)], axis=1
    )


def dp_swap(value, parts, bit):
    return lax.ppermute(value, "dp", [(i, i ^ (1 << bit)) for i in range(parts)])


class Sum:
    def __init__(self, parts, order, meta, line, spare=0):
        self.parts, self.order, self.meta, self.line = parts, list(order), meta, line
        self.spare = spare
        self.turned = False
        self.second = None
        self.extra = self.total = self.got = None

    def begin(self, away, total, extra=None):
        self.total, self.extra = total, extra
        self.level = 0
        self.ship(away)

    def ship(self, away):
        self.got = dp_swap(away, self.parts, self.order[self.level])
        self.level += 1

    def step(self):
        if self.got is None:
            return
        got = self.line.hold(self.got)
        self.got = None
        rows, cols = self.total.shape
        ends = self.level == len(self.order)
        riders = 0 if self.extra is None else self.extra.shape[0]
        bit = 0 if ends else self.order[self.level]
        rest = [shape(riders, cols)] if riders else []
        outputs = [shape(rows, cols)]
        if not ends:
            outputs = [shape(rows // 2 + riders + self.spare, cols), shape(rows // 2, cols)]
        if ends and self.turned and rows % 128 == 0:
            outputs = [shape(rows, cols // 2), shape(cols // 2, rows)]
        given = [self.total, got] + ([self.extra] if riders else [])
        result = whole(
            functools.partial(fold_kernel, riders, ends, bit), "fold", given, outputs + rest, scalars=self.meta
        )
        if riders:
            self.extra = result[-1]
        if ends:
            self.total = result[0]
            self.second = result[1] if len(outputs) == 2 else None
            self.line.mark(self.total)
        else:
            self.total = result[1]
            self.ship(result[0])
            self.line.mark(result[0])

    def finish(self):
        while self.got is not None:
            self.step()
        return self.total


class Line:
    def __init__(self):
        self.token = None

    def mark(self, *values):
        self.token = values

    def hold(self, *values):
        if self.token is not None:
            values = lax.optimization_barrier(tuple(values) + self.token)[: len(values)]
        return values if len(values) > 1 else values[0]


def shards(
    dp_size,
    tokens,
    doc_lengths,
    cls_pos,
    cls_count,
    q_weight,
    q_bias,
    k_weight,
    v_weight,
    v_bias,
    o_weight,
    o_bias,
    ln1_gain,
    ln1_bias,
    up_weight,
    up_bias,
    down_weight,
    down_bias,
    ln2_gain,
    ln2_bias,
    out_grad,
    pooled_grad,
):
    slot_len, width = tokens.shape
    rows = slot_len // 4
    half = 2 * rows
    head_width = q_weight.shape[1]
    rank = lax.axis_index("mp")
    place_id = lax.axis_index("dp")
    bits = dp_size.bit_length() - 1
    order_a = list(range(bits))
    order_b = [1, 0] + list(range(2, bits)) if bits > 1 else order_a
    length = doc_lengths[0]
    blocks = [rank ^ j for j in range(4)]

    line = Line()
    sizes = width // dp_size
    fixed_a = bit_order_blocks(dp_size, order_a) if sizes % 128 == 0 else None
    fixed_b = bit_order_blocks(dp_size, order_b) if sizes % 128 == 0 else None
    unit = rows // 2

    row_ids = lax.iota(jnp.int32, rows)
    positions = jnp.concatenate([row_ids + blocks[j] * rows for j in range(4)])
    bias = jnp.where(positions < length, 0.0, MASKED).astype(f32)[None, :]
    meta = jnp.concatenate(
        [
            jnp.stack(blocks).astype(jnp.int32),
            doc_lengths,
            cls_count,
            cls_pos[0],
            jnp.stack([(place_id >> bit) & 1 for bit in range(max(bits, 1))]).astype(jnp.int32),
        ]
    )
    hidden = up_bias.shape[0]

    meta, bias = lax.optimization_barrier((meta, bias))

    o_part, vectors = prepare(
        meta, o_weight, [o_bias, ln1_gain, ln1_bias, ln2_gain, ln2_bias, down_bias, up_bias]
    )
    o_got = swap_chip(o_part)
    line.mark(o_part)
    local, queries_near, queries_far, key_rows, value_rows = qkv(
        meta, line.hold(tokens), (q_weight, k_weight, v_weight), (q_bias, v_bias)
    )
    away_context, lse_far = attn_fwd(queries_far, key_rows, value_rows, bias, 256, f32)
    arrived = swap_chip(away_context)
    line.mark(away_context)
    o_got = line.hold(o_got)
    o_other = dp_swap(o_got, dp_size, 0)
    line.mark(o_got)
    up_held, down_held = line.hold(up_weight, down_weight)
    wide = whole(
        widen_kernel,
        "widen",
        [up_held, down_held, vectors],
        [shape(width + hidden + 8, width)],
        limit=20,
    )[0]
    line.mark(wide)
    wide = swap_core(wide)
    context_near, lse_near = attn_fwd(line.hold(queries_near), key_rows, value_rows, bias, 256, bf16)
    line.mark(context_near)
    if fixed_a:
        local_a, local_b = whole(
            functools.partial(order_kernel, fixed_a, fixed_b),
            "order",
            [line.hold(local)],
            [shape(slot_len, width, bf16)] * 2,
        )
    else:
        local_a = bit_order_columns(local, dp_size, order_a)
        local_b = bit_order_columns(local, dp_size, order_b)
    line.mark(local_a)
    own, sib, context_other, o_far = whole(
        project_kernel,
        "project",
        [context_near, line.hold(arrived), o_weight, o_got, line.hold(o_other)],
        [shape(rows, width), shape(rows, width), shape(half, head_width, bf16), shape(head_width, width, bf16)],
        scalars=meta,
    )
    n_a, n_b, normed, unit_one, inv_one = whole(
        first_norm_kernel,
        "first_norm",
        [own, swap_core(sib), local, vectors],
        [shape(unit, width), shape(unit, width), shape(rows, width), shape(rows, width), shape(rows, 128)],
    )
    line.mark(n_a)
    chip_a = swap_chip(n_a)
    chip_b = swap_chip(n_b)
    up_far, down_far, vectors_far = whole(
        round_kernel,
        "round",
        [line.hold(wide)],
        [shape(width, hidden, bf16), shape(hidden, width, bf16), shape(8, width)],
        limit=20,
    )
    ups = (up_weight, up_far)
    downs = (down_weight, down_far)
    both = (vectors, vectors_far)
    lo, act, slope_near, own_a, own_b = feed(True, unit, fixed_b, (0, 1), normed, ups, both, downs, ())
    line.mark(own_a)
    lo, act, slope_a, part = feed(
        False, unit, fixed_b, (2,), line.hold(chip_a), ups, both, downs, (lo, act)
    )
    got_a = swap_chip(part)
    line.mark(part)
    lo, act, slope_b, part = feed(
        False, unit, fixed_b, (3,), line.hold(chip_b), ups, both, downs, (lo, act)
    )
    got_b = swap_chip(part)
    line.mark(part)

    def back_rows(own, k, y, slope, offset, filled):
        place = k if own else 2 + k
        return back(
            own, fixed_a, offset, place, 0 if own else 2, k, meta, y, out_grad, pooled_grad[0], vectors,
            slope, downs, ups, filled,
        )

    y_a = add(own_a, line.hold(got_a))
    chip_a = swap_chip(y_a)
    *filled, back_a, ub_a, mark_a, two_a, sums_a = back_rows(True, 0, y_a, slope_near, 0, ())
    line.mark(back_a)
    y_b = add(own_b, line.hold(got_b))
    chip_b = swap_chip(y_b)
    *filled, back_b, ub_b, mark_b, two_b, sums_b = back_rows(True, 1, y_b, slope_near, unit, filled)
    line.mark(back_b)
    *filled, part, ub_c, mark_c = back_rows(False, 0, line.hold(chip_a), slope_a, 0, filled)
    got_a = swap_chip(part)
    line.mark(part)
    *filled, part, ub_d, mark_d = back_rows(False, 1, line.hold(chip_b), slope_b, 0, filled)
    got_b = swap_chip(part)
    line.mark(part)
    back_a = add(back_a, line.hold(got_a))
    line.mark(back_a)
    out_wide, grad_fed, grad_pre = filled

    def in_order(value, fixed, order):
        return value if fixed else bit_order_columns(value, dp_size, order)

    gf_cols, lo_cols = in_order(grad_fed, fixed_a, order_a), in_order(lo, fixed_b, order_b)
    down_sum = Sum(dp_size, order_a, meta, line, 0)
    up_sum = Sum(dp_size, order_b, meta, line, 0)

    def pair(side, sum_of, left, right, given=()):
        half_rows = width // 2
        return whole(
            functools.partial(pair_kernel, side, bool(given), sum_of.order[0]),
            "pair",
            [left, right, *given],
            [shape(half_rows, hidden)] * 2 if given else [shape(width, hidden)],
            scalars=meta,
        )

    down_other = pair(1, down_sum, line.hold(gf_cols), act)[0]
    down_given = swap_core(down_other)
    line.mark(down_other)
    up_other = pair(1, up_sum, lo_cols, line.hold(grad_pre))[0]
    up_given = swap_core(up_other)
    line.mark(up_other)

    down_sum.begin(*pair(0, down_sum, gf_cols, act, [line.hold(down_given)]))
    up_sum.begin(*pair(0, up_sum, lo_cols, grad_pre, [line.hold(up_given)]))

    line.mark(down_sum.total, up_sum.total)
    got_b = line.hold(got_b)
    first_ext, grad_attended_own, up_bias_own = whole(
        first_back_kernel,
        "first_norm_back",
        [two_a, back_a, sums_a, two_b, back_b, sums_b, got_b, ub_a, ub_b, ub_c, ub_d]
        + [mark_a, mark_b, mark_c, mark_d, unit_one, inv_one, vectors],
        [shape(rows + 16, width), shape(rows, width, bf16), shape(1, hidden)],
    )
    sib_ext = swap_core(first_ext)
    riders = 8 * width // head_width
    context_far_grad, grad_context_near, chip_sums, *ga_cols = whole(
        functools.partial(context_back_kernel, fixed_b),
        "context_back",
        [grad_attended_own, first_ext, sib_ext, o_weight, o_far],
        [shape(half + riders, head_width), shape(half, head_width, bf16), shape(riders, head_width)]
        + [shape(half, width, bf16)] * (2 if fixed_b else 1),
    )
    ga_cols = in_order(ga_cols[0], fixed_b, order_b)
    grad_context_far = swap_chip(context_far_grad)
    line.mark(context_far_grad)
    *o_away, o_kept = whole(
        o_kernel,
        "o_grad",
        [line.hold(ga_cols), context_other, context_near],
        [shape(width // 2, head_width)] * 2 + [shape(width, head_width)],
    )
    o_got = [swap_chip(v) for v in o_away]
    line.mark(o_kept)

    queries_near = line.hold(queries_near)
    grad_q_near, key_sum, value_sum = attn_bwd(
        queries_near, grad_context_near, key_rows, value_rows, bias, lse_near, 256
    )
    line.mark(grad_q_near)
    grad_context_far = line.hold(grad_context_far)
    line.mark(grad_context_far)
    queries_far = line.hold(queries_far)
    grad_q_far, grad_k, grad_v = attn_bwd(
        queries_far, grad_context_far, key_rows, value_rows, bias, lse_far, 256, (key_sum, value_sum)
    )
    line.mark(grad_k)

    qk_sum = Sum(dp_size, order_a, meta, line)
    vo_sum = Sum(dp_size, order_b, meta, line)
    vo_sum.turned = True
    riders = 8 * width // head_width
    extra_rows = -(-(riders // 2 + 1 + hidden // (2 * head_width)) // 8) * 8
    qk_away, qk_kept, qk_extra = whole(
        functools.partial(qk_kernel, qk_sum.order[0]),
        "qk_grad",
        [local_a, line.hold(grad_q_near), grad_q_far, grad_k, grad_v, chip_sums, grad_context_far]
        + [up_bias_own, sib_ext],
        [
            shape(width // 2 + extra_rows, 2 * head_width),
            shape(width // 2, 2 * head_width),
            shape(extra_rows, 2 * head_width),
        ],
        scalars=meta,
    )
    line.mark(qk_away)
    o_got = line.hold(*o_got)
    line.mark(*o_got)
    down_sum.step()
    up_sum.step()
    in_mine, in_away = whole(
        input_kernel,
        "input_grad",
        [line.hold(grad_q_near), grad_q_far, grad_k, grad_v, q_weight, k_weight, v_weight, first_ext],
        [shape(half, width)] * 2,
    )
    in_got = swap_core(in_away)
    line.mark(in_mine)
    in_kept, in_sent = whole(
        chip_kernel, "chip_sum", [in_mine, line.hold(in_got)], [shape(half, width)] * 2
    )
    in_got = swap_chip(in_sent)
    line.mark(in_sent)
    vo_away, vo_kept = whole(
        functools.partial(vo_kernel, vo_sum.order[0]),
        "vo_grad",
        [local_b, line.hold(grad_v), o_kept, *o_got],
        [shape(width // 2, 2 * head_width)] * 2,
        scalars=meta,
    )
    line.mark(vo_away)
    down_sum.step()
    up_sum.step()
    qk_sum.begin(line.hold(qk_away), qk_kept, qk_extra)
    vo_sum.begin(line.hold(vo_away), vo_kept)
    for bit in range(bits):
        qk_sum.step()
        if bit == 0:
            down_sum.step()
            up_sum.step()
        vo_sum.step()
        if bit > 1:
            down_sum.step()
            up_sum.step()
        if bit == min(1, bits - 1):
            in_final = add(in_kept, line.hold(in_got))
            in_other = swap_core(in_final)
            out_far = swap_core(line.hold(out_wide))
            line.mark(in_final)
            in_grad = whole(
                place_kernel,
                "place",
                [in_final, line.hold(in_other)],
                [],
                scalars=meta,
                filled=[shape(slot_len, width)],
                sems=4,
                far=True,
            )[0]
            line.mark(in_grad)
            out = whole(
                round_place_kernel,
                "round_place",
                [out_wide, line.hold(out_far)],
                [],
                scalars=meta,
                filled=[shape(slot_len, width, bf16)],
                scratch=[pltpu.VMEM((slot_len, width), bf16)],
                sems=4,
                far=True,
            )[0]
            line.mark(out)
    qk_total, vo_total = qk_sum.finish(), vo_sum.finish()
    riding = qk_sum.extra
    row = riders // 2
    shared = jnp.concatenate([riding[:row, :head_width], riding[:row, head_width:]], axis=0)
    shared = shared.reshape(-1, 8, head_width).transpose(1, 0, 2).reshape(8, width)
    biases = riding[row].reshape(2, head_width)
    up_bias_sum = riding[row + 1 : row + 1 + hidden // (2 * head_width)].reshape(-1)
    if vo_sum.second is None:
        v_sum, o_sum = vo_total[:, :head_width], vo_total[:, head_width:].T
    else:
        v_sum, o_sum = vo_total, vo_sum.second
    down_sum = down_sum.finish().T
    up_sum = up_sum.finish()

    mine = first_ext[rows + 9 : rows + 11]
    theirs = sib_ext[rows + 9 : rows + 11]
    marks = jnp.concatenate([mine[:1], theirs[:1], mine[1:], theirs[1:]], axis=0)
    pooled = jnp.concatenate(
        [lax.dynamic_index_in_dim(marks, blocks[j], keepdims=True) for j in range(4)], axis=0
    )[None]
    return (
        out,
        pooled,
        in_grad,
        qk_total[:, :head_width],
        biases[0],
        qk_total[:, head_width:],
        v_sum,
        biases[1],
        o_sum,
        shared[0],
        shared[1],
        shared[2],
        up_sum,
        up_bias_sum,
        down_sum,
        shared[3],
        shared[4],
        shared[5],
    )


def solution(mesh):
    return jax.shard_map(
        functools.partial(shards, mesh.shape["dp"]),
        mesh=mesh,
        in_specs=(
            P("dp", None),
            P("dp"),
            P("dp", None),
            P("dp"),
            P(None, "mp"),
            P("mp"),
            P(None, "mp"),
            P(None, "mp"),
            P("mp"),
            P("mp", None),
            P(),
            P(),
            P(),
            P(None, "mp"),
            P("mp"),
            P("mp", None),
            P(),
            P(),
            P(),
            P("dp", None),
            P("dp", None, None),
        ),
        out_specs=(
            P("dp", None),
            P("dp", None, None),
            P("dp", None),
            P("dp", "mp"),
            P("mp"),
            P("dp", "mp"),
            P("dp", "mp"),
            P("mp"),
            P("mp", "dp"),
            P(),
            P(),
            P(),
            P("dp", "mp"),
            P("mp"),
            P("mp", "dp"),
            P(),
            P(),
            P(),
        ),
        check_vma=False,
    )
```

```python
import functools

import jax
import jax.numpy as jnp
from jax import lax
from jax.experimental import pallas as pl
from jax.experimental.pallas import tpu as pltpu
from jax.sharding import PartitionSpec as P

HEAD_DIM = 64
NORM_EPS = 1e-05
ROOT_HALF = 0.7071067811865476
INV_ROOT_TAU = 0.3989422804014327
LOG2E = 1.4426950408889634
SCORE_SCALE = 0.125 * LOG2E
MASKED = -1e30

f32 = jnp.float32
bf16 = jnp.bfloat16
VMEM_LIMIT = 20 * 1024 * 1024


def dot_nn(a, b):
    return lax.dot_general(a, b, (((1,), (0,)), ((), ())), preferred_element_type=f32)


def dot_nt(a, b):
    return lax.dot_general(a, b, (((1,), (1,)), ((), ())), preferred_element_type=f32)


def dot_tn(a, b):
    return lax.dot_general(a, b, (((0,), (0,)), ((), ())), preferred_element_type=f32)


def attn_fwd_kernel(q_ref, k_ref, v_ref, bias_ref, o_ref, lse_ref):
    rows, width = q_ref.shape
    heads = width // HEAD_DIM
    lane = lax.broadcasted_iota(jnp.int32, (1, width), 1) // HEAD_DIM
    lse_lane = lax.broadcasted_iota(jnp.int32, (1, 128), 1)
    q = q_ref[...]
    k = k_ref[...]
    v = v_ref[...]
    bias = bias_ref[...]
    out = jnp.zeros((rows, width), f32)
    lse = jnp.zeros((rows, 128), f32)
    for h in range(heads):
        qh = jnp.where(lane == h, q, jnp.zeros_like(q))
        s = dot_nt(qh, k) * SCORE_SCALE + bias
        top = jnp.max(s, axis=1, keepdims=True)
        e = jnp.exp2(s - top)
        total = jnp.sum(e, axis=1, keepdims=True)
        p = (e * (1.0 / total)).astype(bf16)
        c = dot_nn(p, v)
        out = jnp.where(lane == h, c, out)
        lse = jnp.where(lse_lane == h, top + jnp.log2(total), lse)
    o_ref[...] = out.astype(o_ref.dtype)
    lse_ref[...] = lse


def attn_fwd(q, k, v, bias, block, dtype):
    rows, width = q.shape
    keys = k.shape[0]
    full = pl.BlockSpec((keys, width), lambda i: (0, 0))
    return pl.pallas_call(
        attn_fwd_kernel,
        grid=(rows // block,),
        in_specs=[
            pl.BlockSpec((block, width), lambda i: (i, 0)),
            full,
            full,
            pl.BlockSpec((1, keys), lambda i: (0, 0)),
        ],
        out_specs=[
            pl.BlockSpec((block, width), lambda i: (i, 0)),
            pl.BlockSpec((block, 128), lambda i: (i, 0)),
        ],
        out_shape=[
            jax.ShapeDtypeStruct((rows, width), dtype),
            jax.ShapeDtypeStruct((rows, 128), f32),
        ],
        compiler_params=pltpu.CompilerParams(vmem_limit_bytes=VMEM_LIMIT),
        cost_estimate=pl.CostEstimate(flops=1024, bytes_accessed=1024, transcendentals=0),
        name="attn_fwd",
    )(q, k, v, bias)


def attn_bwd_kernel(carried, *refs):
    q_ref, g_ref, k_ref, v_ref, bias_ref, lse_ref = refs[:6]
    refs = refs[6:]
    if carried:
        gk_in, gv_in = refs[:2]
        refs = refs[2:]
    gq_ref, gk_ref, gv_ref, gk_acc, gv_acc, gq_acc = refs
    step = pl.program_id(0)
    width = q_ref.shape[1]
    lane = lax.broadcasted_iota(jnp.int32, (1, width), 1) // HEAD_DIM
    lse_lane = lax.broadcasted_iota(jnp.int32, (1, 128), 1)

    @pl.when(step == 0)
    def _():
        gk_acc[...] = gk_in[...] if carried else jnp.zeros_like(gk_acc)
        gv_acc[...] = gv_in[...] if carried else jnp.zeros_like(gv_acc)

    @pl.loop(0, width // HEAD_DIM)
    def _(h):
        mine = lane == h
        zero = jnp.zeros(q_ref.shape, bf16)
        qh = jnp.where(mine, q_ref[...], zero)
        gh = jnp.where(mine, g_ref[...].astype(bf16), zero)
        lse = jnp.sum(jnp.where(lse_lane == h, lse_ref[...], 0.0), axis=1, keepdims=True)
        s = dot_nt(qh, k_ref[...]) * SCORE_SCALE + bias_ref[...]
        p = jnp.exp2(s - lse)
        dp = dot_nt(gh, v_ref[...])
        inner = jnp.sum(p * dp, axis=1, keepdims=True)
        ds = (p * (dp - inner)).astype(bf16)
        gq_acc[...] = jnp.where(mine, dot_nn(ds, k_ref[...]), gq_acc[...])
        gk_acc[...] += dot_tn(ds, qh)
        gv_acc[...] += dot_tn(p.astype(bf16), gh)

    gq_ref[...] = (gq_acc[...] * 0.125).astype(bf16)

    @pl.when(step == pl.num_programs(0) - 1)
    def _():
        scale = 0.125 if carried else 1.0
        gk_ref[...] = (gk_acc[...] * scale).astype(gk_ref.dtype)
        gv_ref[...] = gv_acc[...].astype(gv_ref.dtype)


def attn_bwd(q, g, k, v, bias, lse, block, sums=()):
    rows, width = q.shape
    keys = k.shape[0]
    full = pl.BlockSpec((keys, width), lambda i: (0, 0))
    part = pl.BlockSpec((block, width), lambda i: (i, 0))
    sum_type = bf16 if sums else f32
    return pl.pallas_call(
        functools.partial(attn_bwd_kernel, bool(sums)),
        grid=(rows // block,),
        in_specs=[
            part,
            part,
            full,
            full,
            pl.BlockSpec((1, keys), lambda i: (0, 0)),
            pl.BlockSpec((block, 128), lambda i: (i, 0)),
        ]
        + [full] * len(sums),
        out_specs=[part, full, full],
        out_shape=[
            jax.ShapeDtypeStruct((rows, width), bf16),
            jax.ShapeDtypeStruct((keys, width), sum_type),
            jax.ShapeDtypeStruct((keys, width), sum_type),
        ],
        scratch_shapes=[pltpu.VMEM((keys, width), f32)] * 2 + [pltpu.VMEM((block, width), f32)],
        compiler_params=pltpu.CompilerParams(vmem_limit_bytes=VMEM_LIMIT),
        cost_estimate=pl.CostEstimate(flops=1024, bytes_accessed=1024, transcendentals=0),
        name="attn_bwd",
    )(q, g, k, v, bias, lse, *sums)


in_vmem = pl.BlockSpec(memory_space=pltpu.VMEM)
STRIP = 256
LENGTH, COUNT, MARKS, BITS = 4, 5, 6, 10
O_BIAS, GAIN_ONE, SHIFT_ONE, GAIN_TWO, SHIFT_TWO, DOWN_BIAS, UP_BIAS, QV_BIAS = range(8)


def row_of(ref, index):
    return ref[index : index + 1, :]


def strip(index, size=STRIP):
    return pl.ds(pl.multiple_of(index * size, size), size)


def shape(rows, cols, dtype=f32):
    return jax.ShapeDtypeStruct((rows, cols), dtype)


def whole(kernel, name, inputs, outputs, scalars=None, filled=(), sems=0, scratch=(), limit=8, far=False):
    lead = [] if scalars is None else [scalars]
    anywhere = pl.BlockSpec(memory_space=pl.ANY)
    given = [v for v in filled if not isinstance(v, jax.ShapeDtypeStruct)]
    begun = [jax.ShapeDtypeStruct(v.shape, v.dtype) for v in filled]
    first = len(lead) + len(inputs)
    return pl.pallas_call(
        kernel,
        in_specs=[pl.BlockSpec(memory_space=pltpu.SMEM)] * len(lead)
        + [in_vmem] * len(inputs)
        + [anywhere] * len(given),
        out_specs=[pl.BlockSpec(memory_space=pltpu.HBM) if far else anywhere] * len(begun)
        + [in_vmem] * len(outputs),
        out_shape=begun + list(outputs),
        scratch_shapes=list(scratch) + ([pltpu.SemaphoreType.DMA((sems,))] if sems else []),
        input_output_aliases={first + p: p for p in range(len(given))},
        compiler_params=pltpu.CompilerParams(vmem_limit_bytes=limit * 1024 * 1024),
        cost_estimate=pl.CostEstimate(flops=1024, bytes_accessed=1024, transcendentals=0),
        name=name,
    )(*lead, *inputs, *given)


class Copies:
    def __init__(self, sems):
        self.sems, self.made = sems, []

    def start(self, source, target):
        copy = pltpu.make_async_copy(source, target, self.sems.at[len(self.made)])
        copy.start()
        self.made.append(copy)

    def wait(self):
        for copy in self.made:
            copy.wait()


def project_kernel(meta_ref, near_ref, other_ref, o_near_ref, o_got_ref, o_other_ref, own_ref, sib_ref, low_ref, o_far_ref):
    rows = own_ref.shape[0]
    part = o_got_ref.shape[0]
    first = meta_ref[BITS] == 0
    o_far_ref[:part, :] = jnp.where(first, o_got_ref[...], o_other_ref[...]).astype(bf16)
    o_far_ref[part:, :] = jnp.where(first, o_other_ref[...], o_got_ref[...]).astype(bf16)
    low_ref[...] = other_ref[...].astype(bf16)
    both = dot_nn(near_ref[...], o_near_ref[...]) + dot_nn(low_ref[...], o_far_ref[...])
    own_ref[...] = both[:rows]
    sib_ref[...] = both[rows:]


def mean_of(values):
    return jnp.sum(values, axis=-1, keepdims=True) * (1.0 / values.shape[-1])


def norm_rows(values):
    centre = values - mean_of(values)
    scale_inv = lax.rsqrt(mean_of(centre * centre) + NORM_EPS)
    return centre * scale_inv, scale_inv


def norm_rows_back(grad_rows, unit_rows, scale_inv, gain):
    scaled = grad_rows * gain
    return scale_inv * (scaled - mean_of(scaled) - unit_rows * mean_of(scaled * unit_rows))


def first_norm_kernel(own_ref, near_ref, tok_ref, vec_ref, na_ref, nb_ref, all_ref, unit_ref, inv_ref):
    gain = row_of(vec_ref, GAIN_ONE)
    shift = row_of(vec_ref, SHIFT_ONE)
    for half, out_ref in enumerate((na_ref, nb_ref)):
        size = out_ref.shape[0]
        rows = pl.ds(half * size, size)
        values = tok_ref[rows, :].astype(f32) + (own_ref[rows, :] + near_ref[rows, :] + row_of(vec_ref, O_BIAS))
        unit, scale_inv = norm_rows(values)
        unit_ref[rows, :] = unit
        inv_ref[rows, :] = jnp.broadcast_to(scale_inv, (size, inv_ref.shape[1]))
        normed = unit * gain + shift
        out_ref[...] = normed
        all_ref[rows, :] = normed


def move_columns(source, target, blocks):
    wide = source.shape[1] // len(blocks)
    for place, block in enumerate(blocks):
        target[:, place * wide : (place + 1) * wide] = source[:, block * wide : (block + 1) * wide]


def order_kernel(blocks_a, blocks_b, in_ref, a_ref, b_ref):
    move_columns(in_ref, a_ref, blocks_a)
    move_columns(in_ref, b_ref, blocks_b)


def prepare_kernel(meta_ref, o_ref, *refs):
    given = refs[:7]
    part_ref, vec_ref, o_in = refs[7:10]
    lines = refs[10:17]
    sems = refs[17]
    copies = Copies(sems)
    copies.start(o_ref.at[strip(meta_ref[BITS], part_ref.shape[0]), :], o_in)
    for line_ref, vector_ref in zip(lines, given):
        copies.start(vector_ref, line_ref)
    copies.wait()
    part_ref[...] = o_in[...].astype(f32)
    vec_ref[...] = jnp.zeros_like(vec_ref)
    for k, line_ref in enumerate(lines):
        vec_ref[k, :] = line_ref[...].astype(f32)


def prepare(meta, o_weight, vectors):
    rows, width = o_weight.shape
    far = pl.BlockSpec(memory_space=pltpu.HBM)
    return pl.pallas_call(
        prepare_kernel,
        in_specs=[pl.BlockSpec(memory_space=pltpu.SMEM)] + [far] * 8,
        out_specs=[in_vmem] * 2,
        out_shape=[shape(rows // 2, width), shape(8, width)],
        scratch_shapes=[pltpu.VMEM((rows // 2, width), bf16)]
        + [pltpu.VMEM((width,), bf16)] * 7
        + [pltpu.SemaphoreType.DMA((8,))],
        compiler_params=pltpu.CompilerParams(vmem_limit_bytes=60 * 1024 * 1024),
        cost_estimate=pl.CostEstimate(flops=1024, bytes_accessed=1024, transcendentals=0),
        name="prepare",
    )(meta, o_weight, *vectors)


def widen_kernel(a_ref, b_ref, vec_ref, wide_ref):
    rows = a_ref.shape[0]
    step = 64

    @pl.loop(0, rows // step)
    def _(i):
        wide_ref[strip(i, step), :] = a_ref[strip(i, step), :].astype(f32)

    @pl.loop(0, b_ref.shape[0] // step)
    def _(i):
        wide_ref[strip(i + rows // step, step), :] = b_ref[strip(i, step), :].astype(f32)

    wide_ref[rows + b_ref.shape[0] :, :] = vec_ref[...]


def qkv_kernel(meta_ref, all_ref, qw_ref, kw_ref, vw_ref, *refs):
    given = refs[:2]
    vec_ref, local_ref, near_ref, far_ref, k_ref, v_ref, q_in, k_in, v_in, qb_in, vb_in, sems = refs[2:]
    half, wide = near_ref.shape
    rows = half // 2
    copies = Copies(sems)
    copies.start(given[0], qb_in)
    copies.start(given[1], vb_in)
    for p in range(4):
        copies.start(all_ref.at[strip(meta_ref[p], rows), :], local_ref.at[pl.ds(p * rows, rows), :])
    copies.start(kw_ref, k_in)
    copies.start(qw_ref, q_in)
    copies.start(vw_ref, v_in)
    copies.wait()
    k_ref[...] = dot_nn(local_ref[...], k_in[...]).astype(bf16)
    vec_ref[0, :] = qb_in[...].astype(f32)
    vec_ref[1, :] = vb_in[...].astype(f32)
    q = (dot_nn(local_ref[...], q_in[...]) + vec_ref[0:1, :]).astype(bf16)
    near_ref[...] = q[:half]
    far_ref[...] = q[half:]
    v_ref[...] = (dot_nn(local_ref[...], v_in[...]) + vec_ref[1:2, :]).astype(bf16)


def qkv(meta, tokens, weights, biases):
    rows, width = tokens.shape
    wide = weights[0].shape[1]
    far = pl.BlockSpec(memory_space=pltpu.HBM)
    return pl.pallas_call(
        qkv_kernel,
        in_specs=[pl.BlockSpec(memory_space=pltpu.SMEM)] + [far] * 6,
        out_specs=[in_vmem] * 6,
        out_shape=[shape(8, wide), shape(rows, width, bf16)]
        + [shape(rows // 2, wide, bf16)] * 2
        + [shape(rows, wide, bf16)] * 2,
        scratch_shapes=[pltpu.VMEM((width, wide), bf16)] * 3
        + [pltpu.VMEM((wide,), bf16)] * 2
        + [pltpu.SemaphoreType.DMA((9,))],
        compiler_params=pltpu.CompilerParams(vmem_limit_bytes=58 * 1024 * 1024),
        cost_estimate=pl.CostEstimate(flops=1024, bytes_accessed=1024, transcendentals=0),
        name="qkv",
    )(meta, tokens, *weights, *biases)[1:]


def add_kernel(*refs):
    step = 64

    @pl.loop(0, refs[0].shape[0] // step)
    def _(i):
        here = strip(i, step)
        total = refs[0][here, :]
        for ref in refs[1:-1]:
            total = total + ref[here, :]
        refs[-1][here, :] = total


def add(*values):
    return whole(add_kernel, "add", list(values), [shape(*values[0].shape)])[0]


def pair_kernel(side, fill, bit, meta_ref, left_ref, right_ref, *refs):
    mine = meta_ref[BITS + bit]
    half = left_ref.shape[1] // 2
    hidden = right_ref.shape[1] // 2
    right = right_ref[:, side * hidden : (side + 1) * hidden]
    for kept in range(2):
        start = pl.multiple_of((mine if kept else 1 - mine) * half, 128)
        value = dot_tn(left_ref[:, pl.ds(start, half)], right)
        if fill:
            refs[1 + kept][...] = value + refs[0][kept * half : (kept + 1) * half, :]
        else:
            refs[0][kept * half : (kept + 1) * half, :] = value


def fold_kernel(riders, ends, bit, meta_ref, total_ref, got_ref, *refs):
    rows = total_ref.shape[0]
    if riders:
        extra_ref = refs[0]
        refs = refs[1:]
        extra = extra_ref[...] + got_ref[rows:, :]
    if ends and len(refs) == 2 and not riders:
        wide = total_ref.shape[1] // 2
        refs[0][...] = total_ref[:, :wide] + got_ref[:rows, :wide]
        refs[1][...] = (total_ref[:, wide:] + got_ref[:rows, wide:]).T
        return
    if ends:
        refs[0][...] = total_ref[...] + got_ref[:rows, :]
        if riders:
            refs[1][...] = extra
        return
    half = rows // 2
    mine = meta_ref[BITS + bit]
    step = min(64, half)

    @pl.loop(0, half // step)
    def _(i):
        away = strip((1 - mine) * (half // step) + i, step)
        kept = strip(mine * (half // step) + i, step)
        refs[0][strip(i, step), :] = total_ref[away, :] + got_ref[away, :]
        refs[1][strip(i, step), :] = total_ref[kept, :] + got_ref[kept, :]

    if riders:
        refs[0][half:, :] = extra
        refs[2][...] = extra
    elif refs[0].shape[0] > half:
        refs[0][half:, :] = jnp.zeros((refs[0].shape[0] - half, refs[0].shape[1]), f32)


def qk_kernel(bit, meta_ref, left_ref, near_ref, far_ref, gk_ref, gv_ref, chip_ref, far_sums_ref, ub_ref, sib_ref, away_ref, kept_ref, extra_ref):
    mine = meta_ref[BITS + bit]
    half = left_ref.shape[1] // 2
    rows = near_ref.shape[0]
    wide = near_ref.shape[1]
    riders = chip_ref.shape[0]
    extra_ref[...] = jnp.zeros_like(extra_ref)
    shared = chip_ref[...] + far_sums_ref[far_sums_ref.shape[0] - riders :, :]
    extra_ref[: riders // 2, :wide] = shared[: riders // 2]
    extra_ref[: riders // 2, wide:] = shared[riders // 2 :]
    row = riders // 2
    query_sum = jnp.sum(near_ref[...].astype(f32), axis=0, keepdims=True)
    extra_ref[row : row + 1, :wide] = query_sum + jnp.sum(far_ref[...].astype(f32), axis=0, keepdims=True)
    extra_ref[row : row + 1, wide:] = jnp.sum(gv_ref[...].astype(f32), axis=0, keepdims=True)
    place = sib_ref.shape[0] - 8
    for k in range(ub_ref.shape[1] // (2 * wide)):
        cols = slice(2 * k * wide, 2 * (k + 1) * wide)
        extra_ref[row + 1 + k : row + 2 + k, :] = ub_ref[:, cols] + sib_ref[place : place + 1, cols]
    for kept, ref in enumerate((away_ref, kept_ref)):
        cols = pl.ds(pl.multiple_of((mine if kept else 1 - mine) * half, 128), half)
        ref[:half, :wide] = dot_tn(left_ref[:rows, cols], near_ref[...]) + dot_tn(left_ref[rows:, cols], far_ref[...])
        ref[:half, wide:] = dot_tn(left_ref[:, cols], gk_ref[...])
    away_ref[half:, :] = extra_ref[...]


def vo_kernel(bit, meta_ref, left_ref, gv_ref, kept_o_ref, got_a_ref, got_b_ref, away_ref, kept_ref):
    mine = meta_ref[BITS + bit]
    half = left_ref.shape[1] // 2
    wide = gv_ref.shape[1]
    for kept, ref in enumerate((away_ref, kept_ref)):
        start = pl.multiple_of((mine if kept else 1 - mine) * half, 128)
        ref[:, :wide] = dot_tn(left_ref[:, pl.ds(start, half)], gv_ref[...])
        rows = pl.ds(start, half)
        top = jnp.where(start == 0, got_a_ref[...], got_b_ref[...])
        ref[:, wide:] = kept_o_ref[rows, :] + top


def o_kernel(cols_ref, other_ref, near_ref, first_ref, second_ref, kept_ref):
    half = first_ref.shape[0]
    first_ref[...] = dot_tn(cols_ref[:, :half], other_ref[...])
    second_ref[...] = dot_tn(cols_ref[:, half:], other_ref[...])
    kept_ref[...] = dot_tn(cols_ref[...], near_ref[...])


def round_kernel(wide_ref, a_ref, b_ref, vec_ref):
    rows = a_ref.shape[0]
    step = 64

    @pl.loop(0, rows // step)
    def _(i):
        a_ref[strip(i, step), :] = wide_ref[strip(i, step), :].astype(bf16)

    @pl.loop(0, b_ref.shape[0] // step)
    def _(i):
        b_ref[strip(i, step), :] = wide_ref[strip(i + rows // step, step), :].astype(bf16)

    vec_ref[...] = wide_ref[rows + b_ref.shape[0] :, :]


def feed_kernel(own, unit, blocks, targets, fresh, *refs):
    in_ref, up_ref, up2_ref, vec_ref, vec2_ref, down_ref, down2_ref = refs[:7]
    refs = refs[7 + (0 if fresh else 2) :]
    lo_full, act_full, slope_ref = refs[:3]
    parts = refs[3:-4]
    low_ref, act_ref, cols_ref, sems = refs[-4:]
    hidden = up_ref.shape[1]
    copies = Copies(sems)
    low_ref[...] = in_ref[...].astype(bf16)
    if blocks:
        move_columns(low_ref, cols_ref, blocks)
    else:
        cols_ref[...] = low_ref[...]
    for p, target in enumerate(targets):
        copies.start(cols_ref.at[pl.ds(p * unit, unit), :], lo_full.at[pl.ds(target * unit, unit), :])
    for side, (weight_ref, bias_ref) in enumerate(((up_ref, vec_ref), (up2_ref, vec2_ref))):

        @pl.loop(0, hidden // STRIP)
        def _(i):
            there = strip(i + side * (hidden // STRIP))
            pre = dot_nn(low_ref[...], weight_ref[:, strip(i)]) + bias_ref[UP_BIAS : UP_BIAS + 1, strip(i)]
            normal_cdf = 0.5 * (1.0 + lax.erf(pre * ROOT_HALF))
            density = jnp.exp(-0.5 * pre * pre) * INV_ROOT_TAU
            act_ref[:, there] = (pre * normal_cdf).astype(bf16)
            slope_ref[:, there] = normal_cdf + pre * density

    for p, target in enumerate(targets):
        copies.start(act_ref.at[pl.ds(p * unit, unit), :], act_full.at[pl.ds(target * unit, unit), :])

    @pl.loop(0, down_ref.shape[1] // STRIP)
    def _(i):
        cols = strip(i)
        part = dot_nn(act_ref[:, :hidden], down_ref[:, cols]) + dot_nn(act_ref[:, hidden:], down2_ref[:, cols])
        if own:
            part = part + (in_ref[:, cols] + vec_ref[DOWN_BIAS : DOWN_BIAS + 1, cols])
        for p, part_ref in enumerate(parts):
            part_ref[:, cols] = part[p * unit : (p + 1) * unit]

    copies.wait()


def feed(own, unit, blocks, targets, rows_in, ups, vectors, downs, filled):
    rows, width = rows_in.shape
    hidden = 2 * ups[0].shape[1]
    return whole(
        functools.partial(feed_kernel, own, unit, blocks, targets, not filled),
        "feed",
        [rows_in, *ups, *vectors, *downs],
        [shape(rows, hidden)] + [shape(unit, width)] * len(targets),
        filled=filled or [shape(4 * unit, width, bf16), shape(4 * unit, hidden, bf16)],
        scratch=[
            pltpu.VMEM((rows, width), bf16),
            pltpu.VMEM((rows, hidden), bf16),
            pltpu.VMEM((rows, width), bf16),
        ],
        sems=2 * len(targets),
    )


def back_kernel(own, blocks, offset, target, fresh, block, part, meta_ref, y_ref, og_ref, extra_ref, vec_ref, slope_ref, down_ref, down2_ref, up_ref, up2_ref, *refs):
    refs = refs[0 if fresh else 3 :]
    out_full, gf_full, gp_full, part_ref, ub_ref, mark_ref = refs[:6]
    refs = refs[6:]
    if own:
        two_ref, sums_ref = refs[:2]
        refs = refs[2:]
    gf_ref, out_ref, gp_ref, cols_ref, sems = refs
    rows = y_ref.shape[0]
    hidden = up_ref.shape[1]
    gain = row_of(vec_ref, GAIN_TWO)
    shift = row_of(vec_ref, SHIFT_TWO)
    copies = Copies(sems)
    ids = lax.broadcasted_iota(jnp.int32, (rows, 1), 0)
    number = meta_ref[block]
    base = pl.multiple_of((2 * number + part) * rows, rows)
    limit = meta_ref[LENGTH] - base
    spot = jnp.where(number < meta_ref[COUNT], meta_ref[MARKS + number] - base, -1)
    there = pl.ds(target * rows, rows)
    keep = (ids < limit).astype(f32)
    unit, scale_inv = norm_rows(y_ref[...])
    out_ref[...] = (unit * gain + shift) * keep
    copies.start(out_ref, out_full.at[there, :])
    grad_out = (og_ref[pl.ds(base, rows), :].astype(f32) + jnp.where(ids == spot, extra_ref[pl.ds(number, 1), :], 0.0)) * keep
    grad_two = norm_rows_back(grad_out, unit, scale_inv, gain)
    grad_low = grad_two.astype(bf16)
    gf_ref[...] = grad_low
    if own:
        two_ref[...] = grad_two
        sums_ref[0:1, :] = jnp.sum(grad_low.astype(f32), axis=0, keepdims=True)
        sums_ref[1:2, :] = jnp.sum(grad_out * unit, axis=0, keepdims=True)
        sums_ref[2:3, :] = jnp.sum(grad_out, axis=0, keepdims=True)
        sums_ref[3:8, :] = jnp.zeros((5, sums_ref.shape[1]), f32)
    mark_ref[...] = jnp.zeros_like(mark_ref)

    @pl.when((spot >= 0) & (spot < rows))
    def _():
        row, _ = norm_rows(y_ref[pl.ds(jnp.clip(spot, 0, rows - 1), 1), :])
        mark_ref[0:1, :] = row * gain + shift

    if blocks:
        move_columns(gf_ref, cols_ref, blocks)
    else:
        cols_ref[...] = gf_ref[...]
    copies.start(cols_ref, gf_full.at[there, :])
    for side, weight_ref in enumerate((down_ref, down2_ref)):

        @pl.loop(0, hidden // STRIP)
        def _(i):
            cols = strip(i + side * (hidden // STRIP))
            grad_act = dot_nt(gf_ref[...], weight_ref[strip(i), :])
            grad_pre = (grad_act * slope_ref[pl.ds(offset, rows), cols]).astype(bf16)
            gp_ref[:, cols] = grad_pre
            ub_ref[:, cols] = jnp.sum(grad_pre.astype(f32), axis=0, keepdims=True)

    copies.start(gp_ref, gp_full.at[there, :])

    @pl.loop(0, up_ref.shape[0] // STRIP)
    def _(i):
        cols = strip(i)
        part_ref[:, cols] = dot_nt(gp_ref[:, :hidden], up_ref[cols, :]) + dot_nt(gp_ref[:, hidden:], up2_ref[cols, :])

    copies.wait()


def back(own, blocks, offset, target, block, part, meta, y, out_grad, extra, vectors, slope, downs, ups, filled):
    rows, width = y.shape
    hidden = 2 * ups[0].shape[1]
    outputs = [shape(rows, width), shape(1, hidden), shape(8, width)]
    if own:
        outputs += [shape(rows, width), shape(8, width)]
    return whole(
        functools.partial(back_kernel, own, blocks, offset, target, not filled, block, part),
        "feed_back",
        [y, out_grad, extra, vectors, slope, *downs, *ups],
        outputs,
        scalars=meta,
        filled=filled
        or [shape(4 * rows, width), shape(4 * rows, width, bf16), shape(4 * rows, hidden, bf16)],
        scratch=[
            pltpu.VMEM((rows, width), bf16),
            pltpu.VMEM((rows, width), f32),
            pltpu.VMEM((rows, hidden), bf16),
            pltpu.VMEM((rows, width), bf16),
        ],
        sems=3,
    )


def context_back_kernel(blocks, own_ref, first_ref, sib_ref, near_w_ref, far_w_ref, far_ref, near_ref, sums_ref, *refs):
    low_ref = refs[-1]
    rows = own_ref.shape[0]
    low_ref[:rows, :] = own_ref[...]
    low_ref[rows:, :] = sib_ref[:rows, :].astype(bf16)
    wide = far_ref.shape[1]
    far_ref[: 2 * rows, :] = dot_nt(low_ref[...], far_w_ref[...])
    near_ref[...] = dot_nt(low_ref[...], near_w_ref[...]).astype(bf16)
    for k in range(first_ref.shape[1] // wide):
        cols = slice(k * wide, (k + 1) * wide)
        chip = first_ref[rows : rows + 8, cols] + sib_ref[rows : rows + 8, cols]
        sums_ref[8 * k : 8 * k + 8, :] = chip
        far_ref[2 * rows + 8 * k : 2 * rows + 8 * k + 8, :] = chip
    if blocks:
        move_columns(low_ref, refs[0], blocks)


def first_back_kernel(*refs):
    streams = (refs[:3], refs[3:6])
    chip_ref = refs[6]
    ub_refs = refs[7:11]
    marks = refs[11:15]
    unit_ref, inv_ref, vec_ref, first_ref, low_ref, ub_ref = refs[15:]
    hidden = ub_ref.shape[1]
    ub = ub_refs[0][...] + ub_refs[1][...] + ub_refs[2][...] + ub_refs[3][...]
    ub_ref[...] = ub[:, :hidden]
    gain = row_of(vec_ref, GAIN_ONE)
    size, width = streams[0][0].shape
    rows = 2 * size
    sums = [0.0] * 6
    for half, (two_ref, own_ref, ffn_ref) in enumerate(streams):
        here = pl.ds(half * size, size)
        grad_normed = two_ref[...] + own_ref[...]
        if half:
            grad_normed = grad_normed + chip_ref[...]
        unit = unit_ref[here, :]
        first = norm_rows_back(grad_normed, unit, inv_ref[here, 0:1], gain)
        low = first.astype(bf16)
        first_ref[here, :] = first
        low_ref[here, :] = low
        terms = [low.astype(f32), grad_normed * unit, grad_normed]
        for k in range(3):
            sums[k] = sums[k] + jnp.sum(terms[k], axis=0, keepdims=True)
            sums[k + 3] = sums[k + 3] + ffn_ref[k : k + 1, :]
    for k in range(6):
        first_ref[rows + k : rows + k + 1, :] = sums[k]
    first_ref[rows + 6 : rows + 8, :] = jnp.zeros((2, width), f32)
    first_ref[rows + 8 : rows + 9, :] = ub[:, hidden:]
    first_ref[rows + 9 : rows + 10, :] = marks[0][0:1, :] + marks[1][0:1, :]
    first_ref[rows + 10 : rows + 11, :] = marks[2][0:1, :] + marks[3][0:1, :]
    first_ref[rows + 11 : rows + 16, :] = jnp.zeros((5, width), f32)


def input_kernel(near_ref, far_ref, gk_ref, gv_ref, qw_ref, kw_ref, vw_ref, first_ref, mine_ref, away_ref):
    rows = near_ref.shape[0] // 2
    for p in range(4):
        gq_ref = (near_ref, far_ref)[p // 2]
        here = pl.ds(p * rows, rows)
        value = (
            dot_nt(gq_ref[pl.ds((p % 2) * rows, rows), :], qw_ref[...])
            + dot_nt(gk_ref[here, :], kw_ref[...])
            + dot_nt(gv_ref[here, :], vw_ref[...])
        )
        if p == 0:
            value = value + first_ref[:rows, :]
        (mine_ref, away_ref)[p % 2][pl.ds((p // 2) * rows, rows), :] = value


def chip_kernel(mine_ref, got_ref, keep_ref, send_ref):
    rows = mine_ref.shape[0] // 2
    step = 64

    @pl.loop(0, rows // step)
    def _(i):
        for p in range(2):
            here = strip(i + p * (rows // step), step)
            there = strip(i + (1 - p) * (rows // step), step)
            value = mine_ref[here, :] + got_ref[here, :]
            keep_ref[here, :] = value
            send_ref[there, :] = value


def place_kernel(meta_ref, mine_ref, other_ref, out_ref, sems):
    rows = mine_ref.shape[0] // 2
    copies = Copies(sems)
    for p, block in enumerate((0, 2, 1, 3)):
        ref = (mine_ref, other_ref)[p // 2]
        copies.start(ref.at[pl.ds((p % 2) * rows, rows), :], out_ref.at[strip(meta_ref[block], rows), :])
    copies.wait()


def round_place_kernel(meta_ref, near_ref, far_ref, out_ref, low_ref, sems):
    rows = near_ref.shape[0] // 2
    copies = Copies(sems)
    for p, block in enumerate((0, 2, 1, 3)):
        ref = (near_ref, far_ref)[p // 2]
        low_ref[p * rows : (p + 1) * rows, :] = ref[(p % 2) * rows : (p % 2 + 1) * rows, :].astype(bf16)
        copies.start(low_ref.at[pl.ds(p * rows, rows), :], out_ref.at[strip(meta_ref[block], rows), :])
    copies.wait()


def swap_core(value):
    return lax.ppermute(value, "mp", [(i, i ^ 1) for i in range(4)])


def swap_chip(value):
    return lax.ppermute(value, "mp", [(i, i ^ 2) for i in range(4)])


def gather_rows(own):
    other = swap_chip(own)
    sibling = swap_core(own)
    diagonal = swap_core(other)
    return own, sibling, other, diagonal


def bit_order_blocks(parts, order):
    bits = len(order)
    blocks = []
    for position in range(parts):
        block = 0
        for level, bit in enumerate(order):
            block |= ((position >> (bits - 1 - level)) & 1) << bit
        blocks.append(block)
    return blocks


def bit_order_columns(matrix, parts, order):
    width = matrix.shape[1] // parts
    return jnp.concatenate(
        [matrix[:, b * width : (b + 1) * width] for b in bit_order_blocks(parts, order)], axis=1
    )


def dp_swap(value, parts, bit):
    return lax.ppermute(value, "dp", [(i, i ^ (1 << bit)) for i in range(parts)])


class Sum:
    def __init__(self, parts, order, meta, line, spare=0):
        self.parts, self.order, self.meta, self.line = parts, list(order), meta, line
        self.spare = spare
        self.turned = False
        self.second = None
        self.extra = self.total = self.got = None

    def begin(self, away, total, extra=None):
        self.total, self.extra = total, extra
        self.level = 0
        self.ship(away)

    def ship(self, away):
        self.got = dp_swap(away, self.parts, self.order[self.level])
        self.level += 1

    def step(self):
        if self.got is None:
            return
        got = self.line.hold(self.got)
        self.got = None
        rows, cols = self.total.shape
        ends = self.level == len(self.order)
        riders = 0 if self.extra is None else self.extra.shape[0]
        bit = 0 if ends else self.order[self.level]
        rest = [shape(riders, cols)] if riders else []
        outputs = [shape(rows, cols)]
        if not ends:
            outputs = [shape(rows // 2 + riders + self.spare, cols), shape(rows // 2, cols)]
        if ends and self.turned and rows % 128 == 0:
            outputs = [shape(rows, cols // 2), shape(cols // 2, rows)]
        given = [self.total, got] + ([self.extra] if riders else [])
        result = whole(
            functools.partial(fold_kernel, riders, ends, bit), "fold", given, outputs + rest, scalars=self.meta
        )
        if riders:
            self.extra = result[-1]
        if ends:
            self.total = result[0]
            self.second = result[1] if len(outputs) == 2 else None
            self.line.mark(self.total)
        else:
            self.total = result[1]
            self.ship(result[0])
            self.line.mark(result[0])

    def finish(self):
        while self.got is not None:
            self.step()
        return self.total


class Line:
    def __init__(self):
        self.token = None

    def mark(self, *values):
        self.token = values

    def hold(self, *values):
        if self.token is not None:
            values = lax.optimization_barrier(tuple(values) + self.token)[: len(values)]
        return values if len(values) > 1 else values[0]


def shards(
    dp_size,
    tokens,
    doc_lengths,
    cls_pos,
    cls_count,
    q_weight,
    q_bias,
    k_weight,
    v_weight,
    v_bias,
    o_weight,
    o_bias,
    ln1_gain,
    ln1_bias,
    up_weight,
    up_bias,
    down_weight,
    down_bias,
    ln2_gain,
    ln2_bias,
    out_grad,
    pooled_grad,
):
    slot_len, width = tokens.shape
    rows = slot_len // 4
    half = 2 * rows
    head_width = q_weight.shape[1]
    rank = lax.axis_index("mp")
    place_id = lax.axis_index("dp")
    bits = dp_size.bit_length() - 1
    order_a = list(range(bits))
    order_b = [1, 0] + list(range(2, bits)) if bits > 1 else order_a
    length = doc_lengths[0]
    blocks = [rank ^ j for j in range(4)]

    line = Line()
    sizes = width // dp_size
    fixed_a = bit_order_blocks(dp_size, order_a) if sizes % 128 == 0 else None
    fixed_b = bit_order_blocks(dp_size, order_b) if sizes % 128 == 0 else None
    unit = rows // 2

    row_ids = lax.iota(jnp.int32, rows)
    positions = jnp.concatenate([row_ids + blocks[j] * rows for j in range(4)])
    bias = jnp.where(positions < length, 0.0, MASKED).astype(f32)[None, :]
    meta = jnp.concatenate(
        [
            jnp.stack(blocks).astype(jnp.int32),
            doc_lengths,
            cls_count,
            cls_pos[0],
            jnp.stack([(place_id >> bit) & 1 for bit in range(max(bits, 1))]).astype(jnp.int32),
        ]
    )
    hidden = up_bias.shape[0]

    meta, bias = lax.optimization_barrier((meta, bias))

    o_part, vectors = prepare(
        meta, o_weight, [o_bias, ln1_gain, ln1_bias, ln2_gain, ln2_bias, down_bias, up_bias]
    )
    o_got = swap_chip(o_part)
    line.mark(o_part)
    local, queries_near, queries_far, key_rows, value_rows = qkv(
        meta, line.hold(tokens), (q_weight, k_weight, v_weight), (q_bias, v_bias)
    )
    away_context, lse_far = attn_fwd(queries_far, key_rows, value_rows, bias, 256, f32)
    arrived = swap_chip(away_context)
    line.mark(away_context)
    o_got = line.hold(o_got)
    o_other = dp_swap(o_got, dp_size, 0)
    line.mark(o_got)
    up_held, down_held = line.hold(up_weight, down_weight)
    wide = whole(
        widen_kernel,
        "widen",
        [up_held, down_held, vectors],
        [shape(width + hidden + 8, width)],
        limit=20,
    )[0]
    line.mark(wide)
    wide = swap_core(wide)
    context_near, lse_near = attn_fwd(line.hold(queries_near), key_rows, value_rows, bias, 256, bf16)
    line.mark(context_near)
    if fixed_a:
        local_a, local_b = whole(
            functools.partial(order_kernel, fixed_a, fixed_b),
            "order",
            [line.hold(local)],
            [shape(slot_len, width, bf16)] * 2,
        )
    else:
        local_a = bit_order_columns(local, dp_size, order_a)
        local_b = bit_order_columns(local, dp_size, order_b)
    line.mark(local_a)
    own, sib, context_other, o_far = whole(
        project_kernel,
        "project",
        [context_near, line.hold(arrived), o_weight, o_got, line.hold(o_other)],
        [shape(rows, width), shape(rows, width), shape(half, head_width, bf16), shape(head_width, width, bf16)],
        scalars=meta,
    )
    n_a, n_b, normed, unit_one, inv_one = whole(
        first_norm_kernel,
        "first_norm",
        [own, swap_core(sib), local, vectors],
        [shape(unit, width), shape(unit, width), shape(rows, width), shape(rows, width), shape(rows, 128)],
    )
    line.mark(n_a)
    chip_a = swap_chip(n_a)
    chip_b = swap_chip(n_b)
    up_far, down_far, vectors_far = whole(
        round_kernel,
        "round",
        [line.hold(wide)],
        [shape(width, hidden, bf16), shape(hidden, width, bf16), shape(8, width)],
        limit=20,
    )
    ups = (up_weight, up_far)
    downs = (down_weight, down_far)
    both = (vectors, vectors_far)
    lo, act, slope_near, own_a, own_b = feed(True, unit, fixed_b, (0, 1), normed, ups, both, downs, ())
    line.mark(own_a)
    lo, act, slope_a, part = feed(
        False, unit, fixed_b, (2,), line.hold(chip_a), ups, both, downs, (lo, act)
    )
    got_a = swap_chip(part)
    line.mark(part)
    lo, act, slope_b, part = feed(
        False, unit, fixed_b, (3,), line.hold(chip_b), ups, both, downs, (lo, act)
    )
    got_b = swap_chip(part)
    line.mark(part)

    def back_rows(own, k, y, slope, offset, filled):
        place = k if own else 2 + k
        return back(
            own, fixed_a, offset, place, 0 if own else 2, k, meta, y, out_grad, pooled_grad[0], vectors,
            slope, downs, ups, filled,
        )

    y_a = add(own_a, line.hold(got_a))
    chip_a = swap_chip(y_a)
    *filled, back_a, ub_a, mark_a, two_a, sums_a = back_rows(True, 0, y_a, slope_near, 0, ())
    line.mark(back_a)
    y_b = add(own_b, line.hold(got_b))
    chip_b = swap_chip(y_b)
    *filled, back_b, ub_b, mark_b, two_b, sums_b = back_rows(True, 1, y_b, slope_near, unit, filled)
    line.mark(back_b)
    *filled, part, ub_c, mark_c = back_rows(False, 0, line.hold(chip_a), slope_a, 0, filled)
    got_a = swap_chip(part)
    line.mark(part)
    *filled, part, ub_d, mark_d = back_rows(False, 1, line.hold(chip_b), slope_b, 0, filled)
    got_b = swap_chip(part)
    line.mark(part)
    back_a = add(back_a, line.hold(got_a))
    line.mark(back_a)
    out_wide, grad_fed, grad_pre = filled

    def in_order(value, fixed, order):
        return value if fixed else bit_order_columns(value, dp_size, order)

    gf_cols, lo_cols = in_order(grad_fed, fixed_a, order_a), in_order(lo, fixed_b, order_b)
    down_sum = Sum(dp_size, order_a, meta, line, 0)
    up_sum = Sum(dp_size, order_b, meta, line, 0)

    def pair(side, sum_of, left, right, given=()):
        half_rows = width // 2
        return whole(
            functools.partial(pair_kernel, side, bool(given), sum_of.order[0]),
            "pair",
            [left, right, *given],
            [shape(half_rows, hidden)] * 2 if given else [shape(width, hidden)],
            scalars=meta,
        )

    down_other = pair(1, down_sum, line.hold(gf_cols), act)[0]
    down_given = swap_core(down_other)
    line.mark(down_other)
    up_other = pair(1, up_sum, lo_cols, line.hold(grad_pre))[0]
    up_given = swap_core(up_other)
    line.mark(up_other)

    down_sum.begin(*pair(0, down_sum, gf_cols, act, [line.hold(down_given)]))
    up_sum.begin(*pair(0, up_sum, lo_cols, grad_pre, [line.hold(up_given)]))

    line.mark(down_sum.total, up_sum.total)
    got_b = line.hold(got_b)
    first_ext, grad_attended_own, up_bias_own = whole(
        first_back_kernel,
        "first_norm_back",
        [two_a, back_a, sums_a, two_b, back_b, sums_b, got_b, ub_a, ub_b, ub_c, ub_d]
        + [mark_a, mark_b, mark_c, mark_d, unit_one, inv_one, vectors],
        [shape(rows + 16, width), shape(rows, width, bf16), shape(1, hidden)],
    )
    sib_ext = swap_core(first_ext)
    riders = 8 * width // head_width
    context_far_grad, grad_context_near, chip_sums, *ga_cols = whole(
        functools.partial(context_back_kernel, fixed_b),
        "context_back",
        [grad_attended_own, first_ext, sib_ext, o_weight, o_far],
        [shape(half + riders, head_width), shape(half, head_width, bf16), shape(riders, head_width)]
        + [shape(half, width, bf16)] * (2 if fixed_b else 1),
    )
    ga_cols = in_order(ga_cols[0], fixed_b, order_b)
    grad_context_far = swap_chip(context_far_grad)
    line.mark(context_far_grad)
    *o_away, o_kept = whole(
        o_kernel,
        "o_grad",
        [line.hold(ga_cols), context_other, context_near],
        [shape(width // 2, head_width)] * 2 + [shape(width, head_width)],
    )
    o_got = [swap_chip(v) for v in o_away]
    line.mark(o_kept)

    queries_near = line.hold(queries_near)
    grad_q_near, key_sum, value_sum = attn_bwd(
        queries_near, grad_context_near, key_rows, value_rows, bias, lse_near, 256
    )
    line.mark(grad_q_near)
    grad_context_far = line.hold(grad_context_far)
    line.mark(grad_context_far)
    queries_far = line.hold(queries_far)
    grad_q_far, grad_k, grad_v = attn_bwd(
        queries_far, grad_context_far, key_rows, value_rows, bias, lse_far, 256, (key_sum, value_sum)
    )
    line.mark(grad_k)

    qk_sum = Sum(dp_size, order_a, meta, line)
    vo_sum = Sum(dp_size, order_b, meta, line)
    vo_sum.turned = True
    riders = 8 * width // head_width
    extra_rows = -(-(riders // 2 + 1 + hidden // (2 * head_width)) // 8) * 8
    qk_away, qk_kept, qk_extra = whole(
        functools.partial(qk_kernel, qk_sum.order[0]),
        "qk_grad",
        [local_a, line.hold(grad_q_near), grad_q_far, grad_k, grad_v, chip_sums, grad_context_far]
        + [up_bias_own, sib_ext],
        [
            shape(width // 2 + extra_rows, 2 * head_width),
            shape(width // 2, 2 * head_width),
            shape(extra_rows, 2 * head_width),
        ],
        scalars=meta,
    )
    line.mark(qk_away)
    o_got = line.hold(*o_got)
    line.mark(*o_got)
    down_sum.step()
    up_sum.step()
    in_mine, in_away = whole(
        input_kernel,
        "input_grad",
        [line.hold(grad_q_near), grad_q_far, grad_k, grad_v, q_weight, k_weight, v_weight, first_ext],
        [shape(half, width)] * 2,
    )
    in_got = swap_core(in_away)
    out_far = swap_core(line.hold(out_wide))
    line.mark(in_mine)
    in_kept, in_sent = whole(
        chip_kernel, "chip_sum", [in_mine, line.hold(in_got)], [shape(half, width)] * 2
    )
    in_got = swap_chip(in_sent)
    line.mark(in_sent)
    out = whole(
        round_place_kernel,
        "round_place",
        [out_wide, line.hold(out_far)],
        [],
        scalars=meta,
        filled=[shape(slot_len, width, bf16)],
        scratch=[pltpu.VMEM((slot_len, width), bf16)],
        sems=4,
        far=True,
    )[0]
    line.mark(out)
    vo_away, vo_kept = whole(
        functools.partial(vo_kernel, vo_sum.order[0]),
        "vo_grad",
        [local_b, line.hold(grad_v), o_kept, *o_got],
        [shape(width // 2, 2 * head_width)] * 2,
        scalars=meta,
    )
    line.mark(vo_away)
    down_sum.step()
    up_sum.step()
    qk_sum.begin(line.hold(qk_away), qk_kept, qk_extra)
    vo_sum.begin(line.hold(vo_away), vo_kept)
    for bit in range(bits):
        qk_sum.step()
        if bit == 0:
            down_sum.step()
            up_sum.step()
        vo_sum.step()
        if bit > 1:
            down_sum.step()
            up_sum.step()
        if bit == min(1, bits - 1):
            in_final = add(in_kept, line.hold(in_got))
            in_other = swap_core(in_final)
            line.mark(in_final)
            in_grad = whole(
                place_kernel,
                "place",
                [in_final, line.hold(in_other)],
                [],
                scalars=meta,
                filled=[shape(slot_len, width)],
                sems=4,
                far=True,
            )[0]
            line.mark(in_grad)
    qk_total, vo_total = qk_sum.finish(), vo_sum.finish()
    riding = qk_sum.extra
    row = riders // 2
    shared = jnp.concatenate([riding[:row, :head_width], riding[:row, head_width:]], axis=0)
    shared = shared.reshape(-1, 8, head_width).transpose(1, 0, 2).reshape(8, width)
    biases = riding[row].reshape(2, head_width)
    up_bias_sum = riding[row + 1 : row + 1 + hidden // (2 * head_width)].reshape(-1)
    if vo_sum.second is None:
        v_sum, o_sum = vo_total[:, :head_width], vo_total[:, head_width:].T
    else:
        v_sum, o_sum = vo_total, vo_sum.second
    down_sum = down_sum.finish().T
    up_sum = up_sum.finish()

    mine = first_ext[rows + 9 : rows + 11]
    theirs = sib_ext[rows + 9 : rows + 11]
    marks = jnp.concatenate([mine[:1], theirs[:1], mine[1:], theirs[1:]], axis=0)
    pooled = jnp.concatenate(
        [lax.dynamic_index_in_dim(marks, blocks[j], keepdims=True) for j in range(4)], axis=0
    )[None]
    return (
        out,
        pooled,
        in_grad,
        qk_total[:, :head_width],
        biases[0],
        qk_total[:, head_width:],
        v_sum,
        biases[1],
        o_sum,
        shared[0],
        shared[1],
        shared[2],
        up_sum,
        up_bias_sum,
        down_sum,
        shared[3],
        shared[4],
        shared[5],
    )


def solution(mesh):
    return jax.shard_map(
        functools.partial(shards, mesh.shape["dp"]),
        mesh=mesh,
        in_specs=(
            P("dp", None),
            P("dp"),
            P("dp", None),
            P("dp"),
            P(None, "mp"),
            P("mp"),
            P(None, "mp"),
            P(None, "mp"),
            P("mp"),
            P("mp", None),
            P(),
            P(),
            P(),
            P(None, "mp"),
            P("mp"),
            P("mp", None),
            P(),
            P(),
            P(),
            P("dp", None),
            P("dp", None, None),
        ),
        out_specs=(
            P("dp", None),
            P("dp", None, None),
            P("dp", None),
            P("dp", "mp"),
            P("mp"),
            P("dp", "mp"),
            P("dp", "mp"),
            P("mp"),
            P("mp", "dp"),
            P(),
            P(),
            P(),
            P("dp", "mp"),
            P("mp"),
            P("mp", "dp"),
            P(),
            P(),
            P(),
        ),
        check_vma=False,
    )
```

```python
import functools

import jax
import jax.numpy as jnp
from jax import lax
from jax.experimental import pallas as pl
from jax.experimental.pallas import tpu as pltpu
from jax.sharding import PartitionSpec as P

HEAD_DIM = 64
NORM_EPS = 1e-05
ROOT_HALF = 0.7071067811865476
INV_ROOT_TAU = 0.3989422804014327
LOG2E = 1.4426950408889634
SCORE_SCALE = 0.125 * LOG2E
MASKED = -1e30

f32 = jnp.float32
bf16 = jnp.bfloat16
VMEM_LIMIT = 20 * 1024 * 1024


def dot_nn(a, b):
    return lax.dot_general(a, b, (((1,), (0,)), ((), ())), preferred_element_type=f32)


def dot_nt(a, b):
    return lax.dot_general(a, b, (((1,), (1,)), ((), ())), preferred_element_type=f32)


def dot_tn(a, b):
    return lax.dot_general(a, b, (((0,), (0,)), ((), ())), preferred_element_type=f32)


def attn_fwd_kernel(q_ref, k_ref, v_ref, bias_ref, o_ref, lse_ref):
    rows, width = q_ref.shape
    heads = width // HEAD_DIM
    lane = lax.broadcasted_iota(jnp.int32, (1, width), 1) // HEAD_DIM
    lse_lane = lax.broadcasted_iota(jnp.int32, (1, 128), 1)
    q = q_ref[...]
    k = k_ref[...]
    v = v_ref[...]
    bias = bias_ref[...]
    out = jnp.zeros((rows, width), f32)
    lse = jnp.zeros((rows, 128), f32)
    for h in range(heads):
        qh = jnp.where(lane == h, q, jnp.zeros_like(q))
        s = dot_nt(qh, k) * SCORE_SCALE + bias
        top = jnp.max(s, axis=1, keepdims=True)
        e = jnp.exp2(s - top)
        total = jnp.sum(e, axis=1, keepdims=True)
        p = (e * (1.0 / total)).astype(bf16)
        c = dot_nn(p, v)
        out = jnp.where(lane == h, c, out)
        lse = jnp.where(lse_lane == h, top + jnp.log2(total), lse)
    o_ref[...] = out.astype(o_ref.dtype)
    lse_ref[...] = lse


def attn_fwd(q, k, v, bias, block, dtype):
    rows, width = q.shape
    keys = k.shape[0]
    full = pl.BlockSpec((keys, width), lambda i: (0, 0))
    return pl.pallas_call(
        attn_fwd_kernel,
        grid=(rows // block,),
        in_specs=[
            pl.BlockSpec((block, width), lambda i: (i, 0)),
            full,
            full,
            pl.BlockSpec((1, keys), lambda i: (0, 0)),
        ],
        out_specs=[
            pl.BlockSpec((block, width), lambda i: (i, 0)),
            pl.BlockSpec((block, 128), lambda i: (i, 0)),
        ],
        out_shape=[
            jax.ShapeDtypeStruct((rows, width), dtype),
            jax.ShapeDtypeStruct((rows, 128), f32),
        ],
        compiler_params=pltpu.CompilerParams(vmem_limit_bytes=VMEM_LIMIT),
        cost_estimate=pl.CostEstimate(flops=1024, bytes_accessed=1024, transcendentals=0),
        name="attn_fwd",
    )(q, k, v, bias)


def attn_bwd_kernel(carried, *refs):
    q_ref, g_ref, k_ref, v_ref, bias_ref, lse_ref = refs[:6]
    refs = refs[6:]
    if carried:
        gk_in, gv_in = refs[:2]
        refs = refs[2:]
    gq_ref, gk_ref, gv_ref, gk_acc, gv_acc, gq_acc = refs
    step = pl.program_id(0)
    width = q_ref.shape[1]
    lane = lax.broadcasted_iota(jnp.int32, (1, width), 1) // HEAD_DIM
    lse_lane = lax.broadcasted_iota(jnp.int32, (1, 128), 1)

    @pl.when(step == 0)
    def _():
        gk_acc[...] = gk_in[...] if carried else jnp.zeros_like(gk_acc)
        gv_acc[...] = gv_in[...] if carried else jnp.zeros_like(gv_acc)

    @pl.loop(0, width // HEAD_DIM)
    def _(h):
        mine = lane == h
        zero = jnp.zeros(q_ref.shape, bf16)
        qh = jnp.where(mine, q_ref[...], zero)
        gh = jnp.where(mine, g_ref[...].astype(bf16), zero)
        lse = jnp.sum(jnp.where(lse_lane == h, lse_ref[...], 0.0), axis=1, keepdims=True)
        s = dot_nt(qh, k_ref[...]) * SCORE_SCALE + bias_ref[...]
        p = jnp.exp2(s - lse)
        dp = dot_nt(gh, v_ref[...])
        inner = jnp.sum(p * dp, axis=1, keepdims=True)
        ds = (p * (dp - inner)).astype(bf16)
        gq_acc[...] = jnp.where(mine, dot_nn(ds, k_ref[...]), gq_acc[...])
        gk_acc[...] += dot_tn(ds, qh)
        gv_acc[...] += dot_tn(p.astype(bf16), gh)

    gq_ref[...] = (gq_acc[...] * 0.125).astype(bf16)

    @pl.when(step == pl.num_programs(0) - 1)
    def _():
        scale = 0.125 if carried else 1.0
        gk_ref[...] = (gk_acc[...] * scale).astype(gk_ref.dtype)
        gv_ref[...] = gv_acc[...].astype(gv_ref.dtype)


def attn_bwd(q, g, k, v, bias, lse, block, sums=()):
    rows, width = q.shape
    keys = k.shape[0]
    full = pl.BlockSpec((keys, width), lambda i: (0, 0))
    part = pl.BlockSpec((block, width), lambda i: (i, 0))
    sum_type = bf16 if sums else f32
    return pl.pallas_call(
        functools.partial(attn_bwd_kernel, bool(sums)),
        grid=(rows // block,),
        in_specs=[
            part,
            part,
            full,
            full,
            pl.BlockSpec((1, keys), lambda i: (0, 0)),
            pl.BlockSpec((block, 128), lambda i: (i, 0)),
        ]
        + [full] * len(sums),
        out_specs=[part, full, full],
        out_shape=[
            jax.ShapeDtypeStruct((rows, width), bf16),
            jax.ShapeDtypeStruct((keys, width), sum_type),
            jax.ShapeDtypeStruct((keys, width), sum_type),
        ],
        scratch_shapes=[pltpu.VMEM((keys, width), f32)] * 2 + [pltpu.VMEM((block, width), f32)],
        compiler_params=pltpu.CompilerParams(vmem_limit_bytes=VMEM_LIMIT),
        cost_estimate=pl.CostEstimate(flops=1024, bytes_accessed=1024, transcendentals=0),
        name="attn_bwd",
    )(q, g, k, v, bias, lse, *sums)


in_vmem = pl.BlockSpec(memory_space=pltpu.VMEM)
STRIP = 256
LENGTH, COUNT, MARKS, BITS = 4, 5, 6, 10
O_BIAS, GAIN_ONE, SHIFT_ONE, GAIN_TWO, SHIFT_TWO, DOWN_BIAS, UP_BIAS, QV_BIAS = range(8)


def row_of(ref, index):
    return ref[index : index + 1, :]


def strip(index, size=STRIP):
    return pl.ds(pl.multiple_of(index * size, size), size)


def shape(rows, cols, dtype=f32):
    return jax.ShapeDtypeStruct((rows, cols), dtype)


def whole(kernel, name, inputs, outputs, scalars=None, filled=(), sems=0, scratch=(), limit=8, far=False):
    lead = [] if scalars is None else [scalars]
    anywhere = pl.BlockSpec(memory_space=pl.ANY)
    given = [v for v in filled if not isinstance(v, jax.ShapeDtypeStruct)]
    begun = [jax.ShapeDtypeStruct(v.shape, v.dtype) for v in filled]
    first = len(lead) + len(inputs)
    return pl.pallas_call(
        kernel,
        in_specs=[pl.BlockSpec(memory_space=pltpu.SMEM)] * len(lead)
        + [in_vmem] * len(inputs)
        + [anywhere] * len(given),
        out_specs=[pl.BlockSpec(memory_space=pltpu.HBM) if far else anywhere] * len(begun)
        + [in_vmem] * len(outputs),
        out_shape=begun + list(outputs),
        scratch_shapes=list(scratch) + ([pltpu.SemaphoreType.DMA((sems,))] if sems else []),
        input_output_aliases={first + p: p for p in range(len(given))},
        compiler_params=pltpu.CompilerParams(vmem_limit_bytes=limit * 1024 * 1024),
        cost_estimate=pl.CostEstimate(flops=1024, bytes_accessed=1024, transcendentals=0),
        name=name,
    )(*lead, *inputs, *given)


class Copies:
    def __init__(self, sems):
        self.sems, self.made = sems, []

    def start(self, source, target):
        copy = pltpu.make_async_copy(source, target, self.sems.at[len(self.made)])
        copy.start()
        self.made.append(copy)

    def wait(self):
        for copy in self.made:
            copy.wait()


def project_kernel(meta_ref, near_ref, other_ref, o_near_ref, o_got_ref, o_other_ref, own_ref, sib_ref, low_ref, o_far_ref):
    rows = own_ref.shape[0]
    part = o_got_ref.shape[0]
    first = meta_ref[BITS] == 0
    o_far_ref[:part, :] = jnp.where(first, o_got_ref[...], o_other_ref[...]).astype(bf16)
    o_far_ref[part:, :] = jnp.where(first, o_other_ref[...], o_got_ref[...]).astype(bf16)
    low_ref[...] = other_ref[...].astype(bf16)
    both = dot_nn(near_ref[...], o_near_ref[...]) + dot_nn(low_ref[...], o_far_ref[...])
    own_ref[...] = both[:rows]
    sib_ref[...] = both[rows:]


def mean_of(values):
    return jnp.sum(values, axis=-1, keepdims=True) * (1.0 / values.shape[-1])


def norm_rows(values):
    centre = values - mean_of(values)
    scale_inv = lax.rsqrt(mean_of(centre * centre) + NORM_EPS)
    return centre * scale_inv, scale_inv


def norm_rows_back(grad_rows, unit_rows, scale_inv, gain):
    scaled = grad_rows * gain
    return scale_inv * (scaled - mean_of(scaled) - unit_rows * mean_of(scaled * unit_rows))


def first_norm_kernel(own_ref, near_ref, tok_ref, vec_ref, na_ref, nb_ref, all_ref, unit_ref, inv_ref):
    gain = row_of(vec_ref, GAIN_ONE)
    shift = row_of(vec_ref, SHIFT_ONE)
    for half, out_ref in enumerate((na_ref, nb_ref)):
        size = out_ref.shape[0]
        rows = pl.ds(half * size, size)
        values = tok_ref[rows, :].astype(f32) + (own_ref[rows, :] + near_ref[rows, :] + row_of(vec_ref, O_BIAS))
        unit, scale_inv = norm_rows(values)
        unit_ref[rows, :] = unit
        inv_ref[rows, :] = jnp.broadcast_to(scale_inv, (size, inv_ref.shape[1]))
        normed = unit * gain + shift
        out_ref[...] = normed
        all_ref[rows, :] = normed


def move_columns(source, target, blocks):
    wide = source.shape[1] // len(blocks)
    for place, block in enumerate(blocks):
        target[:, place * wide : (place + 1) * wide] = source[:, block * wide : (block + 1) * wide]


def order_kernel(blocks_a, blocks_b, in_ref, a_ref, b_ref):
    move_columns(in_ref, a_ref, blocks_a)
    move_columns(in_ref, b_ref, blocks_b)


def prepare_kernel(meta_ref, o_ref, *refs):
    given = refs[:7]
    part_ref, vec_ref, o_in = refs[7:10]
    lines = refs[10:17]
    sems = refs[17]
    copies = Copies(sems)
    copies.start(o_ref.at[strip(meta_ref[BITS], part_ref.shape[0]), :], o_in)
    for line_ref, vector_ref in zip(lines, given):
        copies.start(vector_ref, line_ref)
    copies.wait()
    part_ref[...] = o_in[...].astype(f32)
    vec_ref[...] = jnp.zeros_like(vec_ref)
    for k, line_ref in enumerate(lines):
        vec_ref[k, :] = line_ref[...].astype(f32)


def prepare(meta, o_weight, vectors):
    rows, width = o_weight.shape
    far = pl.BlockSpec(memory_space=pltpu.HBM)
    return pl.pallas_call(
        prepare_kernel,
        in_specs=[pl.BlockSpec(memory_space=pltpu.SMEM)] + [far] * 8,
        out_specs=[in_vmem] * 2,
        out_shape=[shape(rows // 2, width), shape(8, width)],
        scratch_shapes=[pltpu.VMEM((rows // 2, width), bf16)]
        + [pltpu.VMEM((width,), bf16)] * 7
        + [pltpu.SemaphoreType.DMA((8,))],
        compiler_params=pltpu.CompilerParams(vmem_limit_bytes=60 * 1024 * 1024),
        cost_estimate=pl.CostEstimate(flops=1024, bytes_accessed=1024, transcendentals=0),
        name="prepare",
    )(meta, o_weight, *vectors)


def widen_kernel(a_ref, b_ref, vec_ref, wide_ref):
    rows = a_ref.shape[0]
    step = 64

    @pl.loop(0, rows // step)
    def _(i):
        wide_ref[strip(i, step), :] = a_ref[strip(i, step), :].astype(f32)

    @pl.loop(0, b_ref.shape[0] // step)
    def _(i):
        wide_ref[strip(i + rows // step, step), :] = b_ref[strip(i, step), :].astype(f32)

    wide_ref[rows + b_ref.shape[0] :, :] = vec_ref[...]


def qkv_kernel(meta_ref, all_ref, qw_ref, kw_ref, vw_ref, *refs):
    given = refs[:2]
    vec_ref, local_ref, near_ref, far_ref, k_ref, v_ref, q_in, k_in, v_in, qb_in, vb_in, sems = refs[2:]
    half, wide = near_ref.shape
    rows = half // 2
    copies = Copies(sems)
    copies.start(given[0], qb_in)
    copies.start(given[1], vb_in)
    for p in range(4):
        copies.start(all_ref.at[strip(meta_ref[p], rows), :], local_ref.at[pl.ds(p * rows, rows), :])
    copies.start(kw_ref, k_in)
    copies.start(qw_ref, q_in)
    copies.start(vw_ref, v_in)
    copies.wait()
    k_ref[...] = dot_nn(local_ref[...], k_in[...]).astype(bf16)
    vec_ref[0, :] = qb_in[...].astype(f32)
    vec_ref[1, :] = vb_in[...].astype(f32)
    q = (dot_nn(local_ref[...], q_in[...]) + vec_ref[0:1, :]).astype(bf16)
    near_ref[...] = q[:half]
    far_ref[...] = q[half:]
    v_ref[...] = (dot_nn(local_ref[...], v_in[...]) + vec_ref[1:2, :]).astype(bf16)


def qkv(meta, tokens, weights, biases):
    rows, width = tokens.shape
    wide = weights[0].shape[1]
    far = pl.BlockSpec(memory_space=pltpu.HBM)
    return pl.pallas_call(
        qkv_kernel,
        in_specs=[pl.BlockSpec(memory_space=pltpu.SMEM)] + [far] * 6,
        out_specs=[in_vmem] * 6,
        out_shape=[shape(8, wide), shape(rows, width, bf16)]
        + [shape(rows // 2, wide, bf16)] * 2
        + [shape(rows, wide, bf16)] * 2,
        scratch_shapes=[pltpu.VMEM((width, wide), bf16)] * 3
        + [pltpu.VMEM((wide,), bf16)] * 2
        + [pltpu.SemaphoreType.DMA((9,))],
        compiler_params=pltpu.CompilerParams(vmem_limit_bytes=58 * 1024 * 1024),
        cost_estimate=pl.CostEstimate(flops=1024, bytes_accessed=1024, transcendentals=0),
        name="qkv",
    )(meta, tokens, *weights, *biases)[1:]


def add_kernel(*refs):
    step = 64

    @pl.loop(0, refs[0].shape[0] // step)
    def _(i):
        here = strip(i, step)
        total = refs[0][here, :]
        for ref in refs[1:-1]:
            total = total + ref[here, :]
        refs[-1][here, :] = total


def add(*values):
    return whole(add_kernel, "add", list(values), [shape(*values[0].shape)])[0]


def pair_kernel(side, fill, bit, meta_ref, left_ref, right_ref, *refs):
    mine = meta_ref[BITS + bit]
    half = left_ref.shape[1] // 2
    hidden = right_ref.shape[1] // 2
    right = right_ref[:, side * hidden : (side + 1) * hidden]
    for kept in range(2):
        start = pl.multiple_of((mine if kept else 1 - mine) * half, 128)
        value = dot_tn(left_ref[:, pl.ds(start, half)], right)
        if fill:
            refs[1 + kept][...] = value + refs[0][kept * half : (kept + 1) * half, :]
        else:
            refs[0][kept * half : (kept + 1) * half, :] = value


def fold_kernel(riders, ends, bit, meta_ref, total_ref, got_ref, *refs):
    rows = total_ref.shape[0]
    if riders:
        extra_ref = refs[0]
        refs = refs[1:]
        extra = extra_ref[...] + got_ref[rows:, :]
    if ends and len(refs) == 2 and not riders:
        wide = total_ref.shape[1] // 2
        refs[0][...] = total_ref[:, :wide] + got_ref[:rows, :wide]
        refs[1][...] = (total_ref[:, wide:] + got_ref[:rows, wide:]).T
        return
    if ends:
        refs[0][...] = total_ref[...] + got_ref[:rows, :]
        if riders:
            refs[1][...] = extra
        return
    half = rows // 2
    mine = meta_ref[BITS + bit]
    step = min(64, half)

    @pl.loop(0, half // step)
    def _(i):
        away = strip((1 - mine) * (half // step) + i, step)
        kept = strip(mine * (half // step) + i, step)
        refs[0][strip(i, step), :] = total_ref[away, :] + got_ref[away, :]
        refs[1][strip(i, step), :] = total_ref[kept, :] + got_ref[kept, :]

    if riders:
        refs[0][half:, :] = extra
        refs[2][...] = extra
    elif refs[0].shape[0] > half:
        refs[0][half:, :] = jnp.zeros((refs[0].shape[0] - half, refs[0].shape[1]), f32)


def qk_kernel(bit, meta_ref, left_ref, near_ref, far_ref, gk_ref, gv_ref, chip_ref, far_sums_ref, ub_ref, sib_ref, away_ref, kept_ref, extra_ref):
    mine = meta_ref[BITS + bit]
    half = left_ref.shape[1] // 2
    rows = near_ref.shape[0]
    wide = near_ref.shape[1]
    riders = chip_ref.shape[0]
    extra_ref[...] = jnp.zeros_like(extra_ref)
    shared = chip_ref[...] + far_sums_ref[far_sums_ref.shape[0] - riders :, :]
    extra_ref[: riders // 2, :wide] = shared[: riders // 2]
    extra_ref[: riders // 2, wide:] = shared[riders // 2 :]
    row = riders // 2
    query_sum = jnp.sum(near_ref[...].astype(f32), axis=0, keepdims=True)
    extra_ref[row : row + 1, :wide] = query_sum + jnp.sum(far_ref[...].astype(f32), axis=0, keepdims=True)
    extra_ref[row : row + 1, wide:] = jnp.sum(gv_ref[...].astype(f32), axis=0, keepdims=True)
    place = sib_ref.shape[0] - 8
    for k in range(ub_ref.shape[1] // (2 * wide)):
        cols = slice(2 * k * wide, 2 * (k + 1) * wide)
        extra_ref[row + 1 + k : row + 2 + k, :] = ub_ref[:, cols] + sib_ref[place : place + 1, cols]
    for kept, ref in enumerate((away_ref, kept_ref)):
        cols = pl.ds(pl.multiple_of((mine if kept else 1 - mine) * half, 128), half)
        ref[:half, :wide] = dot_tn(left_ref[:rows, cols], near_ref[...]) + dot_tn(left_ref[rows:, cols], far_ref[...])
        ref[:half, wide:] = dot_tn(left_ref[:, cols], gk_ref[...])
    away_ref[half:, :] = extra_ref[...]


def vo_kernel(bit, meta_ref, left_ref, gv_ref, kept_o_ref, got_a_ref, got_b_ref, away_ref, kept_ref):
    mine = meta_ref[BITS + bit]
    half = left_ref.shape[1] // 2
    wide = gv_ref.shape[1]
    for kept, ref in enumerate((away_ref, kept_ref)):
        start = pl.multiple_of((mine if kept else 1 - mine) * half, 128)
        ref[:, :wide] = dot_tn(left_ref[:, pl.ds(start, half)], gv_ref[...])
        rows = pl.ds(start, half)
        top = jnp.where(start == 0, got_a_ref[...], got_b_ref[...])
        ref[:, wide:] = kept_o_ref[rows, :] + top


def o_kernel(cols_ref, other_ref, near_ref, first_ref, second_ref, kept_ref):
    half = first_ref.shape[0]
    first_ref[...] = dot_tn(cols_ref[:, :half], other_ref[...])
    second_ref[...] = dot_tn(cols_ref[:, half:], other_ref[...])
    kept_ref[...] = dot_tn(cols_ref[...], near_ref[...])


def round_kernel(wide_ref, a_ref, b_ref, vec_ref):
    rows = a_ref.shape[0]
    step = 64

    @pl.loop(0, rows // step)
    def _(i):
        a_ref[strip(i, step), :] = wide_ref[strip(i, step), :].astype(bf16)

    @pl.loop(0, b_ref.shape[0] // step)
    def _(i):
        b_ref[strip(i, step), :] = wide_ref[strip(i + rows // step, step), :].astype(bf16)

    vec_ref[...] = wide_ref[rows + b_ref.shape[0] :, :]


def feed_kernel(own, unit, blocks, targets, fresh, *refs):
    in_ref, up_ref, up2_ref, vec_ref, vec2_ref, down_ref, down2_ref = refs[:7]
    refs = refs[7 + (0 if fresh else 2) :]
    lo_full, act_full, slope_ref = refs[:3]
    parts = refs[3:-4]
    low_ref, act_ref, cols_ref, sems = refs[-4:]
    hidden = up_ref.shape[1]
    copies = Copies(sems)
    low_ref[...] = in_ref[...].astype(bf16)
    if blocks:
        move_columns(low_ref, cols_ref, blocks)
    else:
        cols_ref[...] = low_ref[...]
    for p, target in enumerate(targets):
        copies.start(cols_ref.at[pl.ds(p * unit, unit), :], lo_full.at[pl.ds(target * unit, unit), :])
    for side, (weight_ref, bias_ref) in enumerate(((up_ref, vec_ref), (up2_ref, vec2_ref))):

        @pl.loop(0, hidden // STRIP)
        def _(i):
            there = strip(i + side * (hidden // STRIP))
            pre = dot_nn(low_ref[...], weight_ref[:, strip(i)]) + bias_ref[UP_BIAS : UP_BIAS + 1, strip(i)]
            normal_cdf = 0.5 * (1.0 + lax.erf(pre * ROOT_HALF))
            density = jnp.exp(-0.5 * pre * pre) * INV_ROOT_TAU
            act_ref[:, there] = (pre * normal_cdf).astype(bf16)
            slope_ref[:, there] = normal_cdf + pre * density

    for p, target in enumerate(targets):
        copies.start(act_ref.at[pl.ds(p * unit, unit), :], act_full.at[pl.ds(target * unit, unit), :])

    @pl.loop(0, down_ref.shape[1] // STRIP)
    def _(i):
        cols = strip(i)
        part = dot_nn(act_ref[:, :hidden], down_ref[:, cols]) + dot_nn(act_ref[:, hidden:], down2_ref[:, cols])
        if own:
            part = part + (in_ref[:, cols] + vec_ref[DOWN_BIAS : DOWN_BIAS + 1, cols])
        for p, part_ref in enumerate(parts):
            part_ref[:, cols] = part[p * unit : (p + 1) * unit]

    copies.wait()


def feed(own, unit, blocks, targets, rows_in, ups, vectors, downs, filled):
    rows, width = rows_in.shape
    hidden = 2 * ups[0].shape[1]
    return whole(
        functools.partial(feed_kernel, own, unit, blocks, targets, not filled),
        "feed",
        [rows_in, *ups, *vectors, *downs],
        [shape(rows, hidden)] + [shape(unit, width)] * len(targets),
        filled=filled or [shape(4 * unit, width, bf16), shape(4 * unit, hidden, bf16)],
        scratch=[
            pltpu.VMEM((rows, width), bf16),
            pltpu.VMEM((rows, hidden), bf16),
            pltpu.VMEM((rows, width), bf16),
        ],
        sems=2 * len(targets),
    )


def back_kernel(own, blocks, offset, target, fresh, block, part, meta_ref, y_ref, og_ref, extra_ref, vec_ref, slope_ref, down_ref, down2_ref, up_ref, up2_ref, *refs):
    refs = refs[0 if fresh else 3 :]
    out_full, gf_full, gp_full, part_ref, ub_ref, mark_ref = refs[:6]
    refs = refs[6:]
    if own:
        two_ref, sums_ref = refs[:2]
        refs = refs[2:]
    gf_ref, out_ref, gp_ref, cols_ref, sems = refs
    rows = y_ref.shape[0]
    hidden = up_ref.shape[1]
    gain = row_of(vec_ref, GAIN_TWO)
    shift = row_of(vec_ref, SHIFT_TWO)
    copies = Copies(sems)
    ids = lax.broadcasted_iota(jnp.int32, (rows, 1), 0)
    number = meta_ref[block]
    base = pl.multiple_of((2 * number + part) * rows, rows)
    limit = meta_ref[LENGTH] - base
    spot = jnp.where(number < meta_ref[COUNT], meta_ref[MARKS + number] - base, -1)
    there = pl.ds(target * rows, rows)
    keep = (ids < limit).astype(f32)
    unit, scale_inv = norm_rows(y_ref[...])
    out_ref[...] = (unit * gain + shift) * keep
    copies.start(out_ref, out_full.at[there, :])
    grad_out = (og_ref[pl.ds(base, rows), :].astype(f32) + jnp.where(ids == spot, extra_ref[pl.ds(number, 1), :], 0.0)) * keep
    grad_two = norm_rows_back(grad_out, unit, scale_inv, gain)
    grad_low = grad_two.astype(bf16)
    gf_ref[...] = grad_low
    if own:
        two_ref[...] = grad_two
        sums_ref[0:1, :] = jnp.sum(grad_low.astype(f32), axis=0, keepdims=True)
        sums_ref[1:2, :] = jnp.sum(grad_out * unit, axis=0, keepdims=True)
        sums_ref[2:3, :] = jnp.sum(grad_out, axis=0, keepdims=True)
        sums_ref[3:8, :] = jnp.zeros((5, sums_ref.shape[1]), f32)
    mark_ref[...] = jnp.zeros_like(mark_ref)

    @pl.when((spot >= 0) & (spot < rows))
    def _():
        row, _ = norm_rows(y_ref[pl.ds(jnp.clip(spot, 0, rows - 1), 1), :])
        mark_ref[0:1, :] = row * gain + shift

    if blocks:
        move_columns(gf_ref, cols_ref, blocks)
    else:
        cols_ref[...] = gf_ref[...]
    copies.start(cols_ref, gf_full.at[there, :])
    for side, weight_ref in enumerate((down_ref, down2_ref)):

        @pl.loop(0, hidden // STRIP)
        def _(i):
            cols = strip(i + side * (hidden // STRIP))
            grad_act = dot_nt(gf_ref[...], weight_ref[strip(i), :])
            grad_pre = (grad_act * slope_ref[pl.ds(offset, rows), cols]).astype(bf16)
            gp_ref[:, cols] = grad_pre
            ub_ref[:, cols] = jnp.sum(grad_pre.astype(f32), axis=0, keepdims=True)

    copies.start(gp_ref, gp_full.at[there, :])

    @pl.loop(0, up_ref.shape[0] // STRIP)
    def _(i):
        cols = strip(i)
        part_ref[:, cols] = dot_nt(gp_ref[:, :hidden], up_ref[cols, :]) + dot_nt(gp_ref[:, hidden:], up2_ref[cols, :])

    copies.wait()


def back(own, blocks, offset, target, block, part, meta, y, out_grad, extra, vectors, slope, downs, ups, filled):
    rows, width = y.shape
    hidden = 2 * ups[0].shape[1]
    outputs = [shape(rows, width), shape(1, hidden), shape(8, width)]
    if own:
        outputs += [shape(rows, width), shape(8, width)]
    return whole(
        functools.partial(back_kernel, own, blocks, offset, target, not filled, block, part),
        "feed_back",
        [y, out_grad, extra, vectors, slope, *downs, *ups],
        outputs,
        scalars=meta,
        filled=filled
        or [shape(4 * rows, width), shape(4 * rows, width, bf16), shape(4 * rows, hidden, bf16)],
        scratch=[
            pltpu.VMEM((rows, width), bf16),
            pltpu.VMEM((rows, width), f32),
            pltpu.VMEM((rows, hidden), bf16),
            pltpu.VMEM((rows, width), bf16),
        ],
        sems=3,
    )


def context_back_kernel(blocks, own_ref, first_ref, sib_ref, near_w_ref, far_w_ref, far_ref, near_ref, sums_ref, *refs):
    low_ref = refs[-1]
    rows = own_ref.shape[0]
    low_ref[:rows, :] = own_ref[...]
    low_ref[rows:, :] = sib_ref[:rows, :].astype(bf16)
    wide = far_ref.shape[1]
    far_ref[: 2 * rows, :] = dot_nt(low_ref[...], far_w_ref[...])
    near_ref[...] = dot_nt(low_ref[...], near_w_ref[...]).astype(bf16)
    for k in range(first_ref.shape[1] // wide):
        cols = slice(k * wide, (k + 1) * wide)
        chip = first_ref[rows : rows + 8, cols] + sib_ref[rows : rows + 8, cols]
        sums_ref[8 * k : 8 * k + 8, :] = chip
        far_ref[2 * rows + 8 * k : 2 * rows + 8 * k + 8, :] = chip
    if blocks:
        move_columns(low_ref, refs[0], blocks)


def first_back_kernel(*refs):
    streams = (refs[:3], refs[3:6])
    chip_ref = refs[6]
    ub_refs = refs[7:11]
    marks = refs[11:15]
    unit_ref, inv_ref, vec_ref, first_ref, low_ref, ub_ref = refs[15:]
    hidden = ub_ref.shape[1]
    ub = ub_refs[0][...] + ub_refs[1][...] + ub_refs[2][...] + ub_refs[3][...]
    ub_ref[...] = ub[:, :hidden]
    gain = row_of(vec_ref, GAIN_ONE)
    size, width = streams[0][0].shape
    rows = 2 * size
    sums = [0.0] * 6
    for half, (two_ref, own_ref, ffn_ref) in enumerate(streams):
        here = pl.ds(half * size, size)
        grad_normed = two_ref[...] + own_ref[...]
        if half:
            grad_normed = grad_normed + chip_ref[...]
        unit = unit_ref[here, :]
        first = norm_rows_back(grad_normed, unit, inv_ref[here, 0:1], gain)
        low = first.astype(bf16)
        first_ref[here, :] = first
        low_ref[here, :] = low
        terms = [low.astype(f32), grad_normed * unit, grad_normed]
        for k in range(3):
            sums[k] = sums[k] + jnp.sum(terms[k], axis=0, keepdims=True)
            sums[k + 3] = sums[k + 3] + ffn_ref[k : k + 1, :]
    for k in range(6):
        first_ref[rows + k : rows + k + 1, :] = sums[k]
    first_ref[rows + 6 : rows + 8, :] = jnp.zeros((2, width), f32)
    first_ref[rows + 8 : rows + 9, :] = ub[:, hidden:]
    first_ref[rows + 9 : rows + 10, :] = marks[0][0:1, :] + marks[1][0:1, :]
    first_ref[rows + 10 : rows + 11, :] = marks[2][0:1, :] + marks[3][0:1, :]
    first_ref[rows + 11 : rows + 16, :] = jnp.zeros((5, width), f32)


def input_kernel(near_ref, far_ref, gk_ref, gv_ref, qw_ref, kw_ref, vw_ref, first_ref, mine_ref, away_ref):
    rows = near_ref.shape[0] // 2
    for p in range(4):
        gq_ref = (near_ref, far_ref)[p // 2]
        here = pl.ds(p * rows, rows)
        value = (
            dot_nt(gq_ref[pl.ds((p % 2) * rows, rows), :], qw_ref[...])
            + dot_nt(gk_ref[here, :], kw_ref[...])
            + dot_nt(gv_ref[here, :], vw_ref[...])
        )
        if p == 0:
            value = value + first_ref[:rows, :]
        (mine_ref, away_ref)[p % 2][pl.ds((p // 2) * rows, rows), :] = value


def chip_kernel(mine_ref, got_ref, keep_ref, send_ref):
    rows = mine_ref.shape[0] // 2
    step = 64

    @pl.loop(0, rows // step)
    def _(i):
        for p in range(2):
            here = strip(i + p * (rows // step), step)
            there = strip(i + (1 - p) * (rows // step), step)
            value = mine_ref[here, :] + got_ref[here, :]
            keep_ref[here, :] = value
            send_ref[there, :] = value


def place_kernel(meta_ref, mine_ref, other_ref, out_ref, sems):
    rows = mine_ref.shape[0] // 2
    copies = Copies(sems)
    for p, block in enumerate((0, 2, 1, 3)):
        ref = (mine_ref, other_ref)[p // 2]
        copies.start(ref.at[pl.ds((p % 2) * rows, rows), :], out_ref.at[strip(meta_ref[block], rows), :])
    copies.wait()


def round_place_kernel(meta_ref, near_ref, far_ref, out_ref, low_ref, sems):
    rows = near_ref.shape[0] // 2
    copies = Copies(sems)
    for p, block in enumerate((0, 2, 1, 3)):
        ref = (near_ref, far_ref)[p // 2]
        low_ref[p * rows : (p + 1) * rows, :] = ref[(p % 2) * rows : (p % 2 + 1) * rows, :].astype(bf16)
        copies.start(low_ref.at[pl.ds(p * rows, rows), :], out_ref.at[strip(meta_ref[block], rows), :])
    copies.wait()


def swap_core(value):
    return lax.ppermute(value, "mp", [(i, i ^ 1) for i in range(4)])


def swap_chip(value):
    return lax.ppermute(value, "mp", [(i, i ^ 2) for i in range(4)])


def gather_rows(own):
    other = swap_chip(own)
    sibling = swap_core(own)
    diagonal = swap_core(other)
    return own, sibling, other, diagonal


def bit_order_blocks(parts, order):
    bits = len(order)
    blocks = []
    for position in range(parts):
        block = 0
        for level, bit in enumerate(order):
            block |= ((position >> (bits - 1 - level)) & 1) << bit
        blocks.append(block)
    return blocks


def bit_order_columns(matrix, parts, order):
    width = matrix.shape[1] // parts
    return jnp.concatenate(
        [matrix[:, b * width : (b + 1) * width] for b in bit_order_blocks(parts, order)], axis=1
    )


def dp_swap(value, parts, bit):
    return lax.ppermute(value, "dp", [(i, i ^ (1 << bit)) for i in range(parts)])


class Sum:
    def __init__(self, parts, order, meta, line, spare=0):
        self.parts, self.order, self.meta, self.line = parts, list(order), meta, line
        self.spare = spare
        self.turned = False
        self.second = None
        self.extra = self.total = self.got = None

    def begin(self, away, total, extra=None):
        self.total, self.extra = total, extra
        self.level = 0
        self.ship(away)

    def ship(self, away):
        self.got = dp_swap(away, self.parts, self.order[self.level])
        self.level += 1

    def step(self):
        if self.got is None:
            return
        got = self.line.hold(self.got)
        self.got = None
        rows, cols = self.total.shape
        ends = self.level == len(self.order)
        riders = 0 if self.extra is None else self.extra.shape[0]
        bit = 0 if ends else self.order[self.level]
        rest = [shape(riders, cols)] if riders else []
        outputs = [shape(rows, cols)]
        if not ends:
            outputs = [shape(rows // 2 + riders + self.spare, cols), shape(rows // 2, cols)]
        if ends and self.turned and rows % 128 == 0:
            outputs = [shape(rows, cols // 2), shape(cols // 2, rows)]
        given = [self.total, got] + ([self.extra] if riders else [])
        result = whole(
            functools.partial(fold_kernel, riders, ends, bit), "fold", given, outputs + rest, scalars=self.meta
        )
        if riders:
            self.extra = result[-1]
        if ends:
            self.total = result[0]
            self.second = result[1] if len(outputs) == 2 else None
            self.line.mark(self.total)
        else:
            self.total = result[1]
            self.ship(result[0])
            self.line.mark(result[0])

    def finish(self):
        while self.got is not None:
            self.step()
        return self.total


class Line:
    def __init__(self):
        self.token = None

    def mark(self, *values):
        self.token = values

    def hold(self, *values):
        if self.token is not None:
            values = lax.optimization_barrier(tuple(values) + self.token)[: len(values)]
        return values if len(values) > 1 else values[0]


def shards(
    dp_size,
    tokens,
    doc_lengths,
    cls_pos,
    cls_count,
    q_weight,
    q_bias,
    k_weight,
    v_weight,
    v_bias,
    o_weight,
    o_bias,
    ln1_gain,
    ln1_bias,
    up_weight,
    up_bias,
    down_weight,
    down_bias,
    ln2_gain,
    ln2_bias,
    out_grad,
    pooled_grad,
):
    slot_len, width = tokens.shape
    rows = slot_len // 4
    half = 2 * rows
    head_width = q_weight.shape[1]
    rank = lax.axis_index("mp")
    place_id = lax.axis_index("dp")
    bits = dp_size.bit_length() - 1
    order_a = list(range(bits))
    order_b = [1, 0] + list(range(2, bits)) if bits > 1 else order_a
    length = doc_lengths[0]
    blocks = [rank ^ j for j in range(4)]

    line = Line()
    sizes = width // dp_size
    fixed_a = bit_order_blocks(dp_size, order_a) if sizes % 128 == 0 else None
    fixed_b = bit_order_blocks(dp_size, order_b) if sizes % 128 == 0 else None
    unit = rows // 2

    row_ids = lax.iota(jnp.int32, rows)
    positions = jnp.concatenate([row_ids + blocks[j] * rows for j in range(4)])
    bias = jnp.where(positions < length, 0.0, MASKED).astype(f32)[None, :]
    meta = jnp.concatenate(
        [
            jnp.stack(blocks).astype(jnp.int32),
            doc_lengths,
            cls_count,
            cls_pos[0],
            jnp.stack([(place_id >> bit) & 1 for bit in range(max(bits, 1))]).astype(jnp.int32),
        ]
    )
    hidden = up_bias.shape[0]

    meta, bias = lax.optimization_barrier((meta, bias))

    o_part, vectors = prepare(
        meta, o_weight, [o_bias, ln1_gain, ln1_bias, ln2_gain, ln2_bias, down_bias, up_bias]
    )
    o_got = swap_chip(o_part)
    line.mark(o_part)
    local, queries_near, queries_far, key_rows, value_rows = qkv(
        meta, line.hold(tokens), (q_weight, k_weight, v_weight), (q_bias, v_bias)
    )
    away_context, lse_far = attn_fwd(queries_far, key_rows, value_rows, bias, 256, f32)
    arrived = swap_chip(away_context)
    line.mark(away_context)
    o_got = line.hold(o_got)
    o_other = dp_swap(o_got, dp_size, 0)
    line.mark(o_got)
    up_held, down_held = line.hold(up_weight, down_weight)
    wide = whole(
        widen_kernel,
        "widen",
        [up_held, down_held, vectors],
        [shape(width + hidden + 8, width)],
        limit=20,
    )[0]
    line.mark(wide)
    wide = swap_core(wide)
    context_near, lse_near = attn_fwd(line.hold(queries_near), key_rows, value_rows, bias, 256, bf16)
    line.mark(context_near)
    if fixed_a:
        local_a, local_b = whole(
            functools.partial(order_kernel, fixed_a, fixed_b),
            "order",
            [line.hold(local)],
            [shape(slot_len, width, bf16)] * 2,
        )
    else:
        local_a = bit_order_columns(local, dp_size, order_a)
        local_b = bit_order_columns(local, dp_size, order_b)
    line.mark(local_a)
    own, sib, context_other, o_far = whole(
        project_kernel,
        "project",
        [context_near, line.hold(arrived), o_weight, o_got, line.hold(o_other)],
        [shape(rows, width), shape(rows, width), shape(half, head_width, bf16), shape(head_width, width, bf16)],
        scalars=meta,
    )
    n_a, n_b, normed, unit_one, inv_one = whole(
        first_norm_kernel,
        "first_norm",
        [own, swap_core(sib), local, vectors],
        [shape(unit, width), shape(unit, width), shape(rows, width), shape(rows, width), shape(rows, 128)],
    )
    line.mark(n_a)
    chip_a = swap_chip(n_a)
    chip_b = swap_chip(n_b)
    up_far, down_far, vectors_far = whole(
        round_kernel,
        "round",
        [line.hold(wide)],
        [shape(width, hidden, bf16), shape(hidden, width, bf16), shape(8, width)],
        limit=20,
    )
    ups = (up_weight, up_far)
    downs = (down_weight, down_far)
    both = (vectors, vectors_far)
    lo, act, slope_near, own_a, own_b = feed(True, unit, fixed_b, (0, 1), normed, ups, both, downs, ())
    line.mark(own_a)
    lo, act, slope_a, part = feed(
        False, unit, fixed_b, (2,), line.hold(chip_a), ups, both, downs, (lo, act)
    )
    got_a = swap_chip(part)
    line.mark(part)
    lo, act, slope_b, part = feed(
        False, unit, fixed_b, (3,), line.hold(chip_b), ups, both, downs, (lo, act)
    )
    got_b = swap_chip(part)
    line.mark(part)

    def back_rows(own, k, y, slope, offset, filled):
        place = k if own else 2 + k
        return back(
            own, fixed_a, offset, place, 0 if own else 2, k, meta, y, out_grad, pooled_grad[0], vectors,
            slope, downs, ups, filled,
        )

    y_a = add(own_a, line.hold(got_a))
    chip_a = swap_chip(y_a)
    *filled, back_a, ub_a, mark_a, two_a, sums_a = back_rows(True, 0, y_a, slope_near, 0, ())
    line.mark(back_a)
    y_b = add(own_b, line.hold(got_b))
    chip_b = swap_chip(y_b)
    *filled, back_b, ub_b, mark_b, two_b, sums_b = back_rows(True, 1, y_b, slope_near, unit, filled)
    line.mark(back_b)
    *filled, part, ub_c, mark_c = back_rows(False, 0, line.hold(chip_a), slope_a, 0, filled)
    got_a = swap_chip(part)
    line.mark(part)
    *filled, part, ub_d, mark_d = back_rows(False, 1, line.hold(chip_b), slope_b, 0, filled)
    got_b = swap_chip(part)
    line.mark(part)
    back_a = add(back_a, line.hold(got_a))
    line.mark(back_a)
    out_wide, grad_fed, grad_pre = filled

    def in_order(value, fixed, order):
        return value if fixed else bit_order_columns(value, dp_size, order)

    gf_cols, lo_cols = in_order(grad_fed, fixed_a, order_a), in_order(lo, fixed_b, order_b)
    down_sum = Sum(dp_size, order_a, meta, line, 0)
    up_sum = Sum(dp_size, order_b, meta, line, 0)

    def pair(side, sum_of, left, right, given=()):
        half_rows = width // 2
        return whole(
            functools.partial(pair_kernel, side, bool(given), sum_of.order[0]),
            "pair",
            [left, right, *given],
            [shape(half_rows, hidden)] * 2 if given else [shape(width, hidden)],
            scalars=meta,
        )

    down_other = pair(1, down_sum, line.hold(gf_cols), act)[0]
    down_given = swap_core(down_other)
    line.mark(down_other)
    up_other = pair(1, up_sum, lo_cols, line.hold(grad_pre))[0]
    up_given = swap_core(up_other)
    line.mark(up_other)

    down_sum.begin(*pair(0, down_sum, gf_cols, act, [line.hold(down_given)]))
    up_sum.begin(*pair(0, up_sum, lo_cols, grad_pre, [line.hold(up_given)]))

    line.mark(down_sum.total, up_sum.total)
    got_b = line.hold(got_b)
    first_ext, grad_attended_own, up_bias_own = whole(
        first_back_kernel,
        "first_norm_back",
        [two_a, back_a, sums_a, two_b, back_b, sums_b, got_b, ub_a, ub_b, ub_c, ub_d]
        + [mark_a, mark_b, mark_c, mark_d, unit_one, inv_one, vectors],
        [shape(rows + 16, width), shape(rows, width, bf16), shape(1, hidden)],
    )
    sib_ext = swap_core(first_ext)
    riders = 8 * width // head_width
    context_far_grad, grad_context_near, chip_sums, *ga_cols = whole(
        functools.partial(context_back_kernel, fixed_b),
        "context_back",
        [grad_attended_own, first_ext, sib_ext, o_weight, o_far],
        [shape(half + riders, head_width), shape(half, head_width, bf16), shape(riders, head_width)]
        + [shape(half, width, bf16)] * (2 if fixed_b else 1),
    )
    ga_cols = in_order(ga_cols[0], fixed_b, order_b)
    grad_context_far = swap_chip(context_far_grad)
    line.mark(context_far_grad)
    *o_away, o_kept = whole(
        o_kernel,
        "o_grad",
        [line.hold(ga_cols), context_other, context_near],
        [shape(width // 2, head_width)] * 2 + [shape(width, head_width)],
    )
    o_got = [swap_chip(v) for v in o_away]
    line.mark(o_kept)

    queries_near = line.hold(queries_near)
    grad_q_near, key_sum, value_sum = attn_bwd(
        queries_near, grad_context_near, key_rows, value_rows, bias, lse_near, 256
    )
    line.mark(grad_q_near)
    grad_context_far = line.hold(grad_context_far)
    line.mark(grad_context_far)
    queries_far = line.hold(queries_far)
    grad_q_far, grad_k, grad_v = attn_bwd(
        queries_far, grad_context_far, key_rows, value_rows, bias, lse_far, 256, (key_sum, value_sum)
    )
    line.mark(grad_k)

    qk_sum = Sum(dp_size, order_a, meta, line)
    vo_sum = Sum(dp_size, order_b, meta, line)
    vo_sum.turned = True
    riders = 8 * width // head_width
    extra_rows = -(-(riders // 2 + 1 + hidden // (2 * head_width)) // 8) * 8
    qk_away, qk_kept, qk_extra = whole(
        functools.partial(qk_kernel, qk_sum.order[0]),
        "qk_grad",
        [local_a, line.hold(grad_q_near), grad_q_far, grad_k, grad_v, chip_sums, grad_context_far]
        + [up_bias_own, sib_ext],
        [
            shape(width // 2 + extra_rows, 2 * head_width),
            shape(width // 2, 2 * head_width),
            shape(extra_rows, 2 * head_width),
        ],
        scalars=meta,
    )
    line.mark(qk_away)
    o_got = line.hold(*o_got)
    line.mark(*o_got)
    down_sum.step()
    in_mine, in_away = whole(
        input_kernel,
        "input_grad",
        [line.hold(grad_q_near), grad_q_far, grad_k, grad_v, q_weight, k_weight, v_weight, first_ext],
        [shape(half, width)] * 2,
    )
    line.mark(in_mine)
    up_sum.step()
    in_got = swap_core(in_away)
    out_far = swap_core(line.hold(out_wide))
    in_kept, in_sent = whole(
        chip_kernel, "chip_sum", [in_mine, line.hold(in_got)], [shape(half, width)] * 2
    )
    in_got = swap_chip(in_sent)
    line.mark(in_sent)
    out = whole(
        round_place_kernel,
        "round_place",
        [out_wide, line.hold(out_far)],
        [],
        scalars=meta,
        filled=[shape(slot_len, width, bf16)],
        scratch=[pltpu.VMEM((slot_len, width), bf16)],
        sems=4,
        far=True,
    )[0]
    line.mark(out)
    vo_away, vo_kept = whole(
        functools.partial(vo_kernel, vo_sum.order[0]),
        "vo_grad",
        [local_b, line.hold(grad_v), o_kept, *o_got],
        [shape(width // 2, 2 * head_width)] * 2,
        scalars=meta,
    )
    line.mark(vo_away)
    down_sum.step()
    up_sum.step()
    qk_sum.begin(line.hold(qk_away), qk_kept, qk_extra)
    vo_sum.begin(line.hold(vo_away), vo_kept)
    for bit in range(bits):
        qk_sum.step()
        if bit == 0:
            down_sum.step()
            up_sum.step()
        vo_sum.step()
        if bit > 1:
            down_sum.step()
            up_sum.step()
        if bit == min(1, bits - 1):
            in_final = add(in_kept, line.hold(in_got))
            in_other = swap_core(in_final)
            line.mark(in_final)
            in_grad = whole(
                place_kernel,
                "place",
                [in_final, line.hold(in_other)],
                [],
                scalars=meta,
                filled=[shape(slot_len, width)],
                sems=4,
                far=True,
            )[0]
            line.mark(in_grad)
    qk_total, vo_total = qk_sum.finish(), vo_sum.finish()
    riding = qk_sum.extra
    row = riders // 2
    shared = jnp.concatenate([riding[:row, :head_width], riding[:row, head_width:]], axis=0)
    shared = shared.reshape(-1, 8, head_width).transpose(1, 0, 2).reshape(8, width)
    biases = riding[row].reshape(2, head_width)
    up_bias_sum = riding[row + 1 : row + 1 + hidden // (2 * head_width)].reshape(-1)
    if vo_sum.second is None:
        v_sum, o_sum = vo_total[:, :head_width], vo_total[:, head_width:].T
    else:
        v_sum, o_sum = vo_total, vo_sum.second
    down_sum = down_sum.finish().T
    up_sum = up_sum.finish()

    mine = first_ext[rows + 9 : rows + 11]
    theirs = sib_ext[rows + 9 : rows + 11]
    marks = jnp.concatenate([mine[:1], theirs[:1], mine[1:], theirs[1:]], axis=0)
    pooled = jnp.concatenate(
        [lax.dynamic_index_in_dim(marks, blocks[j], keepdims=True) for j in range(4)], axis=0
    )[None]
    return (
        out,
        pooled,
        in_grad,
        qk_total[:, :head_width],
        biases[0],
        qk_total[:, head_width:],
        v_sum,
        biases[1],
        o_sum,
        shared[0],
        shared[1],
        shared[2],
        up_sum,
        up_bias_sum,
        down_sum,
        shared[3],
        shared[4],
        shared[5],
    )


def solution(mesh):
    return jax.shard_map(
        functools.partial(shards, mesh.shape["dp"]),
        mesh=mesh,
        in_specs=(
            P("dp", None),
            P("dp"),
            P("dp", None),
            P("dp"),
            P(None, "mp"),
            P("mp"),
            P(None, "mp"),
            P(None, "mp"),
            P("mp"),
            P("mp", None),
            P(),
            P(),
            P(),
            P(None, "mp"),
            P("mp"),
            P("mp", None),
            P(),
            P(),
            P(),
            P("dp", None),
            P("dp", None, None),
        ),
        out_specs=(
            P("dp", None),
            P("dp", None, None),
            P("dp", None),
            P("dp", "mp"),
            P("mp"),
            P("dp", "mp"),
            P("dp", "mp"),
            P("mp"),
            P("mp", "dp"),
            P(),
            P(),
            P(),
            P("dp", "mp"),
            P("mp"),
            P("mp", "dp"),
            P(),
            P(),
            P(),
        ),
        check_vma=False,
    )
```

```python
import functools

import jax
import jax.numpy as jnp
from jax import lax
from jax.experimental import pallas as pl
from jax.experimental.pallas import tpu as pltpu
from jax.sharding import PartitionSpec as P

HEAD_DIM = 64
NORM_EPS = 1e-05
ROOT_HALF = 0.7071067811865476
INV_ROOT_TAU = 0.3989422804014327
LOG2E = 1.4426950408889634
SCORE_SCALE = 0.125 * LOG2E
MASKED = -1e30

f32 = jnp.float32
bf16 = jnp.bfloat16
VMEM_LIMIT = 20 * 1024 * 1024


def dot_nn(a, b):
    return lax.dot_general(a, b, (((1,), (0,)), ((), ())), preferred_element_type=f32)


def dot_nt(a, b):
    return lax.dot_general(a, b, (((1,), (1,)), ((), ())), preferred_element_type=f32)


def dot_tn(a, b):
    return lax.dot_general(a, b, (((0,), (0,)), ((), ())), preferred_element_type=f32)


def attn_fwd_kernel(q_ref, k_ref, v_ref, bias_ref, o_ref, lse_ref):
    rows, width = q_ref.shape
    heads = width // HEAD_DIM
    lane = lax.broadcasted_iota(jnp.int32, (1, width), 1) // HEAD_DIM
    lse_lane = lax.broadcasted_iota(jnp.int32, (1, 128), 1)
    q = q_ref[...]
    k = k_ref[...]
    v = v_ref[...]
    bias = bias_ref[...]
    out = jnp.zeros((rows, width), f32)
    lse = jnp.zeros((rows, 128), f32)
    for h in range(heads):
        qh = jnp.where(lane == h, q, jnp.zeros_like(q))
        s = dot_nt(qh, k) * SCORE_SCALE + bias
        top = jnp.max(s, axis=1, keepdims=True)
        e = jnp.exp2(s - top)
        total = jnp.sum(e, axis=1, keepdims=True)
        p = (e * (1.0 / total)).astype(bf16)
        c = dot_nn(p, v)
        out = jnp.where(lane == h, c, out)
        lse = jnp.where(lse_lane == h, top + jnp.log2(total), lse)
    o_ref[...] = out.astype(o_ref.dtype)
    lse_ref[...] = lse


def attn_fwd(q, k, v, bias, block, dtype):
    rows, width = q.shape
    keys = k.shape[0]
    full = pl.BlockSpec((keys, width), lambda i: (0, 0))
    return pl.pallas_call(
        attn_fwd_kernel,
        grid=(rows // block,),
        in_specs=[
            pl.BlockSpec((block, width), lambda i: (i, 0)),
            full,
            full,
            pl.BlockSpec((1, keys), lambda i: (0, 0)),
        ],
        out_specs=[
            pl.BlockSpec((block, width), lambda i: (i, 0)),
            pl.BlockSpec((block, 128), lambda i: (i, 0)),
        ],
        out_shape=[
            jax.ShapeDtypeStruct((rows, width), dtype),
            jax.ShapeDtypeStruct((rows, 128), f32),
        ],
        compiler_params=pltpu.CompilerParams(vmem_limit_bytes=VMEM_LIMIT),
        cost_estimate=pl.CostEstimate(flops=1024, bytes_accessed=1024, transcendentals=0),
        name="attn_fwd",
    )(q, k, v, bias)


def attn_bwd_kernel(carried, *refs):
    q_ref, g_ref, k_ref, v_ref, bias_ref, lse_ref = refs[:6]
    refs = refs[6:]
    if carried:
        gk_in, gv_in = refs[:2]
        refs = refs[2:]
    gq_ref, gk_ref, gv_ref, gk_acc, gv_acc, gq_acc = refs
    step = pl.program_id(0)
    width = q_ref.shape[1]
    lane = lax.broadcasted_iota(jnp.int32, (1, width), 1) // HEAD_DIM
    lse_lane = lax.broadcasted_iota(jnp.int32, (1, 128), 1)

    @pl.when(step == 0)
    def _():
        gk_acc[...] = gk_in[...] if carried else jnp.zeros_like(gk_acc)
        gv_acc[...] = gv_in[...] if carried else jnp.zeros_like(gv_acc)

    @pl.loop(0, width // HEAD_DIM)
    def _(h):
        mine = lane == h
        zero = jnp.zeros(q_ref.shape, bf16)
        qh = jnp.where(mine, q_ref[...], zero)
        gh = jnp.where(mine, g_ref[...].astype(bf16), zero)
        lse = jnp.sum(jnp.where(lse_lane == h, lse_ref[...], 0.0), axis=1, keepdims=True)
        s = dot_nt(qh, k_ref[...]) * SCORE_SCALE + bias_ref[...]
        p = jnp.exp2(s - lse)
        dp = dot_nt(gh, v_ref[...])
        inner = jnp.sum(p * dp, axis=1, keepdims=True)
        ds = (p * (dp - inner)).astype(bf16)
        gq_acc[...] = jnp.where(mine, dot_nn(ds, k_ref[...]), gq_acc[...])
        gk_acc[...] += dot_tn(ds, qh)
        gv_acc[...] += dot_tn(p.astype(bf16), gh)

    gq_ref[...] = (gq_acc[...] * 0.125).astype(bf16)

    @pl.when(step == pl.num_programs(0) - 1)
    def _():
        scale = 0.125 if carried else 1.0
        gk_ref[...] = (gk_acc[...] * scale).astype(gk_ref.dtype)
        gv_ref[...] = gv_acc[...].astype(gv_ref.dtype)


def attn_bwd(q, g, k, v, bias, lse, block, sums=()):
    rows, width = q.shape
    keys = k.shape[0]
    full = pl.BlockSpec((keys, width), lambda i: (0, 0))
    part = pl.BlockSpec((block, width), lambda i: (i, 0))
    sum_type = bf16 if sums else f32
    return pl.pallas_call(
        functools.partial(attn_bwd_kernel, bool(sums)),
        grid=(rows // block,),
        in_specs=[
            part,
            part,
            full,
            full,
            pl.BlockSpec((1, keys), lambda i: (0, 0)),
            pl.BlockSpec((block, 128), lambda i: (i, 0)),
        ]
        + [full] * len(sums),
        out_specs=[part, full, full],
        out_shape=[
            jax.ShapeDtypeStruct((rows, width), bf16),
            jax.ShapeDtypeStruct((keys, width), sum_type),
            jax.ShapeDtypeStruct((keys, width), sum_type),
        ],
        scratch_shapes=[pltpu.VMEM((keys, width), f32)] * 2 + [pltpu.VMEM((block, width), f32)],
        compiler_params=pltpu.CompilerParams(vmem_limit_bytes=VMEM_LIMIT),
        cost_estimate=pl.CostEstimate(flops=1024, bytes_accessed=1024, transcendentals=0),
        name="attn_bwd",
    )(q, g, k, v, bias, lse, *sums)


in_vmem = pl.BlockSpec(memory_space=pltpu.VMEM)
STRIP = 256
LENGTH, COUNT, MARKS, BITS = 4, 5, 6, 10
O_BIAS, GAIN_ONE, SHIFT_ONE, GAIN_TWO, SHIFT_TWO, DOWN_BIAS, UP_BIAS, QV_BIAS = range(8)


def row_of(ref, index):
    return ref[index : index + 1, :]


def strip(index, size=STRIP):
    return pl.ds(pl.multiple_of(index * size, size), size)


def shape(rows, cols, dtype=f32):
    return jax.ShapeDtypeStruct((rows, cols), dtype)


def whole(kernel, name, inputs, outputs, scalars=None, filled=(), sems=0, scratch=(), limit=8, far=False):
    lead = [] if scalars is None else [scalars]
    anywhere = pl.BlockSpec(memory_space=pl.ANY)
    given = [v for v in filled if not isinstance(v, jax.ShapeDtypeStruct)]
    begun = [jax.ShapeDtypeStruct(v.shape, v.dtype) for v in filled]
    first = len(lead) + len(inputs)
    return pl.pallas_call(
        kernel,
        in_specs=[pl.BlockSpec(memory_space=pltpu.SMEM)] * len(lead)
        + [in_vmem] * len(inputs)
        + [anywhere] * len(given),
        out_specs=[pl.BlockSpec(memory_space=pltpu.HBM) if far else anywhere] * len(begun)
        + [in_vmem] * len(outputs),
        out_shape=begun + list(outputs),
        scratch_shapes=list(scratch) + ([pltpu.SemaphoreType.DMA((sems,))] if sems else []),
        input_output_aliases={first + p: p for p in range(len(given))},
        compiler_params=pltpu.CompilerParams(vmem_limit_bytes=limit * 1024 * 1024),
        cost_estimate=pl.CostEstimate(flops=1024, bytes_accessed=1024, transcendentals=0),
        name=name,
    )(*lead, *inputs, *given)


class Copies:
    def __init__(self, sems):
        self.sems, self.made = sems, []

    def start(self, source, target):
        copy = pltpu.make_async_copy(source, target, self.sems.at[len(self.made)])
        copy.start()
        self.made.append(copy)

    def wait(self):
        for copy in self.made:
            copy.wait()


def project_kernel(meta_ref, near_ref, other_ref, o_near_ref, o_got_ref, o_other_ref, own_ref, sib_ref, low_ref, o_far_ref):
    rows = own_ref.shape[0]
    part = o_got_ref.shape[0]
    first = meta_ref[BITS] == 0
    o_far_ref[:part, :] = jnp.where(first, o_got_ref[...], o_other_ref[...]).astype(bf16)
    o_far_ref[part:, :] = jnp.where(first, o_other_ref[...], o_got_ref[...]).astype(bf16)
    low_ref[...] = other_ref[...].astype(bf16)
    both = dot_nn(near_ref[...], o_near_ref[...]) + dot_nn(low_ref[...], o_far_ref[...])
    own_ref[...] = both[:rows]
    sib_ref[...] = both[rows:]


def mean_of(values):
    return jnp.sum(values, axis=-1, keepdims=True) * (1.0 / values.shape[-1])


def norm_rows(values):
    centre = values - mean_of(values)
    scale_inv = lax.rsqrt(mean_of(centre * centre) + NORM_EPS)
    return centre * scale_inv, scale_inv


def norm_rows_back(grad_rows, unit_rows, scale_inv, gain):
    scaled = grad_rows * gain
    return scale_inv * (scaled - mean_of(scaled) - unit_rows * mean_of(scaled * unit_rows))


def first_norm_kernel(own_ref, near_ref, tok_ref, vec_ref, na_ref, nb_ref, all_ref, unit_ref, inv_ref):
    gain = row_of(vec_ref, GAIN_ONE)
    shift = row_of(vec_ref, SHIFT_ONE)
    for half, out_ref in enumerate((na_ref, nb_ref)):
        size = out_ref.shape[0]
        rows = pl.ds(half * size, size)
        values = tok_ref[rows, :].astype(f32) + (own_ref[rows, :] + near_ref[rows, :] + row_of(vec_ref, O_BIAS))
        unit, scale_inv = norm_rows(values)
        unit_ref[rows, :] = unit
        inv_ref[rows, :] = jnp.broadcast_to(scale_inv, (size, inv_ref.shape[1]))
        normed = unit * gain + shift
        out_ref[...] = normed
        all_ref[rows, :] = normed


def move_columns(source, target, blocks):
    wide = source.shape[1] // len(blocks)
    for place, block in enumerate(blocks):
        target[:, place * wide : (place + 1) * wide] = source[:, block * wide : (block + 1) * wide]


def order_kernel(blocks_a, blocks_b, in_ref, a_ref, b_ref):
    move_columns(in_ref, a_ref, blocks_a)
    move_columns(in_ref, b_ref, blocks_b)


def prepare_kernel(meta_ref, o_ref, *refs):
    given = refs[:7]
    part_ref, vec_ref, o_in = refs[7:10]
    lines = refs[10:17]
    sems = refs[17]
    copies = Copies(sems)
    copies.start(o_ref.at[strip(meta_ref[BITS], part_ref.shape[0]), :], o_in)
    for line_ref, vector_ref in zip(lines, given):
        copies.start(vector_ref, line_ref)
    copies.wait()
    part_ref[...] = o_in[...].astype(f32)
    vec_ref[...] = jnp.zeros_like(vec_ref)
    for k, line_ref in enumerate(lines):
        vec_ref[k, :] = line_ref[...].astype(f32)


def prepare(meta, o_weight, vectors):
    rows, width = o_weight.shape
    far = pl.BlockSpec(memory_space=pltpu.HBM)
    return pl.pallas_call(
        prepare_kernel,
        in_specs=[pl.BlockSpec(memory_space=pltpu.SMEM)] + [far] * 8,
        out_specs=[in_vmem] * 2,
        out_shape=[shape(rows // 2, width), shape(8, width)],
        scratch_shapes=[pltpu.VMEM((rows // 2, width), bf16)]
        + [pltpu.VMEM((width,), bf16)] * 7
        + [pltpu.SemaphoreType.DMA((8,))],
        compiler_params=pltpu.CompilerParams(vmem_limit_bytes=60 * 1024 * 1024),
        cost_estimate=pl.CostEstimate(flops=1024, bytes_accessed=1024, transcendentals=0),
        name="prepare",
    )(meta, o_weight, *vectors)


def widen_kernel(a_ref, b_ref, vec_ref, wide_ref):
    rows = a_ref.shape[0]
    step = 64

    @pl.loop(0, rows // step)
    def _(i):
        wide_ref[strip(i, step), :] = a_ref[strip(i, step), :].astype(f32)

    @pl.loop(0, b_ref.shape[0] // step)
    def _(i):
        wide_ref[strip(i + rows // step, step), :] = b_ref[strip(i, step), :].astype(f32)

    wide_ref[rows + b_ref.shape[0] :, :] = vec_ref[...]


def qkv_kernel(meta_ref, all_ref, qw_ref, kw_ref, vw_ref, *refs):
    given = refs[:2]
    vec_ref, local_ref, near_ref, far_ref, k_ref, v_ref, q_in, k_in, v_in, qb_in, vb_in, sems = refs[2:]
    half, wide = near_ref.shape
    rows = half // 2
    copies = Copies(sems)
    copies.start(given[0], qb_in)
    copies.start(given[1], vb_in)
    for p in range(4):
        copies.start(all_ref.at[strip(meta_ref[p], rows), :], local_ref.at[pl.ds(p * rows, rows), :])
    copies.start(kw_ref, k_in)
    copies.start(qw_ref, q_in)
    copies.start(vw_ref, v_in)
    copies.wait()
    k_ref[...] = dot_nn(local_ref[...], k_in[...]).astype(bf16)
    vec_ref[0, :] = qb_in[...].astype(f32)
    vec_ref[1, :] = vb_in[...].astype(f32)
    q = (dot_nn(local_ref[...], q_in[...]) + vec_ref[0:1, :]).astype(bf16)
    near_ref[...] = q[:half]
    far_ref[...] = q[half:]
    v_ref[...] = (dot_nn(local_ref[...], v_in[...]) + vec_ref[1:2, :]).astype(bf16)


def qkv(meta, tokens, weights, biases):
    rows, width = tokens.shape
    wide = weights[0].shape[1]
    far = pl.BlockSpec(memory_space=pltpu.HBM)
    return pl.pallas_call(
        qkv_kernel,
        in_specs=[pl.BlockSpec(memory_space=pltpu.SMEM)] + [far] * 6,
        out_specs=[in_vmem] * 6,
        out_shape=[shape(8, wide), shape(rows, width, bf16)]
        + [shape(rows // 2, wide, bf16)] * 2
        + [shape(rows, wide, bf16)] * 2,
        scratch_shapes=[pltpu.VMEM((width, wide), bf16)] * 3
        + [pltpu.VMEM((wide,), bf16)] * 2
        + [pltpu.SemaphoreType.DMA((9,))],
        compiler_params=pltpu.CompilerParams(vmem_limit_bytes=58 * 1024 * 1024),
        cost_estimate=pl.CostEstimate(flops=1024, bytes_accessed=1024, transcendentals=0),
        name="qkv",
    )(meta, tokens, *weights, *biases)[1:]


def add_kernel(*refs):
    step = 64

    @pl.loop(0, refs[0].shape[0] // step)
    def _(i):
        here = strip(i, step)
        total = refs[0][here, :]
        for ref in refs[1:-1]:
            total = total + ref[here, :]
        refs[-1][here, :] = total


def add(*values):
    return whole(add_kernel, "add", list(values), [shape(*values[0].shape)])[0]


def pair_kernel(side, fill, bit, meta_ref, left_ref, right_ref, *refs):
    mine = meta_ref[BITS + bit]
    half = left_ref.shape[1] // 2
    hidden = right_ref.shape[1] // 2
    right = right_ref[:, side * hidden : (side + 1) * hidden]
    for kept in range(2):
        start = pl.multiple_of((mine if kept else 1 - mine) * half, 128)
        value = dot_tn(left_ref[:, pl.ds(start, half)], right)
        if fill:
            refs[1 + kept][...] = value + refs[0][kept * half : (kept + 1) * half, :]
        else:
            refs[0][kept * half : (kept + 1) * half, :] = value


def fold_kernel(riders, ends, bit, meta_ref, total_ref, got_ref, *refs):
    rows = total_ref.shape[0]
    if riders:
        extra_ref = refs[0]
        refs = refs[1:]
        extra = extra_ref[...] + got_ref[rows:, :]
    if ends and len(refs) == 2 and not riders:
        wide = total_ref.shape[1] // 2
        refs[0][...] = total_ref[:, :wide] + got_ref[:rows, :wide]
        refs[1][...] = (total_ref[:, wide:] + got_ref[:rows, wide:]).T
        return
    if ends:
        refs[0][...] = total_ref[...] + got_ref[:rows, :]
        if riders:
            refs[1][...] = extra
        return
    half = rows // 2
    mine = meta_ref[BITS + bit]
    step = min(64, half)

    @pl.loop(0, half // step)
    def _(i):
        away = strip((1 - mine) * (half // step) + i, step)
        kept = strip(mine * (half // step) + i, step)
        refs[0][strip(i, step), :] = total_ref[away, :] + got_ref[away, :]
        refs[1][strip(i, step), :] = total_ref[kept, :] + got_ref[kept, :]

    if riders:
        refs[0][half:, :] = extra
        refs[2][...] = extra
    elif refs[0].shape[0] > half:
        refs[0][half:, :] = jnp.zeros((refs[0].shape[0] - half, refs[0].shape[1]), f32)


def qk_kernel(bit, meta_ref, left_ref, near_ref, far_ref, gk_ref, gv_ref, chip_ref, far_sums_ref, ub_ref, sib_ref, away_ref, kept_ref, extra_ref):
    mine = meta_ref[BITS + bit]
    half = left_ref.shape[1] // 2
    rows = near_ref.shape[0]
    wide = near_ref.shape[1]
    riders = chip_ref.shape[0]
    extra_ref[...] = jnp.zeros_like(extra_ref)
    shared = chip_ref[...] + far_sums_ref[far_sums_ref.shape[0] - riders :, :]
    extra_ref[: riders // 2, :wide] = shared[: riders // 2]
    extra_ref[: riders // 2, wide:] = shared[riders // 2 :]
    row = riders // 2
    query_sum = jnp.sum(near_ref[...].astype(f32), axis=0, keepdims=True)
    extra_ref[row : row + 1, :wide] = query_sum + jnp.sum(far_ref[...].astype(f32), axis=0, keepdims=True)
    extra_ref[row : row + 1, wide:] = jnp.sum(gv_ref[...].astype(f32), axis=0, keepdims=True)
    place = sib_ref.shape[0] - 8
    for k in range(ub_ref.shape[1] // (2 * wide)):
        cols = slice(2 * k * wide, 2 * (k + 1) * wide)
        extra_ref[row + 1 + k : row + 2 + k, :] = ub_ref[:, cols] + sib_ref[place : place + 1, cols]
    for kept, ref in enumerate((away_ref, kept_ref)):
        cols = pl.ds(pl.multiple_of((mine if kept else 1 - mine) * half, 128), half)
        ref[:half, :wide] = dot_tn(left_ref[:rows, cols], near_ref[...]) + dot_tn(left_ref[rows:, cols], far_ref[...])
        ref[:half, wide:] = dot_tn(left_ref[:, cols], gk_ref[...])
    away_ref[half:, :] = extra_ref[...]


def vo_kernel(bit, meta_ref, left_ref, gv_ref, kept_o_ref, got_a_ref, got_b_ref, away_ref, kept_ref):
    mine = meta_ref[BITS + bit]
    half = left_ref.shape[1] // 2
    wide = gv_ref.shape[1]
    for kept, ref in enumerate((away_ref, kept_ref)):
        start = pl.multiple_of((mine if kept else 1 - mine) * half, 128)
        ref[:, :wide] = dot_tn(left_ref[:, pl.ds(start, half)], gv_ref[...])
        rows = pl.ds(start, half)
        top = jnp.where(start == 0, got_a_ref[...], got_b_ref[...])
        ref[:, wide:] = kept_o_ref[rows, :] + top


def o_kernel(cols_ref, other_ref, near_ref, first_ref, second_ref, kept_ref):
    half = first_ref.shape[0]
    first_ref[...] = dot_tn(cols_ref[:, :half], other_ref[...])
    second_ref[...] = dot_tn(cols_ref[:, half:], other_ref[...])
    kept_ref[...] = dot_tn(cols_ref[...], near_ref[...])


def round_kernel(wide_ref, a_ref, b_ref, vec_ref):
    rows = a_ref.shape[0]
    step = 64

    @pl.loop(0, rows // step)
    def _(i):
        a_ref[strip(i, step), :] = wide_ref[strip(i, step), :].astype(bf16)

    @pl.loop(0, b_ref.shape[0] // step)
    def _(i):
        b_ref[strip(i, step), :] = wide_ref[strip(i + rows // step, step), :].astype(bf16)

    vec_ref[...] = wide_ref[rows + b_ref.shape[0] :, :]


def feed_kernel(own, unit, blocks, targets, fresh, *refs):
    in_ref, up_ref, up2_ref, vec_ref, vec2_ref, down_ref, down2_ref = refs[:7]
    refs = refs[7 + (0 if fresh else 2) :]
    lo_full, act_full, slope_ref = refs[:3]
    parts = refs[3:-4]
    low_ref, act_ref, cols_ref, sems = refs[-4:]
    hidden = up_ref.shape[1]
    copies = Copies(sems)
    low_ref[...] = in_ref[...].astype(bf16)
    if blocks:
        move_columns(low_ref, cols_ref, blocks)
    else:
        cols_ref[...] = low_ref[...]
    for p, target in enumerate(targets):
        copies.start(cols_ref.at[pl.ds(p * unit, unit), :], lo_full.at[pl.ds(target * unit, unit), :])
    for side, (weight_ref, bias_ref) in enumerate(((up_ref, vec_ref), (up2_ref, vec2_ref))):

        @pl.loop(0, hidden // STRIP)
        def _(i):
            there = strip(i + side * (hidden // STRIP))
            pre = dot_nn(low_ref[...], weight_ref[:, strip(i)]) + bias_ref[UP_BIAS : UP_BIAS + 1, strip(i)]
            normal_cdf = 0.5 * (1.0 + lax.erf(pre * ROOT_HALF))
            density = jnp.exp(-0.5 * pre * pre) * INV_ROOT_TAU
            act_ref[:, there] = (pre * normal_cdf).astype(bf16)
            slope_ref[:, there] = normal_cdf + pre * density

    for p, target in enumerate(targets):
        copies.start(act_ref.at[pl.ds(p * unit, unit), :], act_full.at[pl.ds(target * unit, unit), :])

    @pl.loop(0, down_ref.shape[1] // STRIP)
    def _(i):
        cols = strip(i)
        part = dot_nn(act_ref[:, :hidden], down_ref[:, cols]) + dot_nn(act_ref[:, hidden:], down2_ref[:, cols])
        if own:
            part = part + (in_ref[:, cols] + vec_ref[DOWN_BIAS : DOWN_BIAS + 1, cols])
        for p, part_ref in enumerate(parts):
            part_ref[:, cols] = part[p * unit : (p + 1) * unit]

    copies.wait()


def feed(own, unit, blocks, targets, rows_in, ups, vectors, downs, filled):
    rows, width = rows_in.shape
    hidden = 2 * ups[0].shape[1]
    return whole(
        functools.partial(feed_kernel, own, unit, blocks, targets, not filled),
        "feed",
        [rows_in, *ups, *vectors, *downs],
        [shape(rows, hidden)] + [shape(unit, width)] * len(targets),
        filled=filled or [shape(4 * unit, width, bf16), shape(4 * unit, hidden, bf16)],
        scratch=[
            pltpu.VMEM((rows, width), bf16),
            pltpu.VMEM((rows, hidden), bf16),
            pltpu.VMEM((rows, width), bf16),
        ],
        sems=2 * len(targets),
    )


def back_kernel(own, blocks, offset, target, fresh, block, part, meta_ref, y_ref, og_ref, extra_ref, vec_ref, slope_ref, down_ref, down2_ref, up_ref, up2_ref, *refs):
    refs = refs[0 if fresh else 3 :]
    out_full, gf_full, gp_full, part_ref, ub_ref, mark_ref = refs[:6]
    refs = refs[6:]
    if own:
        two_ref, sums_ref = refs[:2]
        refs = refs[2:]
    gf_ref, out_ref, gp_ref, cols_ref, sems = refs
    rows = y_ref.shape[0]
    hidden = up_ref.shape[1]
    gain = row_of(vec_ref, GAIN_TWO)
    shift = row_of(vec_ref, SHIFT_TWO)
    copies = Copies(sems)
    ids = lax.broadcasted_iota(jnp.int32, (rows, 1), 0)
    number = meta_ref[block]
    base = pl.multiple_of((2 * number + part) * rows, rows)
    limit = meta_ref[LENGTH] - base
    spot = jnp.where(number < meta_ref[COUNT], meta_ref[MARKS + number] - base, -1)
    there = pl.ds(target * rows, rows)
    keep = (ids < limit).astype(f32)
    unit, scale_inv = norm_rows(y_ref[...])
    out_ref[...] = (unit * gain + shift) * keep
    copies.start(out_ref, out_full.at[there, :])
    grad_out = (og_ref[pl.ds(base, rows), :].astype(f32) + jnp.where(ids == spot, extra_ref[pl.ds(number, 1), :], 0.0)) * keep
    grad_two = norm_rows_back(grad_out, unit, scale_inv, gain)
    grad_low = grad_two.astype(bf16)
    gf_ref[...] = grad_low
    if own:
        two_ref[...] = grad_two
        sums_ref[0:1, :] = jnp.sum(grad_low.astype(f32), axis=0, keepdims=True)
        sums_ref[1:2, :] = jnp.sum(grad_out * unit, axis=0, keepdims=True)
        sums_ref[2:3, :] = jnp.sum(grad_out, axis=0, keepdims=True)
        sums_ref[3:8, :] = jnp.zeros((5, sums_ref.shape[1]), f32)
    mark_ref[...] = jnp.zeros_like(mark_ref)

    @pl.when((spot >= 0) & (spot < rows))
    def _():
        row, _ = norm_rows(y_ref[pl.ds(jnp.clip(spot, 0, rows - 1), 1), :])
        mark_ref[0:1, :] = row * gain + shift

    if blocks:
        move_columns(gf_ref, cols_ref, blocks)
    else:
        cols_ref[...] = gf_ref[...]
    copies.start(cols_ref, gf_full.at[there, :])
    for side, weight_ref in enumerate((down_ref, down2_ref)):

        @pl.loop(0, hidden // STRIP)
        def _(i):
            cols = strip(i + side * (hidden // STRIP))
            grad_act = dot_nt(gf_ref[...], weight_ref[strip(i), :])
            grad_pre = (grad_act * slope_ref[pl.ds(offset, rows), cols]).astype(bf16)
            gp_ref[:, cols] = grad_pre
            ub_ref[:, cols] = jnp.sum(grad_pre.astype(f32), axis=0, keepdims=True)

    copies.start(gp_ref, gp_full.at[there, :])

    @pl.loop(0, up_ref.shape[0] // STRIP)
    def _(i):
        cols = strip(i)
        part_ref[:, cols] = dot_nt(gp_ref[:, :hidden], up_ref[cols, :]) + dot_nt(gp_ref[:, hidden:], up2_ref[cols, :])

    copies.wait()


def back(own, blocks, offset, target, block, part, meta, y, out_grad, extra, vectors, slope, downs, ups, filled):
    rows, width = y.shape
    hidden = 2 * ups[0].shape[1]
    outputs = [shape(rows, width), shape(1, hidden), shape(8, width)]
    if own:
        outputs += [shape(rows, width), shape(8, width)]
    return whole(
        functools.partial(back_kernel, own, blocks, offset, target, not filled, block, part),
        "feed_back",
        [y, out_grad, extra, vectors, slope, *downs, *ups],
        outputs,
        scalars=meta,
        filled=filled
        or [shape(4 * rows, width), shape(4 * rows, width, bf16), shape(4 * rows, hidden, bf16)],
        scratch=[
            pltpu.VMEM((rows, width), bf16),
            pltpu.VMEM((rows, width), f32),
            pltpu.VMEM((rows, hidden), bf16),
            pltpu.VMEM((rows, width), bf16),
        ],
        sems=3,
    )


def context_back_kernel(blocks, own_ref, first_ref, sib_ref, near_w_ref, far_w_ref, far_ref, near_ref, sums_ref, *refs):
    low_ref = refs[-1]
    rows = own_ref.shape[0]
    low_ref[:rows, :] = own_ref[...]
    low_ref[rows:, :] = sib_ref[:rows, :].astype(bf16)
    wide = far_ref.shape[1]
    far_ref[: 2 * rows, :] = dot_nt(low_ref[...], far_w_ref[...])
    near_ref[...] = dot_nt(low_ref[...], near_w_ref[...]).astype(bf16)
    for k in range(first_ref.shape[1] // wide):
        cols = slice(k * wide, (k + 1) * wide)
        chip = first_ref[rows : rows + 8, cols] + sib_ref[rows : rows + 8, cols]
        sums_ref[8 * k : 8 * k + 8, :] = chip
        far_ref[2 * rows + 8 * k : 2 * rows + 8 * k + 8, :] = chip
    if blocks:
        move_columns(low_ref, refs[0], blocks)


def first_back_kernel(*refs):
    streams = (refs[:3], refs[3:6])
    chip_ref = refs[6]
    ub_refs = refs[7:11]
    marks = refs[11:15]
    unit_ref, inv_ref, vec_ref, first_ref, low_ref, ub_ref = refs[15:]
    hidden = ub_ref.shape[1]
    ub = ub_refs[0][...] + ub_refs[1][...] + ub_refs[2][...] + ub_refs[3][...]
    ub_ref[...] = ub[:, :hidden]
    gain = row_of(vec_ref, GAIN_ONE)
    size, width = streams[0][0].shape
    rows = 2 * size
    sums = [0.0] * 6
    for half, (two_ref, own_ref, ffn_ref) in enumerate(streams):
        here = pl.ds(half * size, size)
        grad_normed = two_ref[...] + own_ref[...]
        if half:
            grad_normed = grad_normed + chip_ref[...]
        unit = unit_ref[here, :]
        first = norm_rows_back(grad_normed, unit, inv_ref[here, 0:1], gain)
        low = first.astype(bf16)
        first_ref[here, :] = first
        low_ref[here, :] = low
        terms = [low.astype(f32), grad_normed * unit, grad_normed]
        for k in range(3):
            sums[k] = sums[k] + jnp.sum(terms[k], axis=0, keepdims=True)
            sums[k + 3] = sums[k + 3] + ffn_ref[k : k + 1, :]
    for k in range(6):
        first_ref[rows + k : rows + k + 1, :] = sums[k]
    first_ref[rows + 6 : rows + 8, :] = jnp.zeros((2, width), f32)
    first_ref[rows + 8 : rows + 9, :] = ub[:, hidden:]
    first_ref[rows + 9 : rows + 10, :] = marks[0][0:1, :] + marks[1][0:1, :]
    first_ref[rows + 10 : rows + 11, :] = marks[2][0:1, :] + marks[3][0:1, :]
    first_ref[rows + 11 : rows + 16, :] = jnp.zeros((5, width), f32)


def input_kernel(near_ref, far_ref, gk_ref, gv_ref, qw_ref, kw_ref, vw_ref, first_ref, mine_ref, away_ref):
    rows = near_ref.shape[0] // 2
    for p in range(4):
        gq_ref = (near_ref, far_ref)[p // 2]
        here = pl.ds(p * rows, rows)
        value = (
            dot_nt(gq_ref[pl.ds((p % 2) * rows, rows), :], qw_ref[...])
            + dot_nt(gk_ref[here, :], kw_ref[...])
            + dot_nt(gv_ref[here, :], vw_ref[...])
        )
        if p == 0:
            value = value + first_ref[:rows, :]
        (mine_ref, away_ref)[p % 2][pl.ds((p // 2) * rows, rows), :] = value


def chip_kernel(mine_ref, got_ref, keep_ref, send_ref):
    rows = mine_ref.shape[0] // 2
    step = 64

    @pl.loop(0, rows // step)
    def _(i):
        for p in range(2):
            here = strip(i + p * (rows // step), step)
            there = strip(i + (1 - p) * (rows // step), step)
            value = mine_ref[here, :] + got_ref[here, :]
            keep_ref[here, :] = value
            send_ref[there, :] = value


def place_kernel(meta_ref, mine_ref, other_ref, out_ref, sems):
    rows = mine_ref.shape[0] // 2
    copies = Copies(sems)
    for p, block in enumerate((0, 2, 1, 3)):
        ref = (mine_ref, other_ref)[p // 2]
        copies.start(ref.at[pl.ds((p % 2) * rows, rows), :], out_ref.at[strip(meta_ref[block], rows), :])
    copies.wait()


def round_place_kernel(meta_ref, near_ref, far_ref, out_ref, low_ref, sems):
    rows = near_ref.shape[0] // 2
    copies = Copies(sems)
    for p, block in enumerate((0, 2, 1, 3)):
        ref = (near_ref, far_ref)[p // 2]
        low_ref[p * rows : (p + 1) * rows, :] = ref[(p % 2) * rows : (p % 2 + 1) * rows, :].astype(bf16)
        copies.start(low_ref.at[pl.ds(p * rows, rows), :], out_ref.at[strip(meta_ref[block], rows), :])
    copies.wait()


def swap_core(value):
    return lax.ppermute(value, "mp", [(i, i ^ 1) for i in range(4)])


def swap_chip(value):
    return lax.ppermute(value, "mp", [(i, i ^ 2) for i in range(4)])


def gather_rows(own):
    other = swap_chip(own)
    sibling = swap_core(own)
    diagonal = swap_core(other)
    return own, sibling, other, diagonal


def bit_order_blocks(parts, order):
    bits = len(order)
    blocks = []
    for position in range(parts):
        block = 0
        for level, bit in enumerate(order):
            block |= ((position >> (bits - 1 - level)) & 1) << bit
        blocks.append(block)
    return blocks


def bit_order_columns(matrix, parts, order):
    width = matrix.shape[1] // parts
    return jnp.concatenate(
        [matrix[:, b * width : (b + 1) * width] for b in bit_order_blocks(parts, order)], axis=1
    )


def dp_swap(value, parts, bit):
    return lax.ppermute(value, "dp", [(i, i ^ (1 << bit)) for i in range(parts)])


class Sum:
    def __init__(self, parts, order, meta, line, spare=0):
        self.parts, self.order, self.meta, self.line = parts, list(order), meta, line
        self.spare = spare
        self.turned = False
        self.second = None
        self.extra = self.total = self.got = None

    def begin(self, away, total, extra=None):
        self.total, self.extra = total, extra
        self.level = 0
        self.ship(away)

    def ship(self, away):
        self.got = dp_swap(away, self.parts, self.order[self.level])
        self.level += 1

    def step(self):
        if self.got is None:
            return
        got = self.line.hold(self.got)
        self.got = None
        rows, cols = self.total.shape
        ends = self.level == len(self.order)
        riders = 0 if self.extra is None else self.extra.shape[0]
        bit = 0 if ends else self.order[self.level]
        rest = [shape(riders, cols)] if riders else []
        outputs = [shape(rows, cols)]
        if not ends:
            outputs = [shape(rows // 2 + riders + self.spare, cols), shape(rows // 2, cols)]
        if ends and self.turned and rows % 128 == 0:
            outputs = [shape(rows, cols // 2), shape(cols // 2, rows)]
        given = [self.total, got] + ([self.extra] if riders else [])
        result = whole(
            functools.partial(fold_kernel, riders, ends, bit), "fold", given, outputs + rest, scalars=self.meta
        )
        if riders:
            self.extra = result[-1]
        if ends:
            self.total = result[0]
            self.second = result[1] if len(outputs) == 2 else None
            self.line.mark(self.total)
        else:
            self.total = result[1]
            self.ship(result[0])
            self.line.mark(result[0])

    def finish(self):
        while self.got is not None:
            self.step()
        return self.total


class Line:
    def __init__(self):
        self.token = None

    def mark(self, *values):
        self.token = values

    def hold(self, *values):
        if self.token is not None:
            values = lax.optimization_barrier(tuple(values) + self.token)[: len(values)]
        return values if len(values) > 1 else values[0]


def shards(
    dp_size,
    tokens,
    doc_lengths,
    cls_pos,
    cls_count,
    q_weight,
    q_bias,
    k_weight,
    v_weight,
    v_bias,
    o_weight,
    o_bias,
    ln1_gain,
    ln1_bias,
    up_weight,
    up_bias,
    down_weight,
    down_bias,
    ln2_gain,
    ln2_bias,
    out_grad,
    pooled_grad,
):
    slot_len, width = tokens.shape
    rows = slot_len // 4
    half = 2 * rows
    head_width = q_weight.shape[1]
    rank = lax.axis_index("mp")
    place_id = lax.axis_index("dp")
    bits = dp_size.bit_length() - 1
    order_a = list(range(bits))
    order_b = [1, 0] + list(range(2, bits)) if bits > 1 else order_a
    length = doc_lengths[0]
    blocks = [rank ^ j for j in range(4)]

    line = Line()
    sizes = width // dp_size
    fixed_a = bit_order_blocks(dp_size, order_a) if sizes % 128 == 0 else None
    fixed_b = bit_order_blocks(dp_size, order_b) if sizes % 128 == 0 else None
    unit = rows // 2

    row_ids = lax.iota(jnp.int32, rows)
    positions = jnp.concatenate([row_ids + blocks[j] * rows for j in range(4)])
    bias = jnp.where(positions < length, 0.0, MASKED).astype(f32)[None, :]
    meta = jnp.concatenate(
        [
            jnp.stack(blocks).astype(jnp.int32),
            doc_lengths,
            cls_count,
            cls_pos[0],
            jnp.stack([(place_id >> bit) & 1 for bit in range(max(bits, 1))]).astype(jnp.int32),
        ]
    )
    hidden = up_bias.shape[0]

    meta, bias = lax.optimization_barrier((meta, bias))

    o_part, vectors = prepare(
        meta, o_weight, [o_bias, ln1_gain, ln1_bias, ln2_gain, ln2_bias, down_bias, up_bias]
    )
    o_got = swap_chip(o_part)
    line.mark(o_part)
    local, queries_near, queries_far, key_rows, value_rows = qkv(
        meta, line.hold(tokens), (q_weight, k_weight, v_weight), (q_bias, v_bias)
    )
    away_context, lse_far = attn_fwd(queries_far, key_rows, value_rows, bias, 256, f32)
    arrived = swap_chip(away_context)
    line.mark(away_context)
    o_got = line.hold(o_got)
    o_other = dp_swap(o_got, dp_size, 0)
    line.mark(o_got)
    up_held, down_held = line.hold(up_weight, down_weight)
    wide = whole(
        widen_kernel,
        "widen",
        [up_held, down_held, vectors],
        [shape(width + hidden + 8, width)],
        limit=20,
    )[0]
    line.mark(wide)
    wide = swap_core(wide)
    context_near, lse_near = attn_fwd(line.hold(queries_near), key_rows, value_rows, bias, 256, bf16)
    line.mark(context_near)
    if fixed_a:
        local_a, local_b = whole(
            functools.partial(order_kernel, fixed_a, fixed_b),
            "order",
            [line.hold(local)],
            [shape(slot_len, width, bf16)] * 2,
        )
    else:
        local_a = bit_order_columns(local, dp_size, order_a)
        local_b = bit_order_columns(local, dp_size, order_b)
    line.mark(local_a)
    own, sib, context_other, o_far = whole(
        project_kernel,
        "project",
        [context_near, line.hold(arrived), o_weight, o_got, line.hold(o_other)],
        [shape(rows, width), shape(rows, width), shape(half, head_width, bf16), shape(head_width, width, bf16)],
        scalars=meta,
    )
    n_a, n_b, normed, unit_one, inv_one = whole(
        first_norm_kernel,
        "first_norm",
        [own, swap_core(sib), local, vectors],
        [shape(unit, width), shape(unit, width), shape(rows, width), shape(rows, width), shape(rows, 128)],
    )
    line.mark(n_a)
    chip_a = swap_chip(n_a)
    chip_b = swap_chip(n_b)
    up_far, down_far, vectors_far = whole(
        round_kernel,
        "round",
        [line.hold(wide)],
        [shape(width, hidden, bf16), shape(hidden, width, bf16), shape(8, width)],
        limit=20,
    )
    ups = (up_weight, up_far)
    downs = (down_weight, down_far)
    both = (vectors, vectors_far)
    lo, act, slope_near, own_a, own_b = feed(True, unit, fixed_b, (0, 1), normed, ups, both, downs, ())
    line.mark(own_a)
    lo, act, slope_a, part = feed(
        False, unit, fixed_b, (2,), line.hold(chip_a), ups, both, downs, (lo, act)
    )
    got_a = swap_chip(part)
    line.mark(part)
    lo, act, slope_b, part = feed(
        False, unit, fixed_b, (3,), line.hold(chip_b), ups, both, downs, (lo, act)
    )
    got_b = swap_chip(part)
    line.mark(part)

    def back_rows(own, k, y, slope, offset, filled):
        place = k if own else 2 + k
        return back(
            own, fixed_a, offset, place, 0 if own else 2, k, meta, y, out_grad, pooled_grad[0], vectors,
            slope, downs, ups, filled,
        )

    y_a = add(own_a, line.hold(got_a))
    chip_a = swap_chip(y_a)
    *filled, back_a, ub_a, mark_a, two_a, sums_a = back_rows(True, 0, y_a, slope_near, 0, ())
    line.mark(back_a)
    y_b = add(own_b, line.hold(got_b))
    chip_b = swap_chip(y_b)
    *filled, back_b, ub_b, mark_b, two_b, sums_b = back_rows(True, 1, y_b, slope_near, unit, filled)
    line.mark(back_b)
    *filled, part, ub_c, mark_c = back_rows(False, 0, line.hold(chip_a), slope_a, 0, filled)
    got_a = swap_chip(part)
    line.mark(part)
    *filled, part, ub_d, mark_d = back_rows(False, 1, line.hold(chip_b), slope_b, 0, filled)
    got_b = swap_chip(part)
    line.mark(part)
    out_wide, grad_fed, grad_pre = filled

    def in_order(value, fixed, order):
        return value if fixed else bit_order_columns(value, dp_size, order)

    gf_cols, lo_cols = in_order(grad_fed, fixed_a, order_a), in_order(lo, fixed_b, order_b)
    down_sum = Sum(dp_size, order_a, meta, line, 0)
    up_sum = Sum(dp_size, order_b, meta, line, 0)

    def pair(side, sum_of, left, right, given=()):
        half_rows = width // 2
        return whole(
            functools.partial(pair_kernel, side, bool(given), sum_of.order[0]),
            "pair",
            [left, right, *given],
            [shape(half_rows, hidden)] * 2 if given else [shape(width, hidden)],
            scalars=meta,
        )

    down_other = pair(1, down_sum, line.hold(gf_cols), act)[0]
    down_given = swap_core(down_other)
    line.mark(down_other)
    back_a = add(back_a, line.hold(got_a))
    line.mark(back_a)
    up_other = pair(1, up_sum, lo_cols, line.hold(grad_pre))[0]
    up_given = swap_core(up_other)
    line.mark(up_other)

    down_sum.begin(*pair(0, down_sum, gf_cols, act, [line.hold(down_given)]))
    up_sum.begin(*pair(0, up_sum, lo_cols, grad_pre, [line.hold(up_given)]))

    line.mark(down_sum.total, up_sum.total)
    got_b = line.hold(got_b)
    first_ext, grad_attended_own, up_bias_own = whole(
        first_back_kernel,
        "first_norm_back",
        [two_a, back_a, sums_a, two_b, back_b, sums_b, got_b, ub_a, ub_b, ub_c, ub_d]
        + [mark_a, mark_b, mark_c, mark_d, unit_one, inv_one, vectors],
        [shape(rows + 16, width), shape(rows, width, bf16), shape(1, hidden)],
    )
    sib_ext = swap_core(first_ext)
    riders = 8 * width // head_width
    context_far_grad, grad_context_near, chip_sums, *ga_cols = whole(
        functools.partial(context_back_kernel, fixed_b),
        "context_back",
        [grad_attended_own, first_ext, sib_ext, o_weight, o_far],
        [shape(half + riders, head_width), shape(half, head_width, bf16), shape(riders, head_width)]
        + [shape(half, width, bf16)] * (2 if fixed_b else 1),
    )
    ga_cols = in_order(ga_cols[0], fixed_b, order_b)
    grad_context_far = swap_chip(context_far_grad)
    line.mark(context_far_grad)
    *o_away, o_kept = whole(
        o_kernel,
        "o_grad",
        [line.hold(ga_cols), context_other, context_near],
        [shape(width // 2, head_width)] * 2 + [shape(width, head_width)],
    )
    o_got = [swap_chip(v) for v in o_away]
    line.mark(o_kept)

    queries_near = line.hold(queries_near)
    grad_q_near, key_sum, value_sum = attn_bwd(
        queries_near, grad_context_near, key_rows, value_rows, bias, lse_near, 256
    )
    line.mark(grad_q_near)
    grad_context_far = line.hold(grad_context_far)
    line.mark(grad_context_far)
    queries_far = line.hold(queries_far)
    grad_q_far, grad_k, grad_v = attn_bwd(
        queries_far, grad_context_far, key_rows, value_rows, bias, lse_far, 256, (key_sum, value_sum)
    )
    line.mark(grad_k)

    qk_sum = Sum(dp_size, order_a, meta, line)
    vo_sum = Sum(dp_size, order_b, meta, line)
    vo_sum.turned = True
    riders = 8 * width // head_width
    extra_rows = -(-(riders // 2 + 1 + hidden // (2 * head_width)) // 8) * 8
    qk_away, qk_kept, qk_extra = whole(
        functools.partial(qk_kernel, qk_sum.order[0]),
        "qk_grad",
        [local_a, line.hold(grad_q_near), grad_q_far, grad_k, grad_v, chip_sums, grad_context_far]
        + [up_bias_own, sib_ext],
        [
            shape(width // 2 + extra_rows, 2 * head_width),
            shape(width // 2, 2 * head_width),
            shape(extra_rows, 2 * head_width),
        ],
        scalars=meta,
    )
    line.mark(qk_away)
    o_got = line.hold(*o_got)
    line.mark(*o_got)
    down_sum.step()
    in_mine, in_away = whole(
        input_kernel,
        "input_grad",
        [line.hold(grad_q_near), grad_q_far, grad_k, grad_v, q_weight, k_weight, v_weight, first_ext],
        [shape(half, width)] * 2,
    )
    line.mark(in_mine)
    up_sum.step()
    in_got = swap_core(in_away)
    out_far = swap_core(line.hold(out_wide))
    in_kept, in_sent = whole(
        chip_kernel, "chip_sum", [in_mine, line.hold(in_got)], [shape(half, width)] * 2
    )
    in_got = swap_chip(in_sent)
    line.mark(in_sent)
    out = whole(
        round_place_kernel,
        "round_place",
        [out_wide, line.hold(out_far)],
        [],
        scalars=meta,
        filled=[shape(slot_len, width, bf16)],
        scratch=[pltpu.VMEM((slot_len, width), bf16)],
        sems=4,
        far=True,
    )[0]
    line.mark(out)
    vo_away, vo_kept = whole(
        functools.partial(vo_kernel, vo_sum.order[0]),
        "vo_grad",
        [local_b, line.hold(grad_v), o_kept, *o_got],
        [shape(width // 2, 2 * head_width)] * 2,
        scalars=meta,
    )
    line.mark(vo_away)
    down_sum.step()
    up_sum.step()
    qk_sum.begin(line.hold(qk_away), qk_kept, qk_extra)
    vo_sum.begin(line.hold(vo_away), vo_kept)
    for bit in range(bits):
        qk_sum.step()
        if bit == 0:
            down_sum.step()
            up_sum.step()
        vo_sum.step()
        if bit > 1:
            down_sum.step()
            up_sum.step()
        if bit == min(1, bits - 1):
            in_final = add(in_kept, line.hold(in_got))
            in_other = swap_core(in_final)
            line.mark(in_final)
            in_grad = whole(
                place_kernel,
                "place",
                [in_final, line.hold(in_other)],
                [],
                scalars=meta,
                filled=[shape(slot_len, width)],
                sems=4,
                far=True,
            )[0]
            line.mark(in_grad)
    qk_total, vo_total = qk_sum.finish(), vo_sum.finish()
    riding = qk_sum.extra
    row = riders // 2
    shared = jnp.concatenate([riding[:row, :head_width], riding[:row, head_width:]], axis=0)
    shared = shared.reshape(-1, 8, head_width).transpose(1, 0, 2).reshape(8, width)
    biases = riding[row].reshape(2, head_width)
    up_bias_sum = riding[row + 1 : row + 1 + hidden // (2 * head_width)].reshape(-1)
    if vo_sum.second is None:
        v_sum, o_sum = vo_total[:, :head_width], vo_total[:, head_width:].T
    else:
        v_sum, o_sum = vo_total, vo_sum.second
    down_sum = down_sum.finish().T
    up_sum = up_sum.finish()

    mine = first_ext[rows + 9 : rows + 11]
    theirs = sib_ext[rows + 9 : rows + 11]
    marks = jnp.concatenate([mine[:1], theirs[:1], mine[1:], theirs[1:]], axis=0)
    pooled = jnp.concatenate(
        [lax.dynamic_index_in_dim(marks, blocks[j], keepdims=True) for j in range(4)], axis=0
    )[None]
    return (
        out,
        pooled,
        in_grad,
        qk_total[:, :head_width],
        biases[0],
        qk_total[:, head_width:],
        v_sum,
        biases[1],
        o_sum,
        shared[0],
        shared[1],
        shared[2],
        up_sum,
        up_bias_sum,
        down_sum,
        shared[3],
        shared[4],
        shared[5],
    )


def solution(mesh):
    return jax.shard_map(
        functools.partial(shards, mesh.shape["dp"]),
        mesh=mesh,
        in_specs=(
            P("dp", None),
            P("dp"),
            P("dp", None),
            P("dp"),
            P(None, "mp"),
            P("mp"),
            P(None, "mp"),
            P(None, "mp"),
            P("mp"),
            P("mp", None),
            P(),
            P(),
            P(),
            P(None, "mp"),
            P("mp"),
            P("mp", None),
            P(),
            P(),
            P(),
            P("dp", None),
            P("dp", None, None),
        ),
        out_specs=(
            P("dp", None),
            P("dp", None, None),
            P("dp", None),
            P("dp", "mp"),
            P("mp"),
            P("dp", "mp"),
            P("dp", "mp"),
            P("mp"),
            P("mp", "dp"),
            P(),
            P(),
            P(),
            P("dp", "mp"),
            P("mp"),
            P("mp", "dp"),
            P(),
            P(),
            P(),
        ),
        check_vma=False,
    )
```

```python
import functools

import jax
import jax.numpy as jnp
from jax import lax
from jax.experimental import pallas as pl
from jax.experimental.pallas import tpu as pltpu
from jax.sharding import PartitionSpec as P

HEAD_DIM = 64
NORM_EPS = 1e-05
ROOT_HALF = 0.7071067811865476
INV_ROOT_TAU = 0.3989422804014327
LOG2E = 1.4426950408889634
SCORE_SCALE = 0.125 * LOG2E
MASKED = -1e30

f32 = jnp.float32
bf16 = jnp.bfloat16
VMEM_LIMIT = 20 * 1024 * 1024


def dot_nn(a, b):
    return lax.dot_general(a, b, (((1,), (0,)), ((), ())), preferred_element_type=f32)


def dot_nt(a, b):
    return lax.dot_general(a, b, (((1,), (1,)), ((), ())), preferred_element_type=f32)


def dot_tn(a, b):
    return lax.dot_general(a, b, (((0,), (0,)), ((), ())), preferred_element_type=f32)


def attn_fwd_kernel(q_ref, k_ref, v_ref, bias_ref, o_ref, lse_ref):
    rows, width = q_ref.shape
    heads = width // HEAD_DIM
    lane = lax.broadcasted_iota(jnp.int32, (1, width), 1) // HEAD_DIM
    lse_lane = lax.broadcasted_iota(jnp.int32, (1, 128), 1)
    q = q_ref[...]
    k = k_ref[...]
    v = v_ref[...]
    bias = bias_ref[...]
    out = jnp.zeros((rows, width), f32)
    lse = jnp.zeros((rows, 128), f32)
    for h in range(heads):
        qh = jnp.where(lane == h, q, jnp.zeros_like(q))
        s = dot_nt(qh, k) * SCORE_SCALE + bias
        top = jnp.max(s, axis=1, keepdims=True)
        e = jnp.exp2(s - top)
        total = jnp.sum(e, axis=1, keepdims=True)
        p = (e * (1.0 / total)).astype(bf16)
        c = dot_nn(p, v)
        out = jnp.where(lane == h, c, out)
        lse = jnp.where(lse_lane == h, top + jnp.log2(total), lse)
    o_ref[...] = out.astype(o_ref.dtype)
    lse_ref[...] = lse


def attn_fwd(q, k, v, bias, block, dtype):
    rows, width = q.shape
    keys = k.shape[0]
    full = pl.BlockSpec((keys, width), lambda i: (0, 0))
    return pl.pallas_call(
        attn_fwd_kernel,
        grid=(rows // block,),
        in_specs=[
            pl.BlockSpec((block, width), lambda i: (i, 0)),
            full,
            full,
            pl.BlockSpec((1, keys), lambda i: (0, 0)),
        ],
        out_specs=[
            pl.BlockSpec((block, width), lambda i: (i, 0)),
            pl.BlockSpec((block, 128), lambda i: (i, 0)),
        ],
        out_shape=[
            jax.ShapeDtypeStruct((rows, width), dtype),
            jax.ShapeDtypeStruct((rows, 128), f32),
        ],
        compiler_params=pltpu.CompilerParams(vmem_limit_bytes=VMEM_LIMIT),
        cost_estimate=pl.CostEstimate(flops=1024, bytes_accessed=1024, transcendentals=0),
        name="attn_fwd",
    )(q, k, v, bias)


def attn_bwd_kernel(carried, *refs):
    q_ref, g_ref, k_ref, v_ref, bias_ref, lse_ref = refs[:6]
    refs = refs[6:]
    if carried:
        gk_in, gv_in = refs[:2]
        refs = refs[2:]
    gq_ref, gk_ref, gv_ref, gk_acc, gv_acc, gq_acc = refs
    step = pl.program_id(0)
    width = q_ref.shape[1]
    lane = lax.broadcasted_iota(jnp.int32, (1, width), 1) // HEAD_DIM
    lse_lane = lax.broadcasted_iota(jnp.int32, (1, 128), 1)

    @pl.when(step == 0)
    def _():
        gk_acc[...] = gk_in[...] if carried else jnp.zeros_like(gk_acc)
        gv_acc[...] = gv_in[...] if carried else jnp.zeros_like(gv_acc)

    @pl.loop(0, width // HEAD_DIM)
    def _(h):
        mine = lane == h
        zero = jnp.zeros(q_ref.shape, bf16)
        qh = jnp.where(mine, q_ref[...], zero)
        gh = jnp.where(mine, g_ref[...].astype(bf16), zero)
        lse = jnp.sum(jnp.where(lse_lane == h, lse_ref[...], 0.0), axis=1, keepdims=True)
        s = dot_nt(qh, k_ref[...]) * SCORE_SCALE + bias_ref[...]
        p = jnp.exp2(s - lse)
        dp = dot_nt(gh, v_ref[...])
        inner = jnp.sum(p * dp, axis=1, keepdims=True)
        ds = (p * (dp - inner)).astype(bf16)
        gq_acc[...] = jnp.where(mine, dot_nn(ds, k_ref[...]), gq_acc[...])
        gk_acc[...] += dot_tn(ds, qh)
        gv_acc[...] += dot_tn(p.astype(bf16), gh)

    gq_ref[...] = (gq_acc[...] * 0.125).astype(bf16)

    @pl.when(step == pl.num_programs(0) - 1)
    def _():
        scale = 0.125 if carried else 1.0
        gk_ref[...] = (gk_acc[...] * scale).astype(gk_ref.dtype)
        gv_ref[...] = gv_acc[...].astype(gv_ref.dtype)


def attn_bwd(q, g, k, v, bias, lse, block, sums=()):
    rows, width = q.shape
    keys = k.shape[0]
    full = pl.BlockSpec((keys, width), lambda i: (0, 0))
    part = pl.BlockSpec((block, width), lambda i: (i, 0))
    sum_type = bf16 if sums else f32
    return pl.pallas_call(
        functools.partial(attn_bwd_kernel, bool(sums)),
        grid=(rows // block,),
        in_specs=[
            part,
            part,
            full,
            full,
            pl.BlockSpec((1, keys), lambda i: (0, 0)),
            pl.BlockSpec((block, 128), lambda i: (i, 0)),
        ]
        + [full] * len(sums),
        out_specs=[part, full, full],
        out_shape=[
            jax.ShapeDtypeStruct((rows, width), bf16),
            jax.ShapeDtypeStruct((keys, width), sum_type),
            jax.ShapeDtypeStruct((keys, width), sum_type),
        ],
        scratch_shapes=[pltpu.VMEM((keys, width), f32)] * 2 + [pltpu.VMEM((block, width), f32)],
        compiler_params=pltpu.CompilerParams(vmem_limit_bytes=VMEM_LIMIT),
        cost_estimate=pl.CostEstimate(flops=1024, bytes_accessed=1024, transcendentals=0),
        name="attn_bwd",
    )(q, g, k, v, bias, lse, *sums)


in_vmem = pl.BlockSpec(memory_space=pltpu.VMEM)
STRIP = 256
LENGTH, COUNT, MARKS, BITS = 4, 5, 6, 10
O_BIAS, GAIN_ONE, SHIFT_ONE, GAIN_TWO, SHIFT_TWO, DOWN_BIAS, UP_BIAS, QV_BIAS = range(8)


def row_of(ref, index):
    return ref[index : index + 1, :]


def strip(index, size=STRIP):
    return pl.ds(pl.multiple_of(index * size, size), size)


def shape(rows, cols, dtype=f32):
    return jax.ShapeDtypeStruct((rows, cols), dtype)


def whole(kernel, name, inputs, outputs, scalars=None, filled=(), sems=0, scratch=(), limit=8, far=False):
    lead = [] if scalars is None else [scalars]
    anywhere = pl.BlockSpec(memory_space=pl.ANY)
    given = [v for v in filled if not isinstance(v, jax.ShapeDtypeStruct)]
    begun = [jax.ShapeDtypeStruct(v.shape, v.dtype) for v in filled]
    first = len(lead) + len(inputs)
    return pl.pallas_call(
        kernel,
        in_specs=[pl.BlockSpec(memory_space=pltpu.SMEM)] * len(lead)
        + [in_vmem] * len(inputs)
        + [anywhere] * len(given),
        out_specs=[pl.BlockSpec(memory_space=pltpu.HBM) if far else anywhere] * len(begun)
        + [in_vmem] * len(outputs),
        out_shape=begun + list(outputs),
        scratch_shapes=list(scratch) + ([pltpu.SemaphoreType.DMA((sems,))] if sems else []),
        input_output_aliases={first + p: p for p in range(len(given))},
        compiler_params=pltpu.CompilerParams(vmem_limit_bytes=limit * 1024 * 1024),
        cost_estimate=pl.CostEstimate(flops=1024, bytes_accessed=1024, transcendentals=0),
        name=name,
    )(*lead, *inputs, *given)


class Copies:
    def __init__(self, sems):
        self.sems, self.made = sems, []

    def start(self, source, target):
        copy = pltpu.make_async_copy(source, target, self.sems.at[len(self.made)])
        copy.start()
        self.made.append(copy)

    def wait(self):
        for copy in self.made:
            copy.wait()


def project_kernel(meta_ref, near_ref, other_ref, o_near_ref, o_got_ref, o_other_ref, own_ref, sib_ref, low_ref, o_far_ref):
    rows = own_ref.shape[0]
    part = o_got_ref.shape[0]
    first = meta_ref[BITS] == 0
    o_far_ref[:part, :] = jnp.where(first, o_got_ref[...], o_other_ref[...]).astype(bf16)
    o_far_ref[part:, :] = jnp.where(first, o_other_ref[...], o_got_ref[...]).astype(bf16)
    low_ref[...] = other_ref[...].astype(bf16)
    both = dot_nn(near_ref[...], o_near_ref[...]) + dot_nn(low_ref[...], o_far_ref[...])
    own_ref[...] = both[:rows]
    sib_ref[...] = both[rows:]


def mean_of(values):
    return jnp.sum(values, axis=-1, keepdims=True) * (1.0 / values.shape[-1])


def norm_rows(values):
    centre = values - mean_of(values)
    scale_inv = lax.rsqrt(mean_of(centre * centre) + NORM_EPS)
    return centre * scale_inv, scale_inv


def norm_rows_back(grad_rows, unit_rows, scale_inv, gain):
    scaled = grad_rows * gain
    return scale_inv * (scaled - mean_of(scaled) - unit_rows * mean_of(scaled * unit_rows))


def first_norm_kernel(own_ref, near_ref, tok_ref, vec_ref, na_ref, nb_ref, all_ref, unit_ref, inv_ref):
    gain = row_of(vec_ref, GAIN_ONE)
    shift = row_of(vec_ref, SHIFT_ONE)
    for half, out_ref in enumerate((na_ref, nb_ref)):
        size = out_ref.shape[0]
        rows = pl.ds(half * size, size)
        values = tok_ref[rows, :].astype(f32) + (own_ref[rows, :] + near_ref[rows, :] + row_of(vec_ref, O_BIAS))
        unit, scale_inv = norm_rows(values)
        unit_ref[rows, :] = unit
        inv_ref[rows, :] = jnp.broadcast_to(scale_inv, (size, inv_ref.shape[1]))
        normed = unit * gain + shift
        out_ref[...] = normed
        all_ref[rows, :] = normed


def move_columns(source, target, blocks):
    wide = source.shape[1] // len(blocks)
    for place, block in enumerate(blocks):
        target[:, place * wide : (place + 1) * wide] = source[:, block * wide : (block + 1) * wide]


def order_kernel(blocks_a, blocks_b, in_ref, a_ref, b_ref):
    move_columns(in_ref, a_ref, blocks_a)
    move_columns(in_ref, b_ref, blocks_b)


def prepare_kernel(meta_ref, o_ref, *refs):
    given = refs[:7]
    part_ref, vec_ref, o_in = refs[7:10]
    lines = refs[10:17]
    sems = refs[17]
    copies = Copies(sems)
    copies.start(o_ref.at[strip(meta_ref[BITS], part_ref.shape[0]), :], o_in)
    for line_ref, vector_ref in zip(lines, given):
        copies.start(vector_ref, line_ref)
    copies.wait()
    part_ref[...] = o_in[...].astype(f32)
    vec_ref[...] = jnp.zeros_like(vec_ref)
    for k, line_ref in enumerate(lines):
        vec_ref[k, :] = line_ref[...].astype(f32)


def prepare(meta, o_weight, vectors):
    rows, width = o_weight.shape
    far = pl.BlockSpec(memory_space=pltpu.HBM)
    return pl.pallas_call(
        prepare_kernel,
        in_specs=[pl.BlockSpec(memory_space=pltpu.SMEM)] + [far] * 8,
        out_specs=[in_vmem] * 2,
        out_shape=[shape(rows // 2, width), shape(8, width)],
        scratch_shapes=[pltpu.VMEM((rows // 2, width), bf16)]
        + [pltpu.VMEM((width,), bf16)] * 7
        + [pltpu.SemaphoreType.DMA((8,))],
        compiler_params=pltpu.CompilerParams(vmem_limit_bytes=60 * 1024 * 1024),
        cost_estimate=pl.CostEstimate(flops=1024, bytes_accessed=1024, transcendentals=0),
        name="prepare",
    )(meta, o_weight, *vectors)


def widen_kernel(a_ref, b_ref, vec_ref, wide_ref):
    rows = a_ref.shape[0]
    step = 64

    @pl.loop(0, rows // step)
    def _(i):
        wide_ref[strip(i, step), :] = a_ref[strip(i, step), :].astype(f32)

    @pl.loop(0, b_ref.shape[0] // step)
    def _(i):
        wide_ref[strip(i + rows // step, step), :] = b_ref[strip(i, step), :].astype(f32)

    wide_ref[rows + b_ref.shape[0] :, :] = vec_ref[...]


def qkv_kernel(meta_ref, all_ref, qw_ref, kw_ref, vw_ref, *refs):
    given = refs[:2]
    vec_ref, local_ref, near_ref, far_ref, k_ref, v_ref, q_in, k_in, v_in, qb_in, vb_in, sems = refs[2:]
    half, wide = near_ref.shape
    rows = half // 2
    copies = Copies(sems)
    copies.start(given[0], qb_in)
    copies.start(given[1], vb_in)
    for p in range(4):
        copies.start(all_ref.at[strip(meta_ref[p], rows), :], local_ref.at[pl.ds(p * rows, rows), :])
    copies.start(kw_ref, k_in)
    copies.start(qw_ref, q_in)
    copies.start(vw_ref, v_in)
    copies.wait()
    k_ref[...] = dot_nn(local_ref[...], k_in[...]).astype(bf16)
    vec_ref[0, :] = qb_in[...].astype(f32)
    vec_ref[1, :] = vb_in[...].astype(f32)
    q = (dot_nn(local_ref[...], q_in[...]) + vec_ref[0:1, :]).astype(bf16)
    near_ref[...] = q[:half]
    far_ref[...] = q[half:]
    v_ref[...] = (dot_nn(local_ref[...], v_in[...]) + vec_ref[1:2, :]).astype(bf16)


def qkv(meta, tokens, weights, biases):
    rows, width = tokens.shape
    wide = weights[0].shape[1]
    far = pl.BlockSpec(memory_space=pltpu.HBM)
    return pl.pallas_call(
        qkv_kernel,
        in_specs=[pl.BlockSpec(memory_space=pltpu.SMEM)] + [far] * 6,
        out_specs=[in_vmem] * 6,
        out_shape=[shape(8, wide), shape(rows, width, bf16)]
        + [shape(rows // 2, wide, bf16)] * 2
        + [shape(rows, wide, bf16)] * 2,
        scratch_shapes=[pltpu.VMEM((width, wide), bf16)] * 3
        + [pltpu.VMEM((wide,), bf16)] * 2
        + [pltpu.SemaphoreType.DMA((9,))],
        compiler_params=pltpu.CompilerParams(vmem_limit_bytes=58 * 1024 * 1024),
        cost_estimate=pl.CostEstimate(flops=1024, bytes_accessed=1024, transcendentals=0),
        name="qkv",
    )(meta, tokens, *weights, *biases)[1:]


def add_kernel(*refs):
    step = 64

    @pl.loop(0, refs[0].shape[0] // step)
    def _(i):
        here = strip(i, step)
        total = refs[0][here, :]
        for ref in refs[1:-1]:
            total = total + ref[here, :]
        refs[-1][here, :] = total


def add(*values):
    return whole(add_kernel, "add", list(values), [shape(*values[0].shape)])[0]


def pair_kernel(side, fill, bit, meta_ref, left_ref, right_ref, *refs):
    mine = meta_ref[BITS + bit]
    half = left_ref.shape[1] // 2
    hidden = right_ref.shape[1] // 2
    right = right_ref[:, side * hidden : (side + 1) * hidden]
    for kept in range(2):
        start = pl.multiple_of((mine if kept else 1 - mine) * half, 128)
        value = dot_tn(left_ref[:, pl.ds(start, half)], right)
        if fill:
            refs[1 + kept][...] = value + refs[0][kept * half : (kept + 1) * half, :]
        else:
            refs[0][kept * half : (kept + 1) * half, :] = value


def fold_kernel(riders, ends, bit, meta_ref, total_ref, got_ref, *refs):
    rows = total_ref.shape[0]
    if riders:
        extra_ref = refs[0]
        refs = refs[1:]
        extra = extra_ref[...] + got_ref[rows:, :]
    if ends and len(refs) == 2 and not riders:
        wide = total_ref.shape[1] // 2
        refs[0][...] = total_ref[:, :wide] + got_ref[:rows, :wide]
        refs[1][...] = (total_ref[:, wide:] + got_ref[:rows, wide:]).T
        return
    if ends:
        refs[0][...] = total_ref[...] + got_ref[:rows, :]
        if riders:
            refs[1][...] = extra
        return
    half = rows // 2
    mine = meta_ref[BITS + bit]
    step = min(64, half)

    @pl.loop(0, half // step)
    def _(i):
        away = strip((1 - mine) * (half // step) + i, step)
        kept = strip(mine * (half // step) + i, step)
        refs[0][strip(i, step), :] = total_ref[away, :] + got_ref[away, :]
        refs[1][strip(i, step), :] = total_ref[kept, :] + got_ref[kept, :]

    if riders:
        refs[0][half:, :] = extra
        refs[2][...] = extra
    elif refs[0].shape[0] > half:
        refs[0][half:, :] = jnp.zeros((refs[0].shape[0] - half, refs[0].shape[1]), f32)


def qk_kernel(bit, meta_ref, left_ref, near_ref, far_ref, gk_ref, gv_ref, chip_ref, far_sums_ref, ub_ref, sib_ref, away_ref, kept_ref, extra_ref):
    mine = meta_ref[BITS + bit]
    half = left_ref.shape[1] // 2
    rows = near_ref.shape[0]
    wide = near_ref.shape[1]
    riders = chip_ref.shape[0]
    extra_ref[...] = jnp.zeros_like(extra_ref)
    shared = chip_ref[...] + far_sums_ref[far_sums_ref.shape[0] - riders :, :]
    extra_ref[: riders // 2, :wide] = shared[: riders // 2]
    extra_ref[: riders // 2, wide:] = shared[riders // 2 :]
    row = riders // 2
    query_sum = jnp.sum(near_ref[...].astype(f32), axis=0, keepdims=True)
    extra_ref[row : row + 1, :wide] = query_sum + jnp.sum(far_ref[...].astype(f32), axis=0, keepdims=True)
    extra_ref[row : row + 1, wide:] = jnp.sum(gv_ref[...].astype(f32), axis=0, keepdims=True)
    place = sib_ref.shape[0] - 8
    for k in range(ub_ref.shape[1] // (2 * wide)):
        cols = slice(2 * k * wide, 2 * (k + 1) * wide)
        extra_ref[row + 1 + k : row + 2 + k, :] = ub_ref[:, cols] + sib_ref[place : place + 1, cols]
    for kept, ref in enumerate((away_ref, kept_ref)):
        cols = pl.ds(pl.multiple_of((mine if kept else 1 - mine) * half, 128), half)
        ref[:half, :wide] = dot_tn(left_ref[:rows, cols], near_ref[...]) + dot_tn(left_ref[rows:, cols], far_ref[...])
        ref[:half, wide:] = dot_tn(left_ref[:, cols], gk_ref[...])
    away_ref[half:, :] = extra_ref[...]


def vo_kernel(bit, meta_ref, left_ref, gv_ref, kept_o_ref, got_a_ref, got_b_ref, away_ref, kept_ref):
    mine = meta_ref[BITS + bit]
    half = left_ref.shape[1] // 2
    wide = gv_ref.shape[1]
    for kept, ref in enumerate((away_ref, kept_ref)):
        start = pl.multiple_of((mine if kept else 1 - mine) * half, 128)
        ref[:, :wide] = dot_tn(left_ref[:, pl.ds(start, half)], gv_ref[...])
        rows = pl.ds(start, half)
        top = jnp.where(start == 0, got_a_ref[...], got_b_ref[...])
        ref[:, wide:] = kept_o_ref[rows, :] + top


def o_kernel(cols_ref, other_ref, near_ref, first_ref, second_ref, kept_ref):
    half = first_ref.shape[0]
    first_ref[...] = dot_tn(cols_ref[:, :half], other_ref[...])
    second_ref[...] = dot_tn(cols_ref[:, half:], other_ref[...])
    kept_ref[...] = dot_tn(cols_ref[...], near_ref[...])


def round_kernel(wide_ref, a_ref, b_ref, vec_ref):
    rows = a_ref.shape[0]
    step = 64

    @pl.loop(0, rows // step)
    def _(i):
        a_ref[strip(i, step), :] = wide_ref[strip(i, step), :].astype(bf16)

    @pl.loop(0, b_ref.shape[0] // step)
    def _(i):
        b_ref[strip(i, step), :] = wide_ref[strip(i + rows // step, step), :].astype(bf16)

    vec_ref[...] = wide_ref[rows + b_ref.shape[0] :, :]


def feed_kernel(own, unit, blocks, targets, fresh, *refs):
    in_ref, up_ref, up2_ref, vec_ref, vec2_ref, down_ref, down2_ref = refs[:7]
    refs = refs[7 + (0 if fresh else 2) :]
    lo_full, act_full, slope_ref = refs[:3]
    parts = refs[3:-4]
    low_ref, act_ref, cols_ref, sems = refs[-4:]
    hidden = up_ref.shape[1]
    copies = Copies(sems)
    low_ref[...] = in_ref[...].astype(bf16)
    if blocks:
        move_columns(low_ref, cols_ref, blocks)
    else:
        cols_ref[...] = low_ref[...]
    for p, target in enumerate(targets):
        copies.start(cols_ref.at[pl.ds(p * unit, unit), :], lo_full.at[pl.ds(target * unit, unit), :])
    for side, (weight_ref, bias_ref) in enumerate(((up_ref, vec_ref), (up2_ref, vec2_ref))):

        @pl.loop(0, hidden // STRIP)
        def _(i):
            there = strip(i + side * (hidden // STRIP))
            pre = dot_nn(low_ref[...], weight_ref[:, strip(i)]) + bias_ref[UP_BIAS : UP_BIAS + 1, strip(i)]
            normal_cdf = 0.5 * (1.0 + lax.erf(pre * ROOT_HALF))
            density = jnp.exp(-0.5 * pre * pre) * INV_ROOT_TAU
            act_ref[:, there] = (pre * normal_cdf).astype(bf16)
            slope_ref[:, there] = normal_cdf + pre * density

    for p, target in enumerate(targets):
        copies.start(act_ref.at[pl.ds(p * unit, unit), :], act_full.at[pl.ds(target * unit, unit), :])

    @pl.loop(0, down_ref.shape[1] // STRIP)
    def _(i):
        cols = strip(i)
        part = dot_nn(act_ref[:, :hidden], down_ref[:, cols]) + dot_nn(act_ref[:, hidden:], down2_ref[:, cols])
        if own:
            part = part + (in_ref[:, cols] + vec_ref[DOWN_BIAS : DOWN_BIAS + 1, cols])
        for p, part_ref in enumerate(parts):
            part_ref[:, cols] = part[p * unit : (p + 1) * unit]

    copies.wait()


def feed(own, unit, blocks, targets, rows_in, ups, vectors, downs, filled):
    rows, width = rows_in.shape
    hidden = 2 * ups[0].shape[1]
    return whole(
        functools.partial(feed_kernel, own, unit, blocks, targets, not filled),
        "feed",
        [rows_in, *ups, *vectors, *downs],
        [shape(rows, hidden)] + [shape(unit, width)] * len(targets),
        filled=filled or [shape(4 * unit, width, bf16), shape(4 * unit, hidden, bf16)],
        scratch=[
            pltpu.VMEM((rows, width), bf16),
            pltpu.VMEM((rows, hidden), bf16),
            pltpu.VMEM((rows, width), bf16),
        ],
        sems=2 * len(targets),
    )


def back_kernel(own, blocks, offset, target, fresh, block, part, meta_ref, y_ref, og_ref, extra_ref, vec_ref, slope_ref, down_ref, down2_ref, up_ref, up2_ref, *refs):
    refs = refs[0 if fresh else 3 :]
    out_full, gf_full, gp_full, part_ref, ub_ref, mark_ref = refs[:6]
    refs = refs[6:]
    if own:
        two_ref, sums_ref = refs[:2]
        refs = refs[2:]
    gf_ref, out_ref, gp_ref, cols_ref, sems = refs
    rows = y_ref.shape[0]
    hidden = up_ref.shape[1]
    gain = row_of(vec_ref, GAIN_TWO)
    shift = row_of(vec_ref, SHIFT_TWO)
    copies = Copies(sems)
    ids = lax.broadcasted_iota(jnp.int32, (rows, 1), 0)
    number = meta_ref[block]
    base = pl.multiple_of((2 * number + part) * rows, rows)
    limit = meta_ref[LENGTH] - base
    spot = jnp.where(number < meta_ref[COUNT], meta_ref[MARKS + number] - base, -1)
    there = pl.ds(target * rows, rows)
    keep = (ids < limit).astype(f32)
    unit, scale_inv = norm_rows(y_ref[...])
    out_ref[...] = (unit * gain + shift) * keep
    copies.start(out_ref, out_full.at[there, :])
    grad_out = (og_ref[pl.ds(base, rows), :].astype(f32) + jnp.where(ids == spot, extra_ref[pl.ds(number, 1), :], 0.0)) * keep
    grad_two = norm_rows_back(grad_out, unit, scale_inv, gain)
    grad_low = grad_two.astype(bf16)
    gf_ref[...] = grad_low
    if own:
        two_ref[...] = grad_two
        sums_ref[0:1, :] = jnp.sum(grad_low.astype(f32), axis=0, keepdims=True)
        sums_ref[1:2, :] = jnp.sum(grad_out * unit, axis=0, keepdims=True)
        sums_ref[2:3, :] = jnp.sum(grad_out, axis=0, keepdims=True)
        sums_ref[3:8, :] = jnp.zeros((5, sums_ref.shape[1]), f32)
    mark_ref[...] = jnp.zeros_like(mark_ref)

    @pl.when((spot >= 0) & (spot < rows))
    def _():
        row, _ = norm_rows(y_ref[pl.ds(jnp.clip(spot, 0, rows - 1), 1), :])
        mark_ref[0:1, :] = row * gain + shift

    if blocks:
        move_columns(gf_ref, cols_ref, blocks)
    else:
        cols_ref[...] = gf_ref[...]
    copies.start(cols_ref, gf_full.at[there, :])
    for side, weight_ref in enumerate((down_ref, down2_ref)):

        @pl.loop(0, hidden // STRIP)
        def _(i):
            cols = strip(i + side * (hidden // STRIP))
            grad_act = dot_nt(gf_ref[...], weight_ref[strip(i), :])
            grad_pre = (grad_act * slope_ref[pl.ds(offset, rows), cols]).astype(bf16)
            gp_ref[:, cols] = grad_pre
            ub_ref[:, cols] = jnp.sum(grad_pre.astype(f32), axis=0, keepdims=True)

    copies.start(gp_ref, gp_full.at[there, :])

    @pl.loop(0, up_ref.shape[0] // STRIP)
    def _(i):
        cols = strip(i)
        part_ref[:, cols] = dot_nt(gp_ref[:, :hidden], up_ref[cols, :]) + dot_nt(gp_ref[:, hidden:], up2_ref[cols, :])

    copies.wait()


def back(own, blocks, offset, target, block, part, meta, y, out_grad, extra, vectors, slope, downs, ups, filled):
    rows, width = y.shape
    hidden = 2 * ups[0].shape[1]
    outputs = [shape(rows, width), shape(1, hidden), shape(8, width)]
    if own:
        outputs += [shape(rows, width), shape(8, width)]
    return whole(
        functools.partial(back_kernel, own, blocks, offset, target, not filled, block, part),
        "feed_back",
        [y, out_grad, extra, vectors, slope, *downs, *ups],
        outputs,
        scalars=meta,
        filled=filled
        or [shape(4 * rows, width), shape(4 * rows, width, bf16), shape(4 * rows, hidden, bf16)],
        scratch=[
            pltpu.VMEM((rows, width), bf16),
            pltpu.VMEM((rows, width), f32),
            pltpu.VMEM((rows, hidden), bf16),
            pltpu.VMEM((rows, width), bf16),
        ],
        sems=3,
    )


def context_back_kernel(blocks, own_ref, first_ref, sib_ref, near_w_ref, far_w_ref, far_ref, near_ref, sums_ref, *refs):
    low_ref = refs[-1]
    rows = own_ref.shape[0]
    low_ref[:rows, :] = own_ref[...]
    low_ref[rows:, :] = sib_ref[:rows, :].astype(bf16)
    wide = far_ref.shape[1]
    far_ref[: 2 * rows, :] = dot_nt(low_ref[...], far_w_ref[...])
    near_ref[...] = dot_nt(low_ref[...], near_w_ref[...]).astype(bf16)
    for k in range(first_ref.shape[1] // wide):
        cols = slice(k * wide, (k + 1) * wide)
        chip = first_ref[rows : rows + 8, cols] + sib_ref[rows : rows + 8, cols]
        sums_ref[8 * k : 8 * k + 8, :] = chip
        far_ref[2 * rows + 8 * k : 2 * rows + 8 * k + 8, :] = chip
    if blocks:
        move_columns(low_ref, refs[0], blocks)


def first_back_kernel(*refs):
    streams = (refs[:3], refs[3:6])
    chip_ref = refs[6]
    ub_refs = refs[7:11]
    marks = refs[11:15]
    unit_ref, inv_ref, vec_ref, first_ref, low_ref, ub_ref = refs[15:]
    hidden = ub_ref.shape[1]
    ub = ub_refs[0][...] + ub_refs[1][...] + ub_refs[2][...] + ub_refs[3][...]
    ub_ref[...] = ub[:, :hidden]
    gain = row_of(vec_ref, GAIN_ONE)
    size, width = streams[0][0].shape
    rows = 2 * size
    sums = [0.0] * 6
    for half, (two_ref, own_ref, ffn_ref) in enumerate(streams):
        here = pl.ds(half * size, size)
        grad_normed = two_ref[...] + own_ref[...]
        if half:
            grad_normed = grad_normed + chip_ref[...]
        unit = unit_ref[here, :]
        first = norm_rows_back(grad_normed, unit, inv_ref[here, 0:1], gain)
        low = first.astype(bf16)
        first_ref[here, :] = first
        low_ref[here, :] = low
        terms = [low.astype(f32), grad_normed * unit, grad_normed]
        for k in range(3):
            sums[k] = sums[k] + jnp.sum(terms[k], axis=0, keepdims=True)
            sums[k + 3] = sums[k + 3] + ffn_ref[k : k + 1, :]
    for k in range(6):
        first_ref[rows + k : rows + k + 1, :] = sums[k]
    first_ref[rows + 6 : rows + 8, :] = jnp.zeros((2, width), f32)
    first_ref[rows + 8 : rows + 9, :] = ub[:, hidden:]
    first_ref[rows + 9 : rows + 10, :] = marks[0][0:1, :] + marks[1][0:1, :]
    first_ref[rows + 10 : rows + 11, :] = marks[2][0:1, :] + marks[3][0:1, :]
    first_ref[rows + 11 : rows + 16, :] = jnp.zeros((5, width), f32)


def input_kernel(near_ref, far_ref, gk_ref, gv_ref, qw_ref, kw_ref, vw_ref, first_ref, mine_ref, away_ref):
    rows = near_ref.shape[0] // 2
    for p in range(4):
        gq_ref = (near_ref, far_ref)[p // 2]
        here = pl.ds(p * rows, rows)
        value = (
            dot_nt(gq_ref[pl.ds((p % 2) * rows, rows), :], qw_ref[...])
            + dot_nt(gk_ref[here, :], kw_ref[...])
            + dot_nt(gv_ref[here, :], vw_ref[...])
        )
        if p == 0:
            value = value + first_ref[:rows, :]
        (mine_ref, away_ref)[p % 2][pl.ds((p // 2) * rows, rows), :] = value


def chip_kernel(mine_ref, got_ref, keep_ref, send_ref):
    rows = mine_ref.shape[0] // 2
    step = 64

    @pl.loop(0, rows // step)
    def _(i):
        for p in range(2):
            here = strip(i + p * (rows // step), step)
            there = strip(i + (1 - p) * (rows // step), step)
            value = mine_ref[here, :] + got_ref[here, :]
            keep_ref[here, :] = value
            send_ref[there, :] = value


def place_kernel(meta_ref, mine_ref, other_ref, out_ref, sems):
    rows = mine_ref.shape[0] // 2
    copies = Copies(sems)
    for p, block in enumerate((0, 2, 1, 3)):
        ref = (mine_ref, other_ref)[p // 2]
        copies.start(ref.at[pl.ds((p % 2) * rows, rows), :], out_ref.at[strip(meta_ref[block], rows), :])
    copies.wait()


def round_place_kernel(meta_ref, near_ref, far_ref, out_ref, low_ref, sems):
    rows = near_ref.shape[0] // 2
    copies = Copies(sems)
    for p, block in enumerate((0, 2, 1, 3)):
        ref = (near_ref, far_ref)[p // 2]
        low_ref[p * rows : (p + 1) * rows, :] = ref[(p % 2) * rows : (p % 2 + 1) * rows, :].astype(bf16)
        copies.start(low_ref.at[pl.ds(p * rows, rows), :], out_ref.at[strip(meta_ref[block], rows), :])
    copies.wait()


def swap_core(value):
    return lax.ppermute(value, "mp", [(i, i ^ 1) for i in range(4)])


def swap_chip(value):
    return lax.ppermute(value, "mp", [(i, i ^ 2) for i in range(4)])


def gather_rows(own):
    other = swap_chip(own)
    sibling = swap_core(own)
    diagonal = swap_core(other)
    return own, sibling, other, diagonal


def bit_order_blocks(parts, order):
    bits = len(order)
    blocks = []
    for position in range(parts):
        block = 0
        for level, bit in enumerate(order):
            block |= ((position >> (bits - 1 - level)) & 1) << bit
        blocks.append(block)
    return blocks


def bit_order_columns(matrix, parts, order):
    width = matrix.shape[1] // parts
    return jnp.concatenate(
        [matrix[:, b * width : (b + 1) * width] for b in bit_order_blocks(parts, order)], axis=1
    )


def dp_swap(value, parts, bit):
    return lax.ppermute(value, "dp", [(i, i ^ (1 << bit)) for i in range(parts)])


class Sum:
    def __init__(self, parts, order, meta, line, spare=0):
        self.parts, self.order, self.meta, self.line = parts, list(order), meta, line
        self.spare = spare
        self.turned = False
        self.second = None
        self.extra = self.total = self.got = None

    def begin(self, away, total, extra=None):
        self.total, self.extra = total, extra
        self.level = 0
        self.ship(away)

    def ship(self, away):
        self.got = dp_swap(away, self.parts, self.order[self.level])
        self.level += 1

    def step(self):
        if self.got is None:
            return
        got = self.line.hold(self.got)
        self.got = None
        rows, cols = self.total.shape
        ends = self.level == len(self.order)
        riders = 0 if self.extra is None else self.extra.shape[0]
        bit = 0 if ends else self.order[self.level]
        rest = [shape(riders, cols)] if riders else []
        outputs = [shape(rows, cols)]
        if not ends:
            outputs = [shape(rows // 2 + riders + self.spare, cols), shape(rows // 2, cols)]
        if ends and self.turned and rows % 128 == 0:
            outputs = [shape(rows, cols // 2), shape(cols // 2, rows)]
        given = [self.total, got] + ([self.extra] if riders else [])
        result = whole(
            functools.partial(fold_kernel, riders, ends, bit), "fold", given, outputs + rest, scalars=self.meta
        )
        if riders:
            self.extra = result[-1]
        if ends:
            self.total = result[0]
            self.second = result[1] if len(outputs) == 2 else None
            self.line.mark(self.total)
        else:
            self.total = result[1]
            self.ship(result[0])
            self.line.mark(result[0])

    def finish(self):
        while self.got is not None:
            self.step()
        return self.total


class Line:
    def __init__(self):
        self.token = None

    def mark(self, *values):
        self.token = values

    def hold(self, *values):
        if self.token is not None:
            values = lax.optimization_barrier(tuple(values) + self.token)[: len(values)]
        return values if len(values) > 1 else values[0]


def shards(
    dp_size,
    tokens,
    doc_lengths,
    cls_pos,
    cls_count,
    q_weight,
    q_bias,
    k_weight,
    v_weight,
    v_bias,
    o_weight,
    o_bias,
    ln1_gain,
    ln1_bias,
    up_weight,
    up_bias,
    down_weight,
    down_bias,
    ln2_gain,
    ln2_bias,
    out_grad,
    pooled_grad,
):
    slot_len, width = tokens.shape
    rows = slot_len // 4
    half = 2 * rows
    head_width = q_weight.shape[1]
    rank = lax.axis_index("mp")
    place_id = lax.axis_index("dp")
    bits = dp_size.bit_length() - 1
    order_a = list(range(bits))
    order_b = [1, 0] + list(range(2, bits)) if bits > 1 else order_a
    length = doc_lengths[0]
    blocks = [rank ^ j for j in range(4)]

    line = Line()
    sizes = width // dp_size
    fixed_a = bit_order_blocks(dp_size, order_a) if sizes % 128 == 0 else None
    fixed_b = bit_order_blocks(dp_size, order_b) if sizes % 128 == 0 else None
    unit = rows // 2

    row_ids = lax.iota(jnp.int32, rows)
    positions = jnp.concatenate([row_ids + blocks[j] * rows for j in range(4)])
    bias = jnp.where(positions < length, 0.0, MASKED).astype(f32)[None, :]
    meta = jnp.concatenate(
        [
            jnp.stack(blocks).astype(jnp.int32),
            doc_lengths,
            cls_count,
            cls_pos[0],
            jnp.stack([(place_id >> bit) & 1 for bit in range(max(bits, 1))]).astype(jnp.int32),
        ]
    )
    hidden = up_bias.shape[0]

    meta, bias = lax.optimization_barrier((meta, bias))

    o_part, vectors = prepare(
        meta, o_weight, [o_bias, ln1_gain, ln1_bias, ln2_gain, ln2_bias, down_bias, up_bias]
    )
    o_got = swap_chip(o_part)
    line.mark(o_part)
    local, queries_near, queries_far, key_rows, value_rows = qkv(
        meta, line.hold(tokens), (q_weight, k_weight, v_weight), (q_bias, v_bias)
    )
    away_context, lse_far = attn_fwd(queries_far, key_rows, value_rows, bias, 256, f32)
    arrived = swap_chip(away_context)
    line.mark(away_context)
    o_got = line.hold(o_got)
    o_other = dp_swap(o_got, dp_size, 0)
    line.mark(o_got)
    up_held, down_held = line.hold(up_weight, down_weight)
    wide = whole(
        widen_kernel,
        "widen",
        [up_held, down_held, vectors],
        [shape(width + hidden + 8, width)],
        limit=20,
    )[0]
    line.mark(wide)
    wide = swap_core(wide)
    context_near, lse_near = attn_fwd(line.hold(queries_near), key_rows, value_rows, bias, 256, bf16)
    line.mark(context_near)
    if fixed_a:
        local_a, local_b = whole(
            functools.partial(order_kernel, fixed_a, fixed_b),
            "order",
            [line.hold(local)],
            [shape(slot_len, width, bf16)] * 2,
        )
    else:
        local_a = bit_order_columns(local, dp_size, order_a)
        local_b = bit_order_columns(local, dp_size, order_b)
    line.mark(local_a)
    own, sib, context_other, o_far = whole(
        project_kernel,
        "project",
        [context_near, line.hold(arrived), o_weight, o_got, line.hold(o_other)],
        [shape(rows, width), shape(rows, width), shape(half, head_width, bf16), shape(head_width, width, bf16)],
        scalars=meta,
    )
    n_a, n_b, normed, unit_one, inv_one = whole(
        first_norm_kernel,
        "first_norm",
        [own, swap_core(sib), local, vectors],
        [shape(unit, width), shape(unit, width), shape(rows, width), shape(rows, width), shape(rows, 128)],
    )
    line.mark(n_a)
    chip_a = swap_chip(n_a)
    chip_b = swap_chip(n_b)
    up_far, down_far, vectors_far = whole(
        round_kernel,
        "round",
        [line.hold(wide)],
        [shape(width, hidden, bf16), shape(hidden, width, bf16), shape(8, width)],
        limit=20,
    )
    ups = (up_weight, up_far)
    downs = (down_weight, down_far)
    both = (vectors, vectors_far)
    lo, act, slope_near, own_a, own_b = feed(True, unit, fixed_b, (0, 1), normed, ups, both, downs, ())
    line.mark(own_a)
    lo, act, slope_a, part = feed(
        False, unit, fixed_b, (2,), line.hold(chip_a), ups, both, downs, (lo, act)
    )
    got_a = swap_chip(part)
    line.mark(part)
    lo, act, slope_b, part = feed(
        False, unit, fixed_b, (3,), line.hold(chip_b), ups, both, downs, (lo, act)
    )
    got_b = swap_chip(part)
    line.mark(part)

    def back_rows(own, k, y, slope, offset, filled):
        place = k if own else 2 + k
        return back(
            own, fixed_a, offset, place, 0 if own else 2, k, meta, y, out_grad, pooled_grad[0], vectors,
            slope, downs, ups, filled,
        )

    y_a = add(own_a, line.hold(got_a))
    chip_a = swap_chip(y_a)
    *filled, back_a, ub_a, mark_a, two_a, sums_a = back_rows(True, 0, y_a, slope_near, 0, ())
    line.mark(back_a)
    y_b = add(own_b, line.hold(got_b))
    chip_b = swap_chip(y_b)
    *filled, back_b, ub_b, mark_b, two_b, sums_b = back_rows(True, 1, y_b, slope_near, unit, filled)
    line.mark(back_b)
    *filled, part, ub_c, mark_c = back_rows(False, 0, line.hold(chip_a), slope_a, 0, filled)
    got_a = swap_chip(part)
    line.mark(part)
    *filled, part, ub_d, mark_d = back_rows(False, 1, line.hold(chip_b), slope_b, 0, filled)
    got_b = swap_chip(part)
    line.mark(part)
    out_wide, grad_fed, grad_pre = filled

    def in_order(value, fixed, order):
        return value if fixed else bit_order_columns(value, dp_size, order)

    gf_cols, lo_cols = in_order(grad_fed, fixed_a, order_a), in_order(lo, fixed_b, order_b)
    down_sum = Sum(dp_size, order_a, meta, line, 0)
    up_sum = Sum(dp_size, order_b, meta, line, 0)

    def pair(side, sum_of, left, right, given=()):
        half_rows = width // 2
        return whole(
            functools.partial(pair_kernel, side, bool(given), sum_of.order[0]),
            "pair",
            [left, right, *given],
            [shape(half_rows, hidden)] * 2 if given else [shape(width, hidden)],
            scalars=meta,
        )

    down_other = pair(1, down_sum, line.hold(gf_cols), act)[0]
    down_given = swap_core(down_other)
    line.mark(down_other)
    back_a = add(back_a, line.hold(got_a))
    line.mark(back_a)
    up_other = pair(1, up_sum, lo_cols, line.hold(grad_pre))[0]
    up_given = swap_core(up_other)
    line.mark(up_other)

    down_sum.begin(*pair(0, down_sum, gf_cols, act, [line.hold(down_given)]))
    up_sum.begin(*pair(0, up_sum, lo_cols, grad_pre, [line.hold(up_given)]))

    line.mark(down_sum.total, up_sum.total)
    got_b = line.hold(got_b)
    first_ext, grad_attended_own, up_bias_own = whole(
        first_back_kernel,
        "first_norm_back",
        [two_a, back_a, sums_a, two_b, back_b, sums_b, got_b, ub_a, ub_b, ub_c, ub_d]
        + [mark_a, mark_b, mark_c, mark_d, unit_one, inv_one, vectors],
        [shape(rows + 16, width), shape(rows, width, bf16), shape(1, hidden)],
    )
    sib_ext = swap_core(first_ext)
    riders = 8 * width // head_width
    context_far_grad, grad_context_near, chip_sums, *ga_cols = whole(
        functools.partial(context_back_kernel, fixed_b),
        "context_back",
        [grad_attended_own, first_ext, sib_ext, o_weight, o_far],
        [shape(half + riders, head_width), shape(half, head_width, bf16), shape(riders, head_width)]
        + [shape(half, width, bf16)] * (2 if fixed_b else 1),
    )
    ga_cols = in_order(ga_cols[0], fixed_b, order_b)
    grad_context_far = swap_chip(context_far_grad)
    line.mark(context_far_grad)
    *o_away, o_kept = whole(
        o_kernel,
        "o_grad",
        [line.hold(ga_cols), context_other, context_near],
        [shape(width // 2, head_width)] * 2 + [shape(width, head_width)],
    )
    o_got = [swap_chip(v) for v in o_away]
    line.mark(o_kept)

    queries_near = line.hold(queries_near)
    grad_q_near, key_sum, value_sum = attn_bwd(
        queries_near, grad_context_near, key_rows, value_rows, bias, lse_near, 256
    )
    line.mark(grad_q_near)
    grad_context_far = line.hold(grad_context_far)
    line.mark(grad_context_far)
    queries_far = line.hold(queries_far)
    grad_q_far, grad_k, grad_v = attn_bwd(
        queries_far, grad_context_far, key_rows, value_rows, bias, lse_far, 256, (key_sum, value_sum)
    )
    line.mark(grad_k)

    qk_sum = Sum(dp_size, order_a, meta, line)
    vo_sum = Sum(dp_size, order_b, meta, line)
    vo_sum.turned = True
    riders = 8 * width // head_width
    extra_rows = -(-(riders // 2 + 1 + hidden // (2 * head_width)) // 8) * 8
    qk_away, qk_kept, qk_extra = whole(
        functools.partial(qk_kernel, qk_sum.order[0]),
        "qk_grad",
        [local_a, line.hold(grad_q_near), grad_q_far, grad_k, grad_v, chip_sums, grad_context_far]
        + [up_bias_own, sib_ext],
        [
            shape(width // 2 + extra_rows, 2 * head_width),
            shape(width // 2, 2 * head_width),
            shape(extra_rows, 2 * head_width),
        ],
        scalars=meta,
    )
    line.mark(qk_away)
    o_got = line.hold(*o_got)
    line.mark(*o_got)
    down_sum.step()
    up_sum.step()
    in_mine, in_away = whole(
        input_kernel,
        "input_grad",
        [line.hold(grad_q_near), grad_q_far, grad_k, grad_v, q_weight, k_weight, v_weight, first_ext],
        [shape(half, width)] * 2,
    )
    in_got = swap_core(in_away)
    out_far = swap_core(line.hold(out_wide))
    line.mark(in_mine)
    in_kept, in_sent = whole(
        chip_kernel, "chip_sum", [in_mine, line.hold(in_got)], [shape(half, width)] * 2
    )
    in_got = swap_chip(in_sent)
    line.mark(in_sent)
    out = whole(
        round_place_kernel,
        "round_place",
        [out_wide, line.hold(out_far)],
        [],
        scalars=meta,
        filled=[shape(slot_len, width, bf16)],
        scratch=[pltpu.VMEM((slot_len, width), bf16)],
        sems=4,
        far=True,
    )[0]
    line.mark(out)
    vo_away, vo_kept = whole(
        functools.partial(vo_kernel, vo_sum.order[0]),
        "vo_grad",
        [local_b, line.hold(grad_v), o_kept, *o_got],
        [shape(width // 2, 2 * head_width)] * 2,
        scalars=meta,
    )
    line.mark(vo_away)
    down_sum.step()
    up_sum.step()
    qk_sum.begin(line.hold(qk_away), qk_kept, qk_extra)
    vo_sum.begin(line.hold(vo_away), vo_kept)
    for bit in range(bits):
        qk_sum.step()
        if bit == 0:
            down_sum.step()
            up_sum.step()
        vo_sum.step()
        if bit > 1:
            down_sum.step()
            up_sum.step()
        if bit == min(1, bits - 1):
            in_final = add(in_kept, line.hold(in_got))
            in_other = swap_core(in_final)
            line.mark(in_final)
            in_grad = whole(
                place_kernel,
                "place",
                [in_final, line.hold(in_other)],
                [],
                scalars=meta,
                filled=[shape(slot_len, width)],
                sems=4,
                far=True,
            )[0]
            line.mark(in_grad)
    qk_total, vo_total = qk_sum.finish(), vo_sum.finish()
    riding = qk_sum.extra
    row = riders // 2
    shared = jnp.concatenate([riding[:row, :head_width], riding[:row, head_width:]], axis=0)
    shared = shared.reshape(-1, 8, head_width).transpose(1, 0, 2).reshape(8, width)
    biases = riding[row].reshape(2, head_width)
    up_bias_sum = riding[row + 1 : row + 1 + hidden // (2 * head_width)].reshape(-1)
    if vo_sum.second is None:
        v_sum, o_sum = vo_total[:, :head_width], vo_total[:, head_width:].T
    else:
        v_sum, o_sum = vo_total, vo_sum.second
    down_sum = down_sum.finish().T
    up_sum = up_sum.finish()

    mine = first_ext[rows + 9 : rows + 11]
    theirs = sib_ext[rows + 9 : rows + 11]
    marks = jnp.concatenate([mine[:1], theirs[:1], mine[1:], theirs[1:]], axis=0)
    pooled = jnp.concatenate(
        [lax.dynamic_index_in_dim(marks, blocks[j], keepdims=True) for j in range(4)], axis=0
    )[None]
    return (
        out,
        pooled,
        in_grad,
        qk_total[:, :head_width],
        biases[0],
        qk_total[:, head_width:],
        v_sum,
        biases[1],
        o_sum,
        shared[0],
        shared[1],
        shared[2],
        up_sum,
        up_bias_sum,
        down_sum,
        shared[3],
        shared[4],
        shared[5],
    )


def solution(mesh):
    return jax.shard_map(
        functools.partial(shards, mesh.shape["dp"]),
        mesh=mesh,
        in_specs=(
            P("dp", None),
            P("dp"),
            P("dp", None),
            P("dp"),
            P(None, "mp"),
            P("mp"),
            P(None, "mp"),
            P(None, "mp"),
            P("mp"),
            P("mp", None),
            P(),
            P(),
            P(),
            P(None, "mp"),
            P("mp"),
            P("mp", None),
            P(),
            P(),
            P(),
            P("dp", None),
            P("dp", None, None),
        ),
        out_specs=(
            P("dp", None),
            P("dp", None, None),
            P("dp", None),
            P("dp", "mp"),
            P("mp"),
            P("dp", "mp"),
            P("dp", "mp"),
            P("mp"),
            P("mp", "dp"),
            P(),
            P(),
            P(),
            P("dp", "mp"),
            P("mp"),
            P("mp", "dp"),
            P(),
            P(),
            P(),
        ),
        check_vma=False,
    )
```
